32 devices in a mesh: batch: 8 (over z, y), head: 4 (over x, core).
Axes of the slice: x: 2, y: 2, z: 4, core: 2. Of those that a mesh axis runs over, the one named last changes fastest.
Arguments:
- tokens_in: bfloat16 [32768, 768], P(('batch', 'head')), may hold values from -5.6 to 5.6
- doc_ids: int32 [32768], P('batch'), may hold values from 0 to 3, as said below
- landmark_ids: int32 [32768], P('batch'), may hold values from 0 to 63, as said below
- pad_mask: int32 [32768], P('batch'), may hold values from 0 to 1, as said below
- w_query: bfloat16 [768, 768], P(None, 'head'), may hold values from -0.21875 to 0.21875
- w_key: bfloat16 [768, 768], P(None, 'head'), may hold values from -0.21875 to 0.21875
- w_value: bfloat16 [768, 768], P(None, 'head'), may hold values from -0.21875 to 0.21875
- w_output: bfloat16 [768, 768], P('head'), may hold values from -0.625 to 0.625
- conv_weight: bfloat16 [12, 33], P('head'), may hold values from -0.47851562 to 0.47851562
- first_gain: float32 [768], replicated, may hold values from 0.5 to 1.5
- first_bias: float32 [768], replicated, may hold values from -1.2 to 1.2
- w_inner: bfloat16 [768, 3072], replicated, may hold values from -0.21875 to 0.21875
- w_outer: bfloat16 [3072, 768], replicated, may hold values from -0.109375 to 0.109375
- second_gain: float32 [768], replicated, may hold values from 0.5 to 1.5
- second_bias: float32 [768], replicated, may hold values from -1.2 to 1.2
- out_grad: bfloat16 [32768, 768], P(('batch', 'head')), may hold values from -6 to 6
Outputs:
- layer_out: bfloat16 [32768, 768], P(('batch', 'head'))
- input_grad: bfloat16 [32768, 768], P(('batch', 'head'))
- grad_query: float32 [768, 768], P(None, 'head')
- grad_key: float32 [768, 768], P(None, 'head')
- grad_value: float32 [768, 768], P(None, 'head')
- grad_output: float32 [768, 768], P('head')
- grad_conv: float32 [12, 33], P('head')
- grad_first_gain: float32 [768], replicated
- grad_first_bias: float32 [768], replicated
- grad_inner: float32 [768, 3072], P(None, 'head')
- grad_outer: float32 [3072, 768], P('head')
- grad_second_gain: float32 [768], replicated
- grad_second_bias: float32 [768], replicated
The draws below stay inside these ranges and needn't reach their ends.
Inputs may be any that keep to these rules, and one draw needn't show every extreme that they name: `doc_ids`: within a row of 4096 tokens document numbers never fall, and each document has 128 real tokens or more. `landmark_ids`: within a document landmark numbers never fall, and every landmark of every document has 2 or more real tokens. `pad_mask`: the padding of a row is its last tokens, at least one, and counts to its last document.
All inputs are finite; a program needn't handle non-finite values.
Results may differ from the reference program's by a relative error of at most 0.018.
Values may be sent and summed in bfloat16 or wider, within the bound.
No kernel may reach another device: no remote copies, remote signals or barrier semaphores. Data moves between devices by JAX's collectives and lax.ppermute only.
A program may use at most 256 MiB of HBM per device.

```python
import jax
import jax.numpy as jnp
from jax import lax

D = 768
HEADS = 12
FF = 3072
LAND = 64
KW = 33
HEAD_DIM = 64
NEWTON = 6
DOCS = 4
ROW_LEN = 4096
TOKENS = 32768
N_BATCH = 8


def row_layout(row_key):
    pad_key, cut_key = jax.random.split(row_key)
    pad_count = jax.random.randint(pad_key, (), 1, ROW_LEN // 8)
    spare_room = ROW_LEN - pad_count - DOCS * 2 * LAND
    cut_points = jnp.sort(jax.random.randint(cut_key, (DOCS - 1,), 0, spare_room + 1))
    edge_list = jnp.concatenate([jnp.zeros((1,), jnp.int32), cut_points.astype(jnp.int32), jnp.reshape(spare_room, (1,)).astype(jnp.int32)])
    lengths = 2 * LAND + edge_list[1:] - edge_list[:-1]
    starts = jnp.concatenate([jnp.zeros((1,), jnp.int32), jnp.cumsum(lengths)[:-1].astype(jnp.int32)])
    position = jnp.arange(ROW_LEN, dtype=jnp.int32)
    doc_index = jnp.sum((position[:, None] >= starts[None, 1:]).astype(jnp.int32), axis=1)
    inside = position - starts[doc_index]
    land_index = jnp.minimum(inside * LAND // lengths[doc_index], LAND - 1)
    is_real = (position < ROW_LEN - pad_count).astype(jnp.int32)
    return (doc_index.astype(jnp.int32), land_index.astype(jnp.int32), is_real)


def layout_of(key):
    row_keys = jax.random.split(jax.random.fold_in(key, 17), TOKENS // ROW_LEN)
    return jax.vmap(row_layout)(row_keys)


def pick_rows(table_rows, seg_index):
    return jnp.take(table_rows, seg_index, axis=0)


def draw_doc_ids(key, part):
    return layout_of(key)[0].reshape(TOKENS)


def draw_landmark_ids(key, part):
    return layout_of(key)[1].reshape(TOKENS)


def draw_pad_mask(key, part):
    return layout_of(key)[2].reshape(TOKENS)


def draw_tokens_in(key, part):
    doc_index, land_index, is_real = layout_of(key)
    noise_key, common_key = jax.random.split(jax.random.fold_in(key, 29))
    row_total = TOKENS // ROW_LEN
    noise = jnp.clip(jax.random.normal(noise_key, (row_total, ROW_LEN, D), jnp.float32), -4.0, 4.0)
    common = jnp.clip(jax.random.normal(common_key, (row_total, DOCS * LAND, D), jnp.float32), -4.0, 4.0)
    segment = doc_index * LAND + land_index
    shared = jax.vmap(pick_rows)(common, segment)
    return (0.7 * (noise + shared)).reshape(TOKENS, D).astype(jnp.bfloat16)


def levels(own_key, extent, cuts, least, top_value):
    loudness = 1.0
    for dim, blocks in cuts:
        draws = jax.random.uniform(jax.random.fold_in(jax.random.fold_in(own_key, 6), dim), (blocks,), jnp.float32, least / len(cuts), top_value / len(cuts))
        loudness = loudness * jnp.repeat(jnp.exp(draws), extent[dim] // blocks).reshape((-1,) + (1,) * (len(extent) - 1 - dim))
    return loudness


def bell_draw(key, shape, scale, bound, shards=(), kind=jnp.bfloat16):
    level = levels(key, shape, shards, -0.22, 0.18) if shards else 1.0
    drawn = jax.random.normal(key, shape, jnp.float32) * scale * level
    return jnp.minimum(jnp.maximum(drawn, -bound), bound).astype(kind)


def setup_inputs(seed: int = 0) -> dict:
    keys = jax.random.split(jax.random.key(seed), 17)
    return {
        "tokens_in": draw_tokens_in(jax.random.fold_in(keys[16], 71), 0),
        "doc_ids": draw_doc_ids(jax.random.fold_in(keys[16], 71), 0),
        "landmark_ids": draw_landmark_ids(jax.random.fold_in(keys[16], 71), 0),
        "pad_mask": draw_pad_mask(jax.random.fold_in(keys[16], 71), 0),
        "w_query": bell_draw(keys[4], (D, D), D ** -0.5, 0.21875, ((1, 4),)),
        "w_key": bell_draw(keys[5], (D, D), D ** -0.5, 0.21875, ((1, 4),)),
        "w_value": bell_draw(keys[6], (D, D), D ** -0.5, 0.21875, ((1, 4),)),
        "w_output": bell_draw(keys[7], (D, D), (D // 8) ** -0.5, 0.625, ((0, 4),)),
        "conv_weight": bell_draw(keys[8], (HEADS, KW), 0.08, 0.47851562, ((0, 4),)),
        "first_gain": jnp.clip(1.0 + 0.1 * jax.random.normal(keys[9], (D,), jnp.float32), 0.5, 1.5),
        "first_bias": bell_draw(keys[10], (D,), 0.2, 1.2, (), jnp.float32),
        "w_inner": bell_draw(keys[11], (D, FF), D ** -0.5, 0.21875),
        "w_outer": bell_draw(keys[12], (FF, D), FF ** -0.5, 0.109375),
        "second_gain": jnp.clip(1.0 + 0.1 * jax.random.normal(keys[13], (D,), jnp.float32), 0.5, 1.5),
        "second_bias": bell_draw(keys[14], (D,), 0.2, 1.2, (), jnp.float32),
        "out_grad": bell_draw(keys[15], (TOKENS, D), 1.0, 6.0, ((0, 32),)),
    }


@jax.custom_vjp
def low(v):
    return lax.optimization_barrier(v.astype(jnp.bfloat16)).astype(jnp.float32)

@jax.custom_vjp
def low_back(v):
    return v

def low_keep(v):
    return (low(v), None)

def low_pass(kept, grad):
    return (grad,)

def back_keep(v):
    return (v, None)

def back_low(kept, grad):
    return (low(grad),)
low.defvjp(low_keep, low_pass)
low_back.defvjp(back_keep, back_low)
EXACT_PRECISION = lax.Precision.HIGHEST
NEG_FILL = -1e+30
NORM_EPS = 1e-05

def exact(pattern, first_op, second_op):
    return jnp.einsum(pattern, first_op, second_op, precision=EXACT_PRECISION)

def layer_norm(hidden, scale_vec, shift_vec):
    center = hidden - lax.optimization_barrier(jnp.mean(hidden, axis=-1, keepdims=True))
    spread = lax.optimization_barrier(jnp.mean(center * center, axis=-1, keepdims=True))
    return center * lax.rsqrt(spread + NORM_EPS) * scale_vec + shift_vec

def newton_inverse(kernel):
    square_sum = lax.optimization_barrier(jnp.sum(kernel * kernel, axis=(-2, -1), keepdims=True))
    estimate = jnp.swapaxes(kernel, -1, -2) / square_sum
    identity = jnp.eye(kernel.shape[-1], dtype=kernel.dtype)
    for step_count in range(NEWTON):
        product = jnp.matmul(kernel, estimate, precision=EXACT_PRECISION)
        factor_term = 7.0 * identity - product
        factor_term = 15.0 * identity - jnp.matmul(product, factor_term, precision=EXACT_PRECISION)
        factor_term = 13.0 * identity - jnp.matmul(product, factor_term, precision=EXACT_PRECISION)
        estimate = 0.25 * jnp.matmul(estimate, factor_term, precision=EXACT_PRECISION)
    return estimate

def row_forward(weight_set, row_data):
    w_query, w_key, w_value, w_output, conv_weight, first_gain, first_bias, w_inner, w_outer, second_gain, second_bias = weight_set
    tokens, doc_row, land_row, mask_row = row_data
    is_real = mask_row.astype(tokens.dtype)
    qk_scale = HEAD_DIM ** (-0.25)

    def project(weight, factor):
        mapped = exact('td,dc->tc', tokens, weight) * factor
        return low_back(low(mapped)).reshape(ROW_LEN, HEADS, HEAD_DIM)
    queries = project(w_query, qk_scale)
    key_rows = project(w_key, qk_scale)
    values = project(w_value, 1.0)
    land_total = DOCS * LAND
    columns = jnp.arange(land_total, dtype=jnp.int32)
    segment = doc_row * LAND + land_row
    member = (segment[:, None] == columns[None, :]).astype(tokens.dtype) * is_real[:, None]
    counts = lax.optimization_barrier(jnp.sum(member, axis=0))
    same_doc = doc_row[:, None] == (columns // LAND)[None, :]
    key_valid = jnp.logical_and(same_doc, mask_row[:, None] > 0)
    land_queries = low(exact('ts,thd->shd', member, queries) / counts[:, None, None])
    land_keys = low(exact('ts,thd->shd', member, key_rows) / counts[:, None, None])
    first_scores = low_back(exact('thd,shd->hts', queries, land_keys))
    first_weights = low(jax.nn.softmax(jnp.where(same_doc[None], first_scores, NEG_FILL), axis=-1))
    third_scores = low_back(exact('shd,thd->hst', land_queries, key_rows))
    third_weights = low(jax.nn.softmax(jnp.where(key_valid.T[None], third_scores, NEG_FILL), axis=-1))
    carried = low_back(exact('hst,thd->hsd', third_weights, values))
    doc_queries = land_queries.reshape(DOCS, LAND, HEADS, HEAD_DIM)
    doc_keys = land_keys.reshape(DOCS, LAND, HEADS, HEAD_DIM)
    small_weights = jax.nn.softmax(exact('aihd,ajhd->haij', doc_queries, doc_keys), axis=-1)
    inverse = newton_inverse(small_weights)
    mixed_rows = exact('haij,hajd->haid', inverse, carried.reshape(HEADS, DOCS, LAND, HEAD_DIM))
    mixed_rows = low(mixed_rows.reshape(HEADS, land_total, HEAD_DIM))
    attention = exact('hts,hsd->thd', first_weights, mixed_rows)
    half_width = KW // 2
    padded_values = jnp.pad(values, ((half_width, half_width), (0, 0), (0, 0)))
    padded_docs = jnp.pad(doc_row, (half_width, half_width), constant_values=-1)
    padded_real = jnp.pad(is_real, (half_width, half_width))
    conv_out = jnp.zeros_like(values)
    for offset in range(KW):
        is_valid = jnp.where(padded_docs[offset:offset + ROW_LEN] == doc_row, padded_real[offset:offset + ROW_LEN], 0.0)
        conv_out = conv_out + conv_weight[:, offset][None, :, None] * padded_values[offset:offset + ROW_LEN] * is_valid[:, None, None]
    heads_out = low_back(low((attention + conv_out) * is_real[:, None, None])).reshape(ROW_LEN, D)
    projected = low_back(exact('tc,cd->td', heads_out, w_output))
    first_out = layer_norm(tokens + projected, first_gain, first_bias)
    inner_pre = low_back(exact('td,df->tf', low(first_out), w_inner))
    inner_act = low(jax.nn.gelu(inner_pre, approximate=False))
    outer_out = low_back(exact('tf,fd->td', inner_act, w_outer))
    return layer_norm(first_out + outer_out, second_gain, second_bias)

def reference(tokens_in, doc_ids, landmark_ids, pad_mask, w_query, w_key, w_value, w_output, conv_weight, first_gain, first_bias, w_inner, w_outer, second_gain, second_bias, out_grad):
    weight_list = (w_query, w_key, w_value, w_output, conv_weight, first_gain, first_bias, w_inner, w_outer, second_gain, second_bias)
    weight_set = tuple((weight_arg.astype(jnp.float32) for weight_arg in weight_list))
    x_rows = tokens_in.astype(jnp.float32).reshape(N_BATCH, ROW_LEN, D)
    structure = (doc_ids.reshape(N_BATCH, ROW_LEN), landmark_ids.reshape(N_BATCH, ROW_LEN), pad_mask.reshape(N_BATCH, ROW_LEN))
    checked = jax.checkpoint(row_forward)

    def whole(x_all, weights_now):

        def one_row(row_data):
            return checked(weights_now, row_data)
        return lax.map(one_row, (x_all,) + structure)
    outputs, pullback = jax.vjp(whole, x_rows, weight_set)
    x_grad, weight_grads = pullback(out_grad.astype(jnp.float32).reshape(N_BATCH, ROW_LEN, D))
    grads_out = tuple((grad_item.astype(jnp.float32) for grad_item in weight_grads))
    return (outputs.reshape(TOKENS, D).astype(jnp.bfloat16), x_grad.reshape(TOKENS, D).astype(jnp.bfloat16), grads_out[0], grads_out[1], grads_out[2], grads_out[3], grads_out[4], grads_out[5], grads_out[6], grads_out[7], grads_out[8], grads_out[9], grads_out[10])
```

```python
import functools

import jax
import jax.numpy as jnp
from jax import lax
from jax.experimental import pallas as pl
from jax.experimental.pallas import tpu as pltpu
from jax.sharding import PartitionSpec as P

LAND = 64
KW = 33
HALF = KW // 2
HEAD_DIM = 64
NEWTON = 6
DOCS = 4
SEGS = DOCS * LAND
WIDE = 2 * SEGS
BLOCK = 128
CHUNK = 256
QK_SCALE = HEAD_DIM ** (-0.25)

EXACT_PRECISION = lax.Precision.HIGHEST
NEG_FILL = -1e30
NORM_EPS = 1e-05
BF = jnp.bfloat16
F32 = jnp.float32


def newton_inverse(kernel):
    square_sum = jnp.sum(kernel * kernel, axis=(-2, -1), keepdims=True)
    estimate = jnp.swapaxes(kernel, -1, -2) / square_sum
    identity = jnp.eye(kernel.shape[-1], dtype=kernel.dtype)
    for step_count in range(NEWTON):
        product = jnp.matmul(kernel, estimate, precision=EXACT_PRECISION)
        factor_term = 7.0 * identity - product
        factor_term = 15.0 * identity - jnp.matmul(product, factor_term, precision=EXACT_PRECISION)
        factor_term = 13.0 * identity - jnp.matmul(product, factor_term, precision=EXACT_PRECISION)
        estimate = 0.25 * jnp.matmul(estimate, factor_term, precision=EXACT_PRECISION)
    return estimate


def norm_forward(hidden, scale_vec, shift_vec):
    center = hidden - jnp.mean(hidden, axis=-1, keepdims=True)
    inv_spread = lax.rsqrt(jnp.mean(center * center, axis=-1, keepdims=True) + NORM_EPS)
    normed = center * inv_spread
    return (normed * scale_vec + shift_vec, normed, inv_spread)


def norm_backward(upstream, normed, inv_spread, scale_vec):
    scaled = upstream * scale_vec
    result_grad = inv_spread * (
        scaled
        - jnp.mean(scaled, axis=-1, keepdims=True)
        - normed * jnp.mean(scaled * normed, axis=-1, keepdims=True)
    )
    return (result_grad, jnp.sum(upstream * normed, axis=0), jnp.sum(upstream, axis=0))


def nn(a, b):
    return lax.dot_general(a, b, (((1,), (0,)), ((), ())), preferred_element_type=F32)


def nt(a, b):
    return lax.dot_general(a, b, (((1,), (1,)), ((), ())), preferred_element_type=F32)


def tn(a, b):
    return lax.dot_general(a, b, (((0,), (0,)), ((), ())), preferred_element_type=F32)


def pair_block(ref):
    zero = jnp.zeros((HEAD_DIM, SEGS), BF)
    top = jnp.concatenate([ref[0].astype(BF), zero], axis=1)
    low = jnp.concatenate([zero, ref[1].astype(BF)], axis=1)
    return jnp.concatenate([top, low], axis=0)


def put_pair(ref, value):
    ref[0] = value[:HEAD_DIM, :SEGS].astype(ref.dtype)
    ref[1] = value[HEAD_DIM:, SEGS:].astype(ref.dtype)


def doc_bias(code):
    lane_doc = lax.broadcasted_iota(jnp.int32, (code.shape[0], SEGS), 1) // LAND
    return jnp.where(code == lane_doc, 0.0, NEG_FILL)


def rows_of(i, size, base=0):
    return pl.ds(pl.multiple_of(base + i * size, 16), size)


def third_kernel(code_ref, k_ref, v_ref, lq_ref, c_ref, st_ref, e_ref, s_scr, acc):
    steps = k_ref.shape[0] // CHUNK
    lq2 = pair_block(lq_ref)

    def scores(i, top):
        r = rows_of(i, CHUNK)
        bias = doc_bias(code_ref[r, :])
        s = nn(k_ref[r, :], lq2) + jnp.concatenate([bias, bias], axis=1)
        s_scr[r, :] = s
        return jnp.maximum(top, jnp.max(s, axis=0, keepdims=True))

    top = lax.fori_loop(0, steps, scores, jnp.full((1, WIDE), 3.0 * NEG_FILL, F32))
    acc[...] = jnp.zeros_like(acc)

    def weigh(i, total):
        r = rows_of(i, CHUNK)
        e = jnp.exp(s_scr[r, :] - top)
        low = e.astype(BF)
        e_ref[r, :] = low
        acc[...] += tn(v_ref[rows_of(i, CHUNK, HALF), :], low)
        return total + jnp.sum(e, axis=0, keepdims=True)

    total = lax.fori_loop(0, steps, weigh, jnp.zeros((1, WIDE), F32))
    put_pair(c_ref, acc[...] / total)
    st_ref[0, 0:1, :] = top[:, :SEGS]
    st_ref[1, 0:1, :] = top[:, SEGS:]
    st_ref[0, 1:2, :] = total[:, :SEGS]
    st_ref[1, 1:2, :] = total[:, SEGS:]


def skew(x, left):
    row = lax.broadcasted_iota(jnp.int32, x.shape, 0)
    lanes = x.shape[1]
    for bit in range(x.shape[0].bit_length() - 1):
        step = 1 << bit
        moved = pltpu.roll(x, lanes - step if left else step, 1)
        x = jnp.where((row & step) != 0, moved, x)
    return x


def band(w_ref, index):
    return skew(jnp.broadcast_to(w_ref[index], (BLOCK, 2 * BLOCK)), False).astype(BF)


def band_mask(code_ref, line_ref, i):
    line = line_ref[:, pl.ds(pl.multiple_of(i * BLOCK, BLOCK), 2 * BLOCK)]
    return code_ref[rows_of(i, BLOCK), :] == line


def first_kernel(code_ref, line_ref, q_ref, v_ref, lk_ref, w_ref, p_ref, conv_ref, t_scr):
    lk2 = pair_block(lk_ref)
    t_scr[0] = band(w_ref, 0)
    t_scr[1] = band(w_ref, 1)
    left_lane = lax.broadcasted_iota(jnp.int32, (BLOCK, BLOCK), 1) < HEAD_DIM

    def convolve(i, carry):
        mask = band_mask(code_ref, line_ref, i)
        window = v_ref[rows_of(i, BLOCK), :], v_ref[rows_of(i + 1, BLOCK), :]
        window = jnp.concatenate(window, axis=0)
        zero = jnp.zeros((BLOCK, 2 * BLOCK), BF)
        one = nn(jnp.where(mask, t_scr[0], zero), window)
        two = nn(jnp.where(mask, t_scr[1], zero), window)
        conv_ref[rows_of(i, BLOCK), :] = jnp.where(left_lane, one, two)
        return carry

    lax.fori_loop(0, q_ref.shape[0] // BLOCK, convolve, 0)

    def weigh(i, carry):
        r = rows_of(i, CHUNK)
        bias = doc_bias(code_ref[r, :])
        s = nn(q_ref[r, :], lk2)
        for side in (0, 1):
            cols = slice(side * SEGS, (side + 1) * SEGS)
            part = s[:, cols] + bias
            e = jnp.exp(part - jnp.max(part, axis=1, keepdims=True))
            p_ref[r, cols] = (e * (1.0 / jnp.sum(e, axis=1, keepdims=True))).astype(BF)
        return carry

    lax.fori_loop(0, q_ref.shape[0] // CHUNK, weigh, 0)


def heads_kernel(code_ref, p_ref, mix_ref, conv_ref, out_ref):
    mix2 = pair_block(mix_ref)

    def body(i, carry):
        r = rows_of(i, CHUNK)
        total = nt(p_ref[r, :], mix2) + conv_ref[r, :]
        out_ref[r, :] = jnp.where(code_ref[r, :] >= 0, total, 0.0).astype(BF)
        return carry

    lax.fori_loop(0, p_ref.shape[0] // CHUNK, body, 0)


def mixed_grad_kernel(hg_ref, p_ref, mg_ref):
    put_pair(mg_ref, tn(hg_ref[...], p_ref[...]))


def first_back_kernel(hg_ref, p_ref, q_ref, mix_ref, lk_ref, dq_ref, lkg_ref, acc):
    mix2 = pair_block(mix_ref)
    lk2 = pair_block(lk_ref)
    acc[...] = jnp.zeros_like(acc)

    def body(i, carry):
        r = rows_of(i, CHUNK)
        g = nn(hg_ref[r, :], mix2)
        parts = []
        for side in (0, 1):
            cols = slice(side * SEGS, (side + 1) * SEGS)
            p = p_ref[r, cols].astype(F32)
            gp = g[:, cols] * p
            parts.append((gp - p * jnp.sum(gp, axis=1, keepdims=True)).astype(BF))
        ds = jnp.concatenate(parts, axis=1)
        dq_ref[r, :] = nt(ds, lk2).astype(BF)
        acc[...] += tn(q_ref[r, :], ds)
        return carry

    lax.fori_loop(0, p_ref.shape[0] // CHUNK, body, 0)
    put_pair(lkg_ref, acc[...])


def conv_back_kernel(code_ref, line_ref, hgx_ref, v_ref, w_ref, back_ref, tap_ref, t_scr, acc):
    t_scr[0] = band(w_ref, 0)
    t_scr[1] = band(w_ref, 1)
    acc[...] = jnp.zeros_like(acc)
    left_lane = lax.broadcasted_iota(jnp.int32, (BLOCK, BLOCK), 1) < HEAD_DIM

    def body(i, carry):
        mask = band_mask(code_ref, line_ref, i)
        grads = hgx_ref[rows_of(i, BLOCK), :], hgx_ref[rows_of(i + 1, BLOCK), :]
        grads = jnp.concatenate(grads, axis=0)
        vals = v_ref[rows_of(i, BLOCK), :], v_ref[rows_of(i + 1, BLOCK), :]
        vals = jnp.concatenate(vals, axis=0)
        zero = jnp.zeros((BLOCK, 2 * BLOCK), BF)
        one = nn(jnp.where(mask, t_scr[0], zero), grads)
        two = nn(jnp.where(mask, t_scr[1], zero), grads)
        back_ref[rows_of(i, BLOCK), :] = jnp.where(left_lane, one, two)
        here = hgx_ref[rows_of(i, BLOCK, HALF), :]
        none = jnp.zeros_like(here)
        acc[0] += jnp.where(mask, nt(jnp.where(left_lane, here, none), vals), 0.0)
        acc[1] += jnp.where(mask, nt(jnp.where(left_lane, none, here), vals), 0.0)
        return carry

    lax.fori_loop(0, back_ref.shape[0] // BLOCK, body, 0)
    for side in (0, 1):
        tap_ref[side, 0:1, :] = jnp.sum(skew(acc[side], True), axis=0, keepdims=True)


def third_back_kernel(
    k_ref, v_ref, e_ref, f_ref, d_ref, cg_ref, lq_ref, back_ref, dk_ref, dv_ref, lqg_ref, acc
):
    cg2 = pair_block(cg_ref)
    lq2 = pair_block(lq_ref)
    factor = jnp.concatenate([f_ref[0], f_ref[1]], axis=1)
    delta = jnp.concatenate([d_ref[0], d_ref[1]], axis=1)
    acc[...] = jnp.zeros_like(acc)

    def body(i, carry):
        r = rows_of(i, CHUNK)
        h = nn(v_ref[rows_of(i, CHUNK, HALF), :], cg2)
        p = e_ref[r, :].astype(F32) * factor
        ds = (p * (h - delta)).astype(BF)
        dk_ref[r, :] = nt(ds, lq2).astype(BF)
        dv_ref[r, :] = (nt(p.astype(BF), cg2) + back_ref[r, :]).astype(BF)
        acc[...] += tn(k_ref[r, :], ds)
        return carry

    lax.fori_loop(0, e_ref.shape[0] // CHUNK, body, 0)
    put_pair(lqg_ref, acc[...])


def feed_kernel(x_ref, wi_ref, wo_ref, act_ref, slope_ref, out_ref):
    @pl.when(pl.program_id(0) == 0)
    def _():
        out_ref[...] = jnp.zeros_like(out_ref)

    def body(i, carry):
        r = rows_of(i, CHUNK)
        pre = nn(x_ref[r, :], wi_ref[...])
        cdf = 0.5 * (1.0 + lax.erf(pre * (0.5**0.5)))
        pdf = jnp.exp(-0.5 * pre * pre) * 0.3989422804014327
        act = (pre * cdf).astype(BF)
        act_ref[r, :] = act
        slope_ref[r, :] = (cdf + pre * pdf).astype(BF)
        out_ref[r, :] += nn(act, wo_ref[...])
        return carry

    lax.fori_loop(0, x_ref.shape[0] // CHUNK, body, 0)


def feed_back_kernel(
    table, og_ref, x_ref, wi_ref, wo_ref, act_ref, slope_ref, prev_ref, gi_ref, go_ref, fg_ref, pg
):
    @pl.when(pl.program_id(0) == 0)
    def _():
        fg_ref[...] = prev_ref[...]

    def body(i, carry):
        r = rows_of(i, CHUNK)
        grad = nt(og_ref[r, :], wo_ref[...])
        low = (slope_ref[r, :].astype(F32) * grad).astype(BF)
        pg[r, :] = low
        fg_ref[r, :] += nt(low, wi_ref[...])
        return carry

    lax.fori_loop(0, og_ref.shape[0] // CHUNK, body, 0)
    gi_ref[0] = tn(x_ref[...], pg[...]).astype(BF)
    go_ref[0] = tn(act_ref[...], og_ref[...]).astype(BF)


def call(body, grid, ins, outs, scratch=(), flops=0, moved=0, exps=0, limit=40):
    return pl.pallas_call(
        body,
        grid=grid,
        in_specs=[spec for spec in ins],
        out_specs=[spec for spec, _ in outs],
        out_shape=[shape for _, shape in outs],
        scratch_shapes=list(scratch),
        compiler_params=pltpu.CompilerParams(vmem_limit_bytes=limit << 20),
        cost_estimate=pl.CostEstimate(flops=flops, bytes_accessed=moved, transcendentals=exps),
    )


def whole(shape):
    return pl.BlockSpec(shape, lambda p: (0,) * len(shape))


def column(rows, width):
    return pl.BlockSpec((rows, width), lambda p: (0, p))


def heads_spec(rows, cols):
    return pl.BlockSpec((2, rows, cols), lambda p: (p, 0, 0))


def shape_of(shape, dtype):
    return jax.ShapeDtypeStruct(shape, dtype)


def shards(
    batch_size,
    tokens_in,
    doc_ids,
    landmark_ids,
    pad_mask,
    w_query,
    w_key,
    w_value,
    w_output,
    conv_weight,
    first_gain,
    first_bias,
    w_inner,
    w_outer,
    second_gain,
    second_bias,
    out_grad,
):
    groups = 4
    rows, width = tokens_in.shape
    local = w_query.shape[1]
    own = local // HEAD_DIM
    side = 2 * own
    side_cols = 2 * local
    pairs = side // 2
    ext = rows + BLOCK
    ff = w_inner.shape[1]
    me = lax.axis_index("head")
    bat = lax.axis_index("batch")
    core = me & 1

    def swap(value, bit):
        return lax.ppermute(value, "head", [(i, i ^ bit) for i in range(groups)])

    def swap_batch(value, bit):
        return lax.ppermute(value, "batch", [(i, i ^ bit) for i in range(batch_size)])

    def spread(value):
        two = swap(value, 2)
        return value, swap(value, 1), two, swap(two, 1)

    def add_low(a, b):
        return (a.astype(F32) + b.astype(F32)).astype(BF)

    def ordered(low_bit, mine, other):
        first = jnp.where(low_bit == 0, mine, other)
        second = jnp.where(low_bit == 0, other, mine)
        return jnp.concatenate([first, second], axis=0)

    def head_sum(value):
        half = value.shape[0] // 2
        mine = lax.dynamic_slice_in_dim(value, core * half, half, 0)
        other = lax.dynamic_slice_in_dim(value, (1 - core) * half, half, 0)
        mine = add_low(mine, swap(other, 1))
        mine = add_low(mine, swap(mine, 2))
        return ordered(core, mine, swap(mine, 1))

    def batch_sum(value):
        bits = [1 << b for b in range(batch_size.bit_length() - 1)]
        for bit in bits:
            half = value.shape[0] // 2
            flag = jnp.where((bat & bit) != 0, 1, 0)
            mine = lax.dynamic_slice_in_dim(value, flag * half, half, 0)
            other = lax.dynamic_slice_in_dim(value, (1 - flag) * half, half, 0)
            value = add_low(mine, swap_batch(other, bit))
        for bit in reversed(bits):
            flag = jnp.where((bat & bit) != 0, 1, 0)
            value = ordered(flag, value, swap_batch(value, bit))
        return value.astype(F32)

    def slot_sum(keep, send):
        got = add_low(keep, swap(send, 1))
        return batch_sum(add_low(got[0], swap(got[1], 2)))

    code_row = jnp.where(pad_mask > 0, doc_ids, -1)
    outside = jnp.full((BLOCK - HALF,), -2, jnp.int32)
    code_pad = jnp.concatenate([outside[:HALF], code_row, outside])
    line = lax.dynamic_slice_in_dim(code_pad, me * rows, ext, 0)
    code = line[HALF : HALF + rows].reshape(rows, 1)
    line = line.reshape(1, ext)
    segment_row = jnp.where(pad_mask > 0, doc_ids * LAND + landmark_ids, -1)
    columns = jnp.arange(SEGS, dtype=jnp.int32)
    counts = jnp.sum((segment_row[:, None] == columns[None, :]).astype(F32), axis=0)
    segment = lax.dynamic_slice_in_dim(segment_row, me * rows, rows, 0)
    member = (segment[:, None] == columns[None, :]).astype(BF)

    packed = jnp.concatenate([w_query.T, w_key.T, w_value.T], axis=0)
    got = spread(packed)
    taps = spread(conv_weight.astype(F32))
    wo_parts = spread(w_output)

    def weight_half(half, index):
        return jnp.concatenate(
            [got[2 * half + j][index * local : (index + 1) * local] for j in (0, 1)], axis=0
        )

    wq, wk, wv = ([weight_half(half, index) for half in (0, 1)] for index in range(3))
    wo = [jnp.concatenate(wo_parts[2 * half : 2 * half + 2], axis=0) for half in (0, 1)]
    tap_rows = [jnp.concatenate(taps[2 * half : 2 * half + 2], axis=0) for half in (0, 1)]

    def tap_lines(value):
        value = jnp.pad(value, ((0, 0), (0, 2 * BLOCK - KW)))
        return value.reshape(side, 1, 2 * BLOCK)

    def with_edges(value):
        before = lax.ppermute(value[-HALF:], "head", [(i, i + 1) for i in range(groups - 1)])
        after = lax.ppermute(value[:HALF], "head", [(i + 1, i) for i in range(groups - 1)])
        rest = jnp.zeros((BLOCK - 2 * HALF, value.shape[1]), value.dtype)
        return jnp.concatenate([before, value, after, rest], axis=0)

    tokens_ext = with_edges(tokens_in)

    land_part = tn(member, tokens_in) / counts[:, None]
    land_tokens = head_sum(land_part.astype(BF))

    queries, keys, values, land_q, land_k = [], [], [], [], []
    for half in (0, 1):
        queries.append((nt(tokens_in, wq[half]) * QK_SCALE).astype(BF))
        keys.append((nt(tokens_in, wk[half]) * QK_SCALE).astype(BF))
        values.append(nt(tokens_ext, wv[half]).astype(BF))
        for weight, target in ((wq, land_q), (wk, land_k)):
            mapped = (nt(weight[half], land_tokens) * QK_SCALE).astype(BF)
            target.append(mapped.reshape(side, HEAD_DIM, SEGS))

    third_call = call(
        third_kernel,
        (pairs,),
        [whole((rows, 1)), column(rows, BLOCK), column(ext, BLOCK), heads_spec(HEAD_DIM, SEGS)],
        [
            (heads_spec(HEAD_DIM, SEGS), shape_of((side, HEAD_DIM, SEGS), BF)),
            (heads_spec(8, SEGS), shape_of((side, 8, SEGS), F32)),
            (column(rows, WIDE), shape_of((rows, side * SEGS), BF)),
        ],
        [pltpu.VMEM((rows, WIDE), F32), pltpu.VMEM((BLOCK, WIDE), F32)],
        flops=4 * rows * side_cols * SEGS,
        moved=2 * rows * (side_cols * 2 + side * SEGS),
        exps=rows * side * SEGS,
    )
    carry_low, stats, third_exp = [], [], []
    for half in (0, 1):
        c_out, st_out, e_out = third_call(code, keys[half], values[half], land_q[half])
        carry_low.append(c_out)
        stats.append(st_out[:, :2])
        third_exp.append(e_out)

    def join(c_a, st_a, c_b, st_b):
        top = jnp.maximum(st_a[..., 0, :], st_b[..., 0, :])
        share_a = st_a[..., 1, :] * jnp.exp(st_a[..., 0, :] - top)
        share_b = st_b[..., 1, :] * jnp.exp(st_b[..., 0, :] - top)
        total = share_a + share_b
        joined = (
            c_a.astype(F32) * share_a[..., None, :] + c_b.astype(F32) * share_b[..., None, :]
        ) / total[..., None, :]
        return joined, jnp.stack([top, total], axis=-2)

    c_keep = jnp.stack([carry_low[0][:own], carry_low[1][:own]])
    c_send = jnp.stack([carry_low[0][own:], carry_low[1][own:]])
    st_keep = jnp.stack([stats[0][:own], stats[1][:own]])
    st_send = jnp.stack([stats[0][own:], stats[1][own:]])
    c_join, st_join = join(c_keep, st_keep, swap(c_send, 1), swap(st_send, 1))
    c_far, st_far = swap(c_join[1].astype(BF), 2), swap(st_join[1], 2)
    carried, st_all = join(c_join[0], st_join[0], c_far, st_far)
    third_lse = st_all[:, 0] + jnp.log(st_all[:, 1])

    def small_kernel(q_t, k_t):
        q_docs = q_t.reshape(own, HEAD_DIM, DOCS, LAND)
        k_docs = k_t.reshape(own, HEAD_DIM, DOCS, LAND)
        small_scores = jnp.einsum("hdai,hdaj->haij", q_docs, k_docs, precision=EXACT_PRECISION)
        return newton_inverse(jax.nn.softmax(small_scores, axis=-1))

    inverse, inverse_pull = jax.vjp(
        small_kernel, land_q[0][:own].astype(F32), land_k[0][:own].astype(F32)
    )
    carried_docs = carried.reshape(own, HEAD_DIM, DOCS, LAND)
    mixed_own = jnp.einsum("haij,hdaj->hdai", inverse, carried_docs, precision=EXACT_PRECISION)
    mixed_own = mixed_own.reshape(own, HEAD_DIM, SEGS).astype(BF)

    def spread_halves(value):
        parts = spread(value)
        return [jnp.concatenate(parts[2 * half : 2 * half + 2], axis=0) for half in (0, 1)]

    mixed = spread_halves(mixed_own)
    lse_all = spread_halves(third_lse)

    first_call = call(
        first_kernel,
        (pairs,),
        [
            whole((rows, 1)),
            whole((1, ext)),
            column(rows, BLOCK),
            column(ext, BLOCK),
            heads_spec(HEAD_DIM, SEGS),
            heads_spec(1, 2 * BLOCK),
        ],
        [
            (column(rows, WIDE), shape_of((rows, side * SEGS), BF)),
            (column(rows, BLOCK), shape_of((rows, side_cols), F32)),
        ],
        [pltpu.VMEM((2, BLOCK, 2 * BLOCK), BF)],
        flops=4 * rows * side_cols * SEGS,
        moved=2 * rows * (side_cols * 4 + side * SEGS),
        exps=rows * side * SEGS,
    )
    heads_call = call(
        heads_kernel,
        (pairs,),
        [whole((rows, 1)), column(rows, WIDE), heads_spec(HEAD_DIM, SEGS), column(rows, BLOCK)],
        [(column(rows, BLOCK), shape_of((rows, side_cols), BF))],
        flops=2 * rows * side_cols * SEGS,
        moved=2 * rows * (side_cols * 3 + side * SEGS),
    )
    first_low, heads_out = [], []
    for half in (0, 1):
        p_out, conv_out = first_call(
            code, line, queries[half], values[half], land_k[half], tap_lines(tap_rows[half])
        )
        first_low.append(p_out)
        heads_out.append(heads_call(code, p_out, mixed[half], conv_out)[0])

    projected = nn(heads_out[0], wo[0]) + nn(heads_out[1], wo[1])
    first_out, first_normed, first_inv = norm_forward(
        tokens_in.astype(F32) + projected, first_gain, first_bias
    )
    norm_low = first_out.astype(BF)

    block = 512 if ff % 512 == 0 else ff
    act, slope, outer_out = call(
        feed_kernel,
        (ff // block,),
        [whole((rows, width)), column(width, block), pl.BlockSpec((block, width), lambda p: (p, 0))],
        [
            (column(rows, block), shape_of((rows, ff), BF)),
            (column(rows, block), shape_of((rows, ff), BF)),
            (whole((rows, width)), shape_of((rows, width), F32)),
        ],
        flops=4 * rows * width * ff,
        moved=2 * (2 * width * ff + 2 * rows * ff + 3 * rows * width),
        exps=2 * rows * ff,
    )(norm_low, w_inner, w_outer)
    second_out, second_normed, second_inv = norm_forward(
        first_out + outer_out, second_gain, second_bias
    )
    layer_out = second_out.astype(BF)
    second_grad, grad_second_gain, grad_second_bias = norm_backward(
        out_grad.astype(F32), second_normed, second_inv, second_gain
    )
    outer_low = second_grad.astype(BF)

    share = ff // groups
    cut = share // 2

    def feed_back(slots, previous):
        table = jnp.stack([(me ^ slot) * 2 + part for slot in slots for part in (0, 1)])
        grid_spec = pltpu.PrefetchScalarGridSpec(
            num_scalar_prefetch=1,
            grid=(2 * len(slots),),
            in_specs=[
                pl.BlockSpec((rows, width), lambda p, t: (0, 0)),
                pl.BlockSpec((rows, width), lambda p, t: (0, 0)),
                pl.BlockSpec((width, cut), lambda p, t: (0, t[p])),
                pl.BlockSpec((cut, width), lambda p, t: (t[p], 0)),
                pl.BlockSpec((rows, cut), lambda p, t: (0, t[p])),
                pl.BlockSpec((rows, cut), lambda p, t: (0, t[p])),
                pl.BlockSpec((rows, width), lambda p, t: (0, 0)),
            ],
            out_specs=[
                pl.BlockSpec((1, width, cut), lambda p, t: (p // 2, 0, p % 2)),
                pl.BlockSpec((1, cut, width), lambda p, t: (p // 2, p % 2, 0)),
                pl.BlockSpec((rows, width), lambda p, t: (0, 0)),
            ],
            scratch_shapes=[pltpu.VMEM((rows, cut), BF)],
        )
        return pl.pallas_call(
            feed_back_kernel,
            grid_spec=grid_spec,
            out_shape=[
                shape_of((len(slots), width, share), BF),
                shape_of((len(slots), share, width), BF),
                shape_of((rows, width), F32),
            ],
            compiler_params=pltpu.CompilerParams(vmem_limit_bytes=48 << 20),
            cost_estimate=pl.CostEstimate(
                flops=8 * rows * width * share * len(slots),
                bytes_accessed=2 * len(slots) * share * (4 * width + 2 * rows) + 12 * rows * width,
                transcendentals=0,
            ),
        )(table, outer_low, norm_low, w_inner, w_outer, act, slope, previous)

    gi_send, go_send, first_grad = feed_back((1, 3), second_grad)
    gi_keep, go_keep, first_grad = feed_back((0, 2), first_grad)
    grad_inner = slot_sum(gi_keep, gi_send)
    grad_outer = slot_sum(go_keep, go_send)

    first_in_grad, grad_first_gain, grad_first_bias = norm_backward(
        first_grad, first_normed, first_inv, first_gain
    )
    proj_low = first_in_grad.astype(BF)

    def slots_of(parts):
        cut_rows = parts[0].shape[0] // 2
        keep = jnp.stack([part[:cut_rows] for part in parts])
        send = jnp.stack([part[cut_rows:] for part in parts])
        return keep, send

    grad_output = slot_sum(*slots_of([tn(part, proj_low).astype(BF) for part in heads_out]))
    proj_ext = with_edges(proj_low)
    real_ext = line.reshape(ext, 1) >= 0
    heads_grad_ext = [
        jnp.where(real_ext, nt(proj_ext, wo[half]), 0.0).astype(BF) for half in (0, 1)
    ]
    heads_grad = [part[HALF : HALF + rows] for part in heads_grad_ext]

    mixed_grad_call = call(
        mixed_grad_kernel,
        (pairs,),
        [column(rows, BLOCK), column(rows, WIDE)],
        [(heads_spec(HEAD_DIM, SEGS), shape_of((side, HEAD_DIM, SEGS), BF))],
        flops=2 * rows * side_cols * SEGS,
        moved=2 * rows * (side_cols + side * SEGS),
    )
    mixed_part = [mixed_grad_call(heads_grad[half], first_low[half])[0] for half in (0, 1)]

    def own_sum(parts):
        keep = jnp.stack([part[:own] for part in parts])
        send = jnp.stack([part[own:] for part in parts])
        got = keep.astype(F32) + swap(send, 1).astype(F32)
        return got[0] + swap(got[1].astype(BF), 2).astype(F32)

    mixed_grad = own_sum(mixed_part).reshape(own, HEAD_DIM, DOCS, LAND)
    inverse_grad = jnp.einsum("hdai,hdaj->haij", mixed_grad, carried_docs, precision=EXACT_PRECISION)
    carried_low = jnp.einsum("haij,hdai->hdaj", inverse, mixed_grad, precision=EXACT_PRECISION)
    carried_low = carried_low.reshape(own, HEAD_DIM, SEGS).astype(BF)
    third_delta = jnp.sum(carried_low.astype(F32) * carried, axis=1)
    carried_grad = spread_halves(carried_low)
    delta_all = spread_halves(third_delta)
    small_query, small_key = inverse_pull(inverse_grad)

    first_back_call = call(
        first_back_kernel,
        (pairs,),
        [
            column(rows, BLOCK),
            column(rows, WIDE),
            column(rows, BLOCK),
            heads_spec(HEAD_DIM, SEGS),
            heads_spec(HEAD_DIM, SEGS),
        ],
        [
            (column(rows, BLOCK), shape_of((rows, side_cols), BF)),
            (heads_spec(HEAD_DIM, SEGS), shape_of((side, HEAD_DIM, SEGS), F32)),
        ],
        [pltpu.VMEM((BLOCK, WIDE), F32)],
        flops=6 * rows * side_cols * SEGS,
        moved=2 * rows * (side_cols * 3 + side * SEGS),
    )
    conv_back_call = call(
        conv_back_kernel,
        (pairs,),
        [
            whole((rows, 1)),
            whole((1, ext)),
            column(ext, BLOCK),
            column(ext, BLOCK),
            heads_spec(1, 2 * BLOCK),
        ],
        [
            (column(rows, BLOCK), shape_of((rows, side_cols), F32)),
            (heads_spec(8, 2 * BLOCK), shape_of((side, 8, 2 * BLOCK), F32)),
        ],
        [pltpu.VMEM((2, BLOCK, 2 * BLOCK), BF), pltpu.VMEM((2, BLOCK, 2 * BLOCK), F32)],
        flops=4 * rows * side_cols * SEGS,
        moved=2 * rows * side_cols * 4,
    )
    third_back_call = call(
        third_back_kernel,
        (pairs,),
        [
            column(rows, BLOCK),
            column(ext, BLOCK),
            column(rows, WIDE),
            heads_spec(1, SEGS),
            heads_spec(1, SEGS),
            heads_spec(HEAD_DIM, SEGS),
            heads_spec(HEAD_DIM, SEGS),
            column(rows, BLOCK),
        ],
        [
            (column(rows, BLOCK), shape_of((rows, side_cols), BF)),
            (column(rows, BLOCK), shape_of((rows, side_cols), BF)),
            (heads_spec(HEAD_DIM, SEGS), shape_of((side, HEAD_DIM, SEGS), F32)),
        ],
        [pltpu.VMEM((BLOCK, WIDE), F32)],
        flops=8 * rows * side_cols * SEGS,
        moved=2 * rows * (side_cols * 6 + side * SEGS),
    )
    query_low, key_low, value_low, land_qg, land_kg, tap_grads = [], [], [], [], [], []
    for half in (0, 1):
        dq, lkg = first_back_call(
            heads_grad[half], first_low[half], queries[half], mixed[half], land_k[half]
        )
        back, tap_out = conv_back_call(
            code, line, heads_grad_ext[half], values[half], tap_lines(tap_rows[half][:, ::-1])
        )
        factor = jnp.exp(stats[half][:, 0] - lse_all[half]).reshape(side, 1, SEGS)
        dk, dv, lqg = third_back_call(
            keys[half],
            values[half],
            third_exp[half],
            factor,
            delta_all[half].reshape(side, 1, SEGS),
            carried_grad[half],
            land_q[half],
            back,
        )
        if half == 0:
            lqg = jnp.concatenate([lqg[:own] + small_query, lqg[own:]], axis=0)
            lkg = jnp.concatenate([lkg[:own] + small_key, lkg[own:]], axis=0)
        query_low.append(dq)
        key_low.append(dk)
        value_low.append(dv)
        land_qg.append(lqg.reshape(side_cols, SEGS).astype(BF))
        land_kg.append(lkg.reshape(side_cols, SEGS).astype(BF))
        tap_grads.append(tap_out[:, 0, :KW])

    def weight_grad(lows, lands, factor):
        parts = []
        for half in (0, 1):
            part = tn(lows[half], tokens_in)
            if lands is not None:
                part = part + nn(lands[half], land_tokens)
            parts.append((part * factor).astype(BF))
        return slot_sum(*slots_of(parts)).T

    grad_value = weight_grad(value_low, None, 1.0)
    grad_key = weight_grad(key_low, land_kg, QK_SCALE)
    grad_query = weight_grad(query_low, land_qg, QK_SCALE)

    land_back = sum(tn(land_qg[half], wq[half]) + tn(land_kg[half], wk[half]) for half in (0, 1))
    land_back = head_sum((QK_SCALE * land_back / counts[:, None]).astype(BF))
    scaled = sum(nn(query_low[half], wq[half]) + nn(key_low[half], wk[half]) for half in (0, 1))
    plain = sum(nn(value_low[half], wv[half]) for half in (0, 1))
    input_grad = (first_in_grad + QK_SCALE * scaled + plain + nn(member, land_back)).astype(BF)

    tap_keep = jnp.stack([part[:own] for part in tap_grads])
    tap_send = jnp.stack([part[own:] for part in tap_grads])
    tap_got = tap_keep + swap(tap_send, 1)
    tap_own = tap_got[0] + swap(tap_got[1], 2)
    norms = jnp.stack([grad_first_gain, grad_first_bias, grad_second_gain, grad_second_bias])
    for bit in (1, 2):
        norms = norms + swap(norms, bit)
    small = jnp.concatenate([norms, jnp.pad(tap_own, ((0, 0), (0, width - KW)))], axis=0)
    for b in range(batch_size.bit_length() - 1):
        small = small + swap_batch(small, 1 << b)
    return (
        layer_out,
        input_grad,
        grad_query,
        grad_key,
        grad_value,
        grad_output,
        small[4 : 4 + own, :KW],
        small[0],
        small[1],
        grad_inner,
        grad_outer,
        small[2],
        small[3],
    )


def solution(mesh):
    tokens = P(("batch", "head"), None)
    row = P("batch")
    cols = P(None, "head")
    lines = P("head", None)
    rep = P()
    return jax.shard_map(
        functools.partial(shards, mesh.shape["batch"]),
        mesh=mesh,
        in_specs=(
            tokens, row, row, row, cols, cols, cols, lines, lines,
            rep, rep, rep, rep, rep, rep, tokens,
        ),
        out_specs=(
            tokens, tokens, cols, cols, cols, lines, lines, rep, rep, cols, lines, rep, rep,
        ),
        check_vma=False,
    )
```

```python
import functools

import jax
import jax.numpy as jnp
from jax import lax
from jax.experimental import pallas as pl
from jax.experimental.pallas import tpu as pltpu
from jax.sharding import PartitionSpec as P

LAND = 64
KW = 33
HALF = KW // 2
HEAD_DIM = 64
NEWTON = 6
DOCS = 4
SEGS = DOCS * LAND
WIDE = 2 * SEGS
BLOCK = 128
CHUNK = 256
QK_SCALE = HEAD_DIM ** (-0.25)

NEG_FILL = -1e30
NORM_EPS = 1e-05
BF = jnp.bfloat16
F32 = jnp.float32


def norm_forward(hidden, scale_vec, shift_vec):
    center = hidden - jnp.mean(hidden, axis=-1, keepdims=True)
    inv_spread = lax.rsqrt(jnp.mean(center * center, axis=-1, keepdims=True) + NORM_EPS)
    normed = center * inv_spread
    return (normed * scale_vec + shift_vec, normed, inv_spread)


def norm_backward(upstream, normed, inv_spread, scale_vec):
    scaled = upstream * scale_vec
    result_grad = inv_spread * (
        scaled
        - jnp.mean(scaled, axis=-1, keepdims=True)
        - normed * jnp.mean(scaled * normed, axis=-1, keepdims=True)
    )
    return (result_grad, jnp.sum(upstream * normed, axis=0), jnp.sum(upstream, axis=0))


def nn(a, b):
    return lax.dot_general(a, b, (((1,), (0,)), ((), ())), preferred_element_type=F32)


def nt(a, b):
    return lax.dot_general(a, b, (((1,), (1,)), ((), ())), preferred_element_type=F32)


def tn(a, b):
    return lax.dot_general(a, b, (((0,), (0,)), ((), ())), preferred_element_type=F32)


def pair_block(ref):
    zero = jnp.zeros((HEAD_DIM, SEGS), BF)
    top = jnp.concatenate([ref[0, :HEAD_DIM, :].astype(BF), zero], axis=1)
    low = jnp.concatenate([zero, ref[1, :HEAD_DIM, :].astype(BF)], axis=1)
    return jnp.concatenate([top, low], axis=0)


def put_pair(ref, value):
    ref[0] = value[:HEAD_DIM, :SEGS].astype(ref.dtype)
    ref[1] = value[HEAD_DIM:, SEGS:].astype(ref.dtype)


def doc_bias(code):
    lane_doc = lax.broadcasted_iota(jnp.int32, (code.shape[0], SEGS), 1) // LAND
    return jnp.where(code == lane_doc, 0.0, NEG_FILL)


def rows_of(i, size, base=0):
    return pl.ds(pl.multiple_of(base + i * size, 16), size)


def third_kernel(code_ref, k_ref, v_ref, lq_ref, c_ref, e_ref, s_scr, acc):
    steps = k_ref.shape[0] // CHUNK
    lq2 = pair_block(lq_ref)

    def scores(i, top):
        r = rows_of(i, CHUNK)
        bias = doc_bias(code_ref[r, :])
        s = nn(k_ref[r, :], lq2) + jnp.concatenate([bias, bias], axis=1)
        s_scr[r, :] = s
        return jnp.maximum(top, jnp.max(s, axis=0, keepdims=True))

    top = lax.fori_loop(0, steps, scores, jnp.full((1, WIDE), 3.0 * NEG_FILL, F32), unroll=True)
    acc[...] = jnp.zeros_like(acc)

    def weigh(i, total):
        r = rows_of(i, CHUNK)
        e = jnp.exp(s_scr[r, :] - top)
        low = e.astype(BF)
        e_ref[r, :] = low
        acc[...] += tn(v_ref[rows_of(i, CHUNK, HALF), :], low)
        return total + jnp.sum(e, axis=0, keepdims=True)

    total = lax.fori_loop(0, steps, weigh, jnp.zeros((1, WIDE), F32), unroll=True)
    mean = acc[...] / total
    for side in (0, 1):
        cols = slice(side * SEGS, (side + 1) * SEGS)
        c_ref[side, :HEAD_DIM, :] = mean[side * HEAD_DIM : (side + 1) * HEAD_DIM, cols]
        low = [top[:, cols], total[:, cols], jnp.zeros((6, SEGS), F32)]
        c_ref[side, HEAD_DIM:, :] = jnp.concatenate(low, axis=0)


def skew(x, left):
    row = lax.broadcasted_iota(jnp.int32, x.shape, 0)
    lanes = x.shape[1]
    for bit in range(x.shape[0].bit_length() - 1):
        step = 1 << bit
        moved = pltpu.roll(x, lanes - step if left else step, 1)
        x = jnp.where((row & step) != 0, moved, x)
    return x


def band(w_ref, index):
    return skew(jnp.broadcast_to(w_ref[index], (BLOCK, 2 * BLOCK)), False).astype(BF)


def band_mask(code_ref, line_ref, i):
    line = line_ref[:, pl.ds(pl.multiple_of(i * BLOCK, BLOCK), 2 * BLOCK)]
    return code_ref[rows_of(i, BLOCK), :] == line


def first_kernel(code_ref, line_ref, q_ref, v_ref, lk_ref, w_ref, p_ref, conv_ref, t_scr):
    lk2 = pair_block(lk_ref)
    t_scr[0] = band(w_ref, 0)
    t_scr[1] = band(w_ref, 1)
    left_lane = lax.broadcasted_iota(jnp.int32, (BLOCK, BLOCK), 1) < HEAD_DIM

    def convolve(i, carry):
        mask = band_mask(code_ref, line_ref, i)
        window = v_ref[rows_of(i, BLOCK), :], v_ref[rows_of(i + 1, BLOCK), :]
        window = jnp.concatenate(window, axis=0)
        zero = jnp.zeros((BLOCK, 2 * BLOCK), BF)
        one = nn(jnp.where(mask, t_scr[0], zero), window)
        two = nn(jnp.where(mask, t_scr[1], zero), window)
        conv_ref[rows_of(i, BLOCK), :] = jnp.where(left_lane, one, two)
        return carry

    lax.fori_loop(0, q_ref.shape[0] // BLOCK, convolve, 0, unroll=True)

    def weigh(i, carry):
        r = rows_of(i, CHUNK)
        bias = doc_bias(code_ref[r, :])
        s = nn(q_ref[r, :], lk2)
        for side in (0, 1):
            cols = slice(side * SEGS, (side + 1) * SEGS)
            part = s[:, cols] + bias
            e = jnp.exp(part - jnp.max(part, axis=1, keepdims=True))
            p_ref[r, cols] = (e * (1.0 / jnp.sum(e, axis=1, keepdims=True))).astype(BF)
        return carry

    lax.fori_loop(0, q_ref.shape[0] // CHUNK, weigh, 0, unroll=True)


def heads_kernel(code_ref, p_ref, mix_ref, conv_ref, out_ref):
    mix2 = pair_block(mix_ref)

    def body(i, carry):
        r = rows_of(i, CHUNK)
        total = nt(p_ref[r, :], mix2) + conv_ref[r, :]
        out_ref[r, :] = jnp.where(code_ref[r, :] >= 0, total, 0.0).astype(BF)
        return carry

    lax.fori_loop(0, p_ref.shape[0] // CHUNK, body, 0, unroll=True)


def mixed_grad_kernel(hg_ref, p_ref, mg_ref):
    put_pair(mg_ref, tn(hg_ref[...], p_ref[...]))


def first_back_kernel(hg_ref, p_ref, q_ref, mix_ref, lk_ref, dq_ref, lkg_ref, acc):
    mix2 = pair_block(mix_ref)
    lk2 = pair_block(lk_ref)
    acc[...] = jnp.zeros_like(acc)

    def body(i, carry):
        r = rows_of(i, CHUNK)
        g = nn(hg_ref[r, :], mix2)
        parts = []
        for side in (0, 1):
            cols = slice(side * SEGS, (side + 1) * SEGS)
            p = p_ref[r, cols].astype(F32)
            gp = g[:, cols] * p
            parts.append((gp - p * jnp.sum(gp, axis=1, keepdims=True)).astype(BF))
        ds = jnp.concatenate(parts, axis=1)
        dq_ref[r, :] = nt(ds, lk2).astype(BF)
        acc[...] += tn(q_ref[r, :], ds)
        return carry

    lax.fori_loop(0, p_ref.shape[0] // CHUNK, body, 0, unroll=True)
    put_pair(lkg_ref, acc[...])


def conv_back_kernel(code_ref, line_ref, hgx_ref, v_ref, w_ref, back_ref, tap_ref, t_scr, acc):
    t_scr[0] = band(w_ref, 0)
    t_scr[1] = band(w_ref, 1)
    acc[...] = jnp.zeros_like(acc)
    left_lane = lax.broadcasted_iota(jnp.int32, (BLOCK, BLOCK), 1) < HEAD_DIM

    def body(i, carry):
        mask = band_mask(code_ref, line_ref, i)
        grads = hgx_ref[rows_of(i, BLOCK), :], hgx_ref[rows_of(i + 1, BLOCK), :]
        grads = jnp.concatenate(grads, axis=0)
        vals = v_ref[rows_of(i, BLOCK), :], v_ref[rows_of(i + 1, BLOCK), :]
        vals = jnp.concatenate(vals, axis=0)
        zero = jnp.zeros((BLOCK, 2 * BLOCK), BF)
        one = nn(jnp.where(mask, t_scr[0], zero), grads)
        two = nn(jnp.where(mask, t_scr[1], zero), grads)
        back_ref[rows_of(i, BLOCK), :] = jnp.where(left_lane, one, two)
        here = hgx_ref[rows_of(i, BLOCK, HALF), :]
        none = jnp.zeros_like(here)
        acc[0] += jnp.where(mask, nt(jnp.where(left_lane, here, none), vals), 0.0)
        acc[1] += jnp.where(mask, nt(jnp.where(left_lane, none, here), vals), 0.0)
        return carry

    lax.fori_loop(0, back_ref.shape[0] // BLOCK, body, 0, unroll=True)
    for side in (0, 1):
        tap_ref[side, 0:1, :] = jnp.sum(skew(acc[side], True), axis=0, keepdims=True)


def third_back_kernel(
    k_ref, v_ref, e_ref, f_ref, d_ref, cg_ref, lq_ref, back_ref, dk_ref, dv_ref, lqg_ref, acc
):
    cg2 = pair_block(cg_ref)
    lq2 = pair_block(lq_ref)
    factor = jnp.concatenate([f_ref[0], f_ref[1]], axis=1)
    delta = jnp.concatenate([d_ref[0], d_ref[1]], axis=1)
    acc[...] = jnp.zeros_like(acc)

    def body(i, carry):
        r = rows_of(i, CHUNK)
        h = nn(v_ref[rows_of(i, CHUNK, HALF), :], cg2)
        p = e_ref[r, :].astype(F32) * factor
        ds = (p * (h - delta)).astype(BF)
        dk_ref[r, :] = nt(ds, lq2).astype(BF)
        dv_ref[r, :] = (nt(p.astype(BF), cg2) + back_ref[r, :]).astype(BF)
        acc[...] += tn(k_ref[r, :], ds)
        return carry

    lax.fori_loop(0, e_ref.shape[0] // CHUNK, body, 0, unroll=True)
    put_pair(lqg_ref, acc[...])


def feed_kernel(x_ref, wi_ref, wo_ref, act_ref, slope_ref, out_ref):
    @pl.when(pl.program_id(0) == 0)
    def _():
        out_ref[...] = jnp.zeros_like(out_ref)

    def body(i, carry):
        r = rows_of(i, CHUNK)
        pre = nn(x_ref[r, :], wi_ref[...])
        cdf = 0.5 * (1.0 + lax.erf(pre * (0.5**0.5)))
        pdf = jnp.exp(-0.5 * pre * pre) * 0.3989422804014327
        act = (pre * cdf).astype(BF)
        act_ref[r, :] = act
        slope_ref[r, :] = (cdf + pre * pdf).astype(BF)
        out_ref[r, :] += nn(act, wo_ref[...])
        return carry

    lax.fori_loop(0, x_ref.shape[0] // CHUNK, body, 0, unroll=True)


def feed_back_kernel(
    table, og_ref, x_ref, wi_ref, wo_ref, act_ref, slope_ref, prev_ref, gi_ref, go_ref, fg_ref, pg
):
    @pl.when(pl.program_id(0) == 0)
    def _():
        fg_ref[...] = prev_ref[...]

    def body(i, carry):
        r = rows_of(i, CHUNK)
        grad = nt(og_ref[r, :], wo_ref[...])
        low = (slope_ref[r, :].astype(F32) * grad).astype(BF)
        pg[r, :] = low
        fg_ref[r, :] += nt(low, wi_ref[...])
        return carry

    lax.fori_loop(0, og_ref.shape[0] // CHUNK, body, 0, unroll=True)
    gi_ref[0] = tn(x_ref[...], pg[...]).astype(BF)
    go_ref[0] = tn(act_ref[...], og_ref[...]).astype(BF)


def split_low(a):
    high = a.astype(BF)
    return high, (a - high.astype(F32)).astype(BF)


def spread_docs(a):
    tall = jnp.concatenate([a] * DOCS, axis=0)
    row = lax.broadcasted_iota(jnp.int32, tall.shape, 0) // LAND
    lane = lax.broadcasted_iota(jnp.int32, tall.shape, 1) // LAND
    return jnp.where(row == lane, tall, jnp.zeros_like(tall))


def fold_docs(a):
    lane = lax.broadcasted_iota(jnp.int32, (LAND, SEGS), 1) // LAND
    out = a[:LAND]
    for doc in range(1, DOCS):
        out = jnp.where(lane == doc, a[doc * LAND : (doc + 1) * LAND], out)
    return out


def blocks_of(a):
    high, low = split_low(a)
    return spread_docs(high), spread_docs(low)


def times(a, blocks, form=nn):
    high, low = split_low(a)
    both = form(jnp.concatenate([high, low], axis=0), blocks[0])
    return both[:LAND] + (both[LAND:] + form(high, blocks[1]))


def cross(a, b):
    ah, al = split_low(a)
    bh, bl = split_low(b)
    return tn(ah, bh) + (tn(ah, bl) + tn(al, bh))


def doc_sum(a):
    line = jnp.sum(a, axis=0, keepdims=True)
    lane = lax.broadcasted_iota(jnp.int32, line.shape, 1) // LAND
    out = jnp.zeros_like(line)
    for doc in range(DOCS):
        part = jnp.sum(jnp.where(lane == doc, line, 0.0), axis=1, keepdims=True)
        out = jnp.where(lane == doc, part, out)
    return out


def eye_docs():
    row = lax.broadcasted_iota(jnp.int32, (LAND, SEGS), 0)
    lane = lax.broadcasted_iota(jnp.int32, (LAND, SEGS), 1) % LAND
    return jnp.where(row == lane, 1.0, 0.0)


def newton_kernel(lq_ref, lk_ref, inv_ref, at_ref, save_ref):
    heads = lq_ref.shape[0]
    eye = eye_docs()
    fixed, state = [], []
    for h in range(heads):
        scores = fold_docs(tn(lk_ref[h], lq_ref[h]))
        e = jnp.exp(scores - jnp.max(scores, axis=0, keepdims=True))
        at = e / jnp.sum(e, axis=0, keepdims=True)
        at_ref[h] = at
        blocks = blocks_of(at)
        fixed.append(blocks)
        state.append(times(eye, blocks, nt) / doc_sum(at * at))
    for step in range(NEWTON):
        x = [times(w, b) for w, b in zip(state, fixed)]
        t2 = [15.0 * eye - times(a, blocks_of(7.0 * eye - a)) for a in x]
        t3 = [13.0 * eye - times(a, blocks_of(b)) for a, b in zip(x, t2)]
        for h in range(heads):
            save_ref[step, h, 0] = state[h]
            save_ref[step, h, 1] = x[h]
            save_ref[step, h, 2] = t2[h]
            save_ref[step, h, 3] = t3[h]
        state = [0.25 * times(t, blocks_of(w)) for t, w in zip(t3, state)]
    for h in range(heads):
        inv_ref[h] = state[h]


def join_packs(a, b):
    top_a, top_b = a[HEAD_DIM : HEAD_DIM + 1], b[HEAD_DIM : HEAD_DIM + 1]
    top = jnp.maximum(top_a, top_b)
    share_a = a[HEAD_DIM + 1 : HEAD_DIM + 2] * jnp.exp(top_a - top)
    share_b = b[HEAD_DIM + 1 : HEAD_DIM + 2] * jnp.exp(top_b - top)
    total = share_a + share_b
    mean = (a[:HEAD_DIM] * share_a + b[:HEAD_DIM] * share_b) / total
    return mean, top, total


def join_kernel(a_ref, b_ref, o_ref):
    for h in range(a_ref.shape[0]):
        mean, top, total = join_packs(a_ref[h], b_ref[h])
        rest = jnp.zeros((6, SEGS), F32)
        o_ref[h] = jnp.concatenate([mean, top, total, rest], axis=0)


def three_parts(a):
    one = a.astype(BF)
    left = a - one.astype(F32)
    two = left.astype(BF)
    three = (left - two.astype(F32)).astype(BF)
    rows = [one.astype(F32), two.astype(F32), three.astype(F32), jnp.zeros((13, a.shape[1]), F32)]
    return jnp.concatenate(rows, axis=0).astype(BF)


def mix_kernel(a_ref, b_ref, inv_ref, mix_ref, carried_ref):
    for h in range(a_ref.shape[0]):
        mean, top, total = join_packs(a_ref[h], b_ref[h])
        carried_ref[h] = mean
        mix_ref[h, :HEAD_DIM, :] = times(mean, blocks_of(inv_ref[h])).astype(BF)
        mix_ref[h, HEAD_DIM:, :] = three_parts(top + jnp.log(total))


def carry_back_kernel(a_ref, b_ref, carried_ref, inv_ref, mg_ref, cg_ref):
    for h in range(a_ref.shape[0]):
        mg = a_ref[h] + b_ref[h]
        mg_ref[h] = mg
        cg = times(mg, blocks_of(inv_ref[h]), nt).astype(BF)
        cg_ref[h, :HEAD_DIM, :] = cg
        delta = jnp.sum(cg.astype(F32) * carried_ref[h], axis=0, keepdims=True)
        cg_ref[h, HEAD_DIM:, :] = three_parts(delta)


def newton_back_kernel(mg_ref, carried_ref, at_ref, save_ref, lq_ref, lk_ref, dq_ref, dk_ref, acc):
    heads = mg_ref.shape[0]
    eye = eye_docs()
    at = [at_ref[h] for h in range(heads)]
    fixed = [blocks_of(a) for a in at]
    grad = [fold_docs(cross(carried_ref[h], mg_ref[h])) for h in range(heads)]
    for step in reversed(range(NEWTON)):
        w, x, t2, t3 = ([save_ref[step, h, kind] for h in range(heads)] for kind in range(4))
        t3g = [0.25 * times(g, blocks_of(a), nt) for g, a in zip(grad, w)]
        wg = [0.25 * times(a, blocks_of(g)) for a, g in zip(t3, grad)]
        t2g = [-times(a, blocks_of(g)) for a, g in zip(x, t3g)]
        xg = [-times(g, blocks_of(a)) for g, a in zip(t3g, t2)]
        t1g = [-times(a, blocks_of(g)) for a, g in zip(x, t2g)]
        xg = [
            a - times(g, blocks_of(7.0 * eye - b)) - c
            for a, g, b, c in zip(xg, t2g, x, t1g)
        ]
        grad = [a + times(g, b, nt) for a, g, b in zip(wg, xg, fixed)]
        for h in range(heads):
            part = cross(w[h], xg[h])
            acc[h] = part if step == NEWTON - 1 else acc[h] + part
    for h in range(heads):
        square = doc_sum(at[h] * at[h])
        start = times(eye, fixed[h], nt)
        start_grad = grad[h] / square - start * (2.0 * doc_sum(grad[h] * start) / (square * square))
        atg = fold_docs(acc[h]) + times(eye, blocks_of(start_grad), nt)
        sg = at[h] * (atg - jnp.sum(atg * at[h], axis=0, keepdims=True))
        blocks = blocks_of(sg)
        dq_ref[h] = nn(lk_ref[h], blocks[0]) + nn(lk_ref[h], blocks[1])
        dk_ref[h] = nt(lq_ref[h], blocks[0]) + nt(lq_ref[h], blocks[1])


def call(body, grid, ins, outs, scratch=(), flops=0, moved=0, exps=0, limit=40):
    return pl.pallas_call(
        body,
        grid=grid,
        in_specs=[spec for spec in ins],
        out_specs=[spec for spec, _ in outs],
        out_shape=[shape for _, shape in outs],
        scratch_shapes=list(scratch),
        compiler_params=pltpu.CompilerParams(vmem_limit_bytes=limit << 20),
        cost_estimate=pl.CostEstimate(flops=flops, bytes_accessed=moved, transcendentals=exps),
    )


def plain(body, outs, scratch=(), flops=0, moved=0, limit=40):
    return pl.pallas_call(
        body,
        out_shape=list(outs),
        scratch_shapes=list(scratch),
        compiler_params=pltpu.CompilerParams(vmem_limit_bytes=limit << 20),
        cost_estimate=pl.CostEstimate(flops=flops, bytes_accessed=moved, transcendentals=0),
    )


def whole(shape):
    return pl.BlockSpec(shape, lambda p: (0,) * len(shape))


def column(rows, width):
    return pl.BlockSpec((rows, width), lambda p: (0, p))


def heads_spec(rows, cols):
    return pl.BlockSpec((2, rows, cols), lambda p: (p, 0, 0))


def shape_of(shape, dtype):
    return jax.ShapeDtypeStruct(shape, dtype)


def shards(
    batch_size,
    tokens_in,
    doc_ids,
    landmark_ids,
    pad_mask,
    w_query,
    w_key,
    w_value,
    w_output,
    conv_weight,
    first_gain,
    first_bias,
    w_inner,
    w_outer,
    second_gain,
    second_bias,
    out_grad,
):
    groups = 4
    rows, width = tokens_in.shape
    local = w_query.shape[1]
    own = local // HEAD_DIM
    side = 2 * own
    side_cols = 2 * local
    pairs = side // 2
    ext = rows + BLOCK
    ff = w_inner.shape[1]
    me = lax.axis_index("head")
    bat = lax.axis_index("batch")
    core = me & 1

    def swap(value, bit, name="swap"):
        with jax.named_scope(name):
            return lax.ppermute(value, "head", [(i, i ^ bit) for i in range(groups)])

    def swap_batch(value, bit, name="swap"):
        with jax.named_scope(name):
            return lax.ppermute(value, "batch", [(i, i ^ bit) for i in range(batch_size)])

    def spread(value):
        two = swap(value, 2)
        return value, swap(value, 1), two, swap(two, 1)

    def add_low(a, b):
        return (a.astype(F32) + b.astype(F32)).astype(BF)

    def gate(*values):
        return lax.optimization_barrier(values)

    def ordered(low_bit, mine, other):
        first = jnp.where(low_bit == 0, mine, other)
        second = jnp.where(low_bit == 0, other, mine)
        return jnp.concatenate([first, second], axis=0)

    def halves(value, flag):
        half = value.shape[0] // 2
        mine = lax.dynamic_slice_in_dim(value, flag * half, half, 0)
        return mine, lax.dynamic_slice_in_dim(value, (1 - flag) * half, half, 0)

    def head_sum(value):
        mine, other = halves(value, core)
        mine = mine + swap(other, 1)
        mine = mine + swap(mine, 2)
        return ordered(core, mine, swap(mine, 1))

    bits = [1 << b for b in range(batch_size.bit_length() - 1)]

    def gather_heads(value):
        got = lax.all_gather(value, "head", axis=0, tiled=False)
        parts = [lax.dynamic_index_in_dim(got, me ^ slot, 0, False) for slot in range(groups)]
        return [jnp.concatenate(parts[2 * half : 2 * half + 2], axis=0) for half in (0, 1)]

    code_row = jnp.where(pad_mask > 0, doc_ids, -1)
    outside = jnp.full((BLOCK - HALF,), -2, jnp.int32)
    code_pad = jnp.concatenate([outside[:HALF], code_row, outside])
    line = lax.dynamic_slice_in_dim(code_pad, me * rows, ext, 0)
    code = line[HALF : HALF + rows].reshape(rows, 1)
    line = line.reshape(1, ext)
    segment_row = jnp.where(pad_mask > 0, doc_ids * LAND + landmark_ids, -1)
    columns = jnp.arange(SEGS, dtype=jnp.int32)
    counts = jnp.sum((segment_row[:, None] == columns[None, :]).astype(F32), axis=0)
    segment = lax.dynamic_slice_in_dim(segment_row, me * rows, rows, 0)
    member = (segment[:, None] == columns[None, :]).astype(BF)

    packed = jnp.concatenate([w_query.T, w_key.T, w_value.T], axis=0)
    got = spread(packed)
    tap_pad = jnp.pad(conv_weight, ((0, 16 - own), (0, width - KW)))
    out_parts = spread(jnp.concatenate([w_output, tap_pad], axis=0))

    def weight_half(half, index):
        return jnp.concatenate(
            [got[2 * half + j][index * local : (index + 1) * local] for j in (0, 1)], axis=0
        )

    wq, wk, wv = ([weight_half(half, index) for half in (0, 1)] for index in range(3))
    wo = [
        jnp.concatenate([out_parts[2 * half + j][:local] for j in (0, 1)], axis=0)
        for half in (0, 1)
    ]
    tap_rows = [
        jnp.concatenate([out_parts[2 * half + j][local : local + own, :KW] for j in (0, 1)], axis=0)
        for half in (0, 1)
    ]

    def tap_lines(value):
        value = jnp.pad(value.astype(F32), ((0, 0), (0, 2 * BLOCK - KW)))
        return value.reshape(side, 1, 2 * BLOCK)

    def with_edges(value):
        before = lax.ppermute(value[-HALF:], "head", [(i, i + 1) for i in range(groups - 1)])
        after = lax.ppermute(value[:HALF], "head", [(i + 1, i) for i in range(groups - 1)])
        rest = jnp.zeros((BLOCK - 2 * HALF, value.shape[1]), value.dtype)
        return jnp.concatenate([before, value, after, rest], axis=0)

    tokens_ext = with_edges(tokens_in)

    land_part = tn(member, tokens_in) / counts[:, None]
    land_sum = head_sum(land_part)
    land_tokens, land_rest = split_low(land_sum)

    queries, keys, values, land_q, land_k = [], [], [], [], []
    for half in (0, 1):
        queries.append((nt(tokens_in, wq[half]) * QK_SCALE).astype(BF))
        keys.append((nt(tokens_in, wk[half]) * QK_SCALE).astype(BF))
        values.append(nt(tokens_ext, wv[half]).astype(BF))
        for weight, target in ((wq, land_q), (wk, land_k)):
            mapped = nt(weight[half], land_tokens) + nt(weight[half], land_rest)
            mapped = (mapped * QK_SCALE).astype(BF)
            target.append(mapped.reshape(side, HEAD_DIM, SEGS))

    third_call = call(
        third_kernel,
        (pairs,),
        [whole((rows, 1)), column(rows, BLOCK), column(ext, BLOCK), heads_spec(HEAD_DIM, SEGS)],
        [
            (heads_spec(HEAD_DIM + 8, SEGS), shape_of((side, HEAD_DIM + 8, SEGS), F32)),
            (column(rows, WIDE), shape_of((rows, side * SEGS), BF)),
        ],
        [pltpu.VMEM((rows, WIDE), F32), pltpu.VMEM((BLOCK, WIDE), F32)],
        flops=4 * rows * side_cols * SEGS,
        moved=2 * rows * (side_cols * 2 + side * SEGS),
        exps=rows * side * SEGS,
    )
    packs, third_exp = [], []
    for half in (0, 1):
        pack, e_out = third_call(code, keys[half], values[half], land_q[half])
        packs.append(pack)
        third_exp.append(e_out)

    docs_shape = shape_of((own, HEAD_DIM, SEGS), F32)
    own_q, own_k = land_q[0][:own], land_k[0][:own]
    inverse, small_t, saved = plain(
        newton_kernel,
        [docs_shape, docs_shape, shape_of((NEWTON, own, 4, HEAD_DIM, SEGS), F32)],
        flops=own * NEWTON * 4 * 6 * LAND * SEGS * SEGS,
        moved=4 * own * NEWTON * 4 * HEAD_DIM * SEGS,
    )(own_q, own_k)

    tall = HEAD_DIM + 8
    pack_keep = jnp.concatenate([part[:own] for part in packs], axis=0)
    pack_send = jnp.concatenate([part[own:] for part in packs], axis=0)
    joined = plain(join_kernel, [shape_of((side, tall, SEGS), F32)], moved=12 * side * tall * SEGS)(
        pack_keep, swap(pack_send, 1)
    )[0]
    mixed_own, carried = plain(
        mix_kernel,
        [shape_of((own, HEAD_DIM + 16, SEGS), BF), docs_shape],
        flops=6 * own * LAND * SEGS * SEGS,
        moved=16 * own * tall * SEGS,
    )(joined[:own], swap(joined[own:], 2), inverse)
    mixed = gather_heads(mixed_own)

    def row_of(parts):
        return [
            jnp.sum(part[:, HEAD_DIM : HEAD_DIM + 3].astype(F32), axis=1, keepdims=True)
            for part in parts
        ]

    first_call = call(
        first_kernel,
        (pairs,),
        [
            whole((rows, 1)),
            whole((1, ext)),
            column(rows, BLOCK),
            column(ext, BLOCK),
            heads_spec(HEAD_DIM, SEGS),
            heads_spec(1, 2 * BLOCK),
        ],
        [
            (column(rows, WIDE), shape_of((rows, side * SEGS), BF)),
            (column(rows, BLOCK), shape_of((rows, side_cols), F32)),
        ],
        [pltpu.VMEM((2, BLOCK, 2 * BLOCK), BF)],
        flops=4 * rows * side_cols * SEGS,
        moved=2 * rows * (side_cols * 4 + side * SEGS),
        exps=rows * side * SEGS,
    )
    heads_call = call(
        heads_kernel,
        (pairs,),
        [whole((rows, 1)), column(rows, WIDE), heads_spec(HEAD_DIM + 16, SEGS), column(rows, BLOCK)],
        [(column(rows, BLOCK), shape_of((rows, side_cols), BF))],
        flops=2 * rows * side_cols * SEGS,
        moved=2 * rows * (side_cols * 3 + side * SEGS),
    )
    first_low, heads_out = [], []
    for half in (0, 1):
        p_out, conv_out = first_call(
            code, line, queries[half], values[half], land_k[half], tap_lines(tap_rows[half])
        )
        first_low.append(p_out)
        heads_out.append(heads_call(code, p_out, mixed[half], conv_out)[0])

    projected = nn(heads_out[0], wo[0]) + nn(heads_out[1], wo[1])
    first_out, first_normed, first_inv = norm_forward(
        tokens_in.astype(F32) + projected, first_gain, first_bias
    )
    norm_low = first_out.astype(BF)

    block = 512 if ff % 512 == 0 else ff
    act, slope, outer_out = call(
        feed_kernel,
        (ff // block,),
        [whole((rows, width)), column(width, block), pl.BlockSpec((block, width), lambda p: (p, 0))],
        [
            (column(rows, block), shape_of((rows, ff), BF)),
            (column(rows, block), shape_of((rows, ff), BF)),
            (whole((rows, width)), shape_of((rows, width), F32)),
        ],
        flops=4 * rows * width * ff,
        moved=2 * (2 * width * ff + 2 * rows * ff + 3 * rows * width),
        exps=2 * rows * ff,
    )(norm_low, w_inner, w_outer)
    second_out, second_normed, second_inv = norm_forward(
        first_out + outer_out, second_gain, second_bias
    )
    layer_out = second_out.astype(BF)
    second_grad, grad_second_gain, grad_second_bias = norm_backward(
        out_grad.astype(F32), second_normed, second_inv, second_gain
    )
    outer_low = second_grad.astype(BF)

    share = ff // groups
    cut = share // 2

    def feed_back(slots, previous):
        table = jnp.stack([(me ^ slot) * 2 + part for slot in slots for part in (0, 1)])
        grid_spec = pltpu.PrefetchScalarGridSpec(
            num_scalar_prefetch=1,
            grid=(2 * len(slots),),
            in_specs=[
                pl.BlockSpec((rows, width), lambda p, t: (0, 0)),
                pl.BlockSpec((rows, width), lambda p, t: (0, 0)),
                pl.BlockSpec((width, cut), lambda p, t: (0, t[p])),
                pl.BlockSpec((cut, width), lambda p, t: (t[p], 0)),
                pl.BlockSpec((rows, cut), lambda p, t: (0, t[p])),
                pl.BlockSpec((rows, cut), lambda p, t: (0, t[p])),
                pl.BlockSpec((rows, width), lambda p, t: (0, 0)),
            ],
            out_specs=[
                pl.BlockSpec((1, width, cut), lambda p, t: (p // 2, 0, p % 2)),
                pl.BlockSpec((1, cut, width), lambda p, t: (p // 2, p % 2, 0)),
                pl.BlockSpec((rows, width), lambda p, t: (0, 0)),
            ],
            scratch_shapes=[pltpu.VMEM((rows, cut), BF)],
        )
        return pl.pallas_call(
            feed_back_kernel,
            grid_spec=grid_spec,
            out_shape=[
                shape_of((len(slots), width, share), BF),
                shape_of((len(slots), share, width), BF),
                shape_of((rows, width), F32),
            ],
            compiler_params=pltpu.CompilerParams(vmem_limit_bytes=48 << 20),
            cost_estimate=pl.CostEstimate(
                flops=8 * rows * width * share * len(slots),
                bytes_accessed=2 * len(slots) * share * (4 * width + 2 * rows) + 12 * rows * width,
                transcendentals=0,
            ),
        )(table, outer_low, norm_low, w_inner, w_outer, act, slope, previous)

    gi_send, go_send, first_grad = feed_back((1, 3), second_grad)
    gi_core, go_core = swap(gi_send, 1, "inner_core"), swap(go_send, 1, "outer_core")
    gi_keep, go_keep, first_grad = feed_back((0, 2), first_grad)
    first_grad, gi_core, go_core = gate(first_grad, gi_core, go_core)
    inner_far = swap(add_low(gi_keep[1], gi_core[1]), 2, "inner_x")
    outer_flags = [jnp.where((bat & bit) != 0, 1, 0) for bit in bits]

    def split_rows(value, flag):
        half = value.shape[1] // 2
        mine = lax.dynamic_slice_in_dim(value, flag * half, half, 1)
        return mine, lax.dynamic_slice_in_dim(value, (1 - flag) * half, half, 1)

    own_keep, other_keep = split_rows(go_keep, outer_flags[0])
    own_core, other_core = split_rows(go_core, outer_flags[0])
    outer_near = swap_batch(add_low(other_keep, other_core), bits[0], "outer_y")
    first_in_grad, grad_first_gain, grad_first_bias = norm_backward(
        first_grad, first_normed, first_inv, first_gain
    )
    proj_low = first_in_grad.astype(BF)

    proj_ext = with_edges(proj_low)
    real_ext = line.reshape(ext, 1) >= 0
    heads_grad_ext = [
        jnp.where(real_ext, nt(proj_ext, wo[half]), 0.0).astype(BF) for half in (0, 1)
    ]
    heads_grad = [part[HALF : HALF + rows] for part in heads_grad_ext]

    mixed_grad_call = call(
        mixed_grad_kernel,
        (pairs,),
        [column(rows, BLOCK), column(rows, WIDE)],
        [(heads_spec(HEAD_DIM, SEGS), shape_of((side, HEAD_DIM, SEGS), F32))],
        flops=2 * rows * side_cols * SEGS,
        moved=2 * rows * (side_cols + side * SEGS),
    )
    mixed_part = [mixed_grad_call(heads_grad[half], first_low[half])[0] for half in (0, 1)]

    mg_keep = jnp.concatenate([part[:own] for part in mixed_part], axis=0)
    mg_send = jnp.concatenate([part[own:] for part in mixed_part], axis=0)
    mg_sum = mg_keep + swap(mg_send, 1)
    mixed_grad, carried_low = plain(
        carry_back_kernel,
        [docs_shape, shape_of((own, HEAD_DIM + 16, SEGS), BF)],
        flops=6 * own * LAND * SEGS * SEGS,
        moved=24 * own * tall * SEGS,
    )(mg_sum[:own], swap(mg_sum[own:], 2), carried, inverse)
    carried_grad = gather_heads(carried_low)
    small_query, small_key = plain(
        newton_back_kernel,
        [docs_shape, docs_shape],
        [pltpu.VMEM((own, SEGS, SEGS), F32)],
        flops=own * NEWTON * 8 * 6 * LAND * SEGS * SEGS,
        moved=4 * own * NEWTON * 4 * HEAD_DIM * SEGS,
    )(mixed_grad, carried, small_t, saved, own_q, own_k)
    delta_all, lse_all = row_of(carried_grad), row_of(mixed)

    first_back_call = call(
        first_back_kernel,
        (pairs,),
        [
            column(rows, BLOCK),
            column(rows, WIDE),
            column(rows, BLOCK),
            heads_spec(HEAD_DIM + 16, SEGS),
            heads_spec(HEAD_DIM, SEGS),
        ],
        [
            (column(rows, BLOCK), shape_of((rows, side_cols), BF)),
            (heads_spec(HEAD_DIM, SEGS), shape_of((side, HEAD_DIM, SEGS), F32)),
        ],
        [pltpu.VMEM((BLOCK, WIDE), F32)],
        flops=6 * rows * side_cols * SEGS,
        moved=2 * rows * (side_cols * 3 + side * SEGS),
    )
    conv_back_call = call(
        conv_back_kernel,
        (pairs,),
        [
            whole((rows, 1)),
            whole((1, ext)),
            column(ext, BLOCK),
            column(ext, BLOCK),
            heads_spec(1, 2 * BLOCK),
        ],
        [
            (column(rows, BLOCK), shape_of((rows, side_cols), F32)),
            (heads_spec(8, 2 * BLOCK), shape_of((side, 8, 2 * BLOCK), F32)),
        ],
        [pltpu.VMEM((2, BLOCK, 2 * BLOCK), BF), pltpu.VMEM((2, BLOCK, 2 * BLOCK), F32)],
        flops=4 * rows * side_cols * SEGS,
        moved=2 * rows * side_cols * 4,
    )
    third_back_call = call(
        third_back_kernel,
        (pairs,),
        [
            column(rows, BLOCK),
            column(ext, BLOCK),
            column(rows, WIDE),
            heads_spec(1, SEGS),
            heads_spec(1, SEGS),
            heads_spec(HEAD_DIM + 16, SEGS),
            heads_spec(HEAD_DIM, SEGS),
            column(rows, BLOCK),
        ],
        [
            (column(rows, BLOCK), shape_of((rows, side_cols), BF)),
            (column(rows, BLOCK), shape_of((rows, side_cols), BF)),
            (heads_spec(HEAD_DIM, SEGS), shape_of((side, HEAD_DIM, SEGS), F32)),
        ],
        [pltpu.VMEM((BLOCK, WIDE), F32)],
        flops=8 * rows * side_cols * SEGS,
        moved=2 * rows * (side_cols * 6 + side * SEGS),
    )
    def hop_sum(value, got):
        return (value.astype(F32) + got.astype(F32)).astype(BF)

    def slot_parts(parts):
        cut_rows = parts[0].shape[0] // 2
        keep = [part[:cut_rows] for part in parts]
        send = jnp.stack([part[cut_rows:] for part in parts])
        return keep, send

    out_keep, out_send = slot_parts([tn(part, proj_low).astype(BF) for part in heads_out])
    out_core = swap(out_send, 1, "out_core")

    dq_parts, lkg_parts, backs, tap_grads = [], [], [], []
    for half in (0, 1):
        dq, lkg = first_back_call(
            heads_grad[half], first_low[half], queries[half], mixed[half], land_k[half]
        )
        dq_parts.append(dq)
        lkg_parts.append(lkg)

    conv_in, lkg_parts[1], inner_far, outer_near, out_core = gate(
        heads_grad_ext[0], lkg_parts[1], inner_far, outer_near, out_core
    )
    inner = (gi_keep[0].astype(F32) + gi_core[0].astype(F32) + inner_far.astype(F32)).astype(BF)
    inner, other = halves(inner, outer_flags[0])
    inner_hop = swap_batch(other, bits[0], "inner_y")
    outer = (own_keep.astype(F32) + own_core.astype(F32) + outer_near.astype(F32)).astype(BF)
    outer, other = split_rows(outer, outer_flags[1])
    outer_hop = swap_batch(other, bits[1], "outer_z")
    out_far = swap(add_low(out_keep[1], out_core[1]), 2, "out_x")
    for half in (0, 1):
        back, tap_out = conv_back_call(
            code, line, (conv_in, heads_grad_ext[1])[half], values[half],
            tap_lines(tap_rows[half][:, ::-1]),
        )
        backs.append(back)
        tap_grads.append(tap_out[:, 0, :KW])

    exp_in, small_query, inner_hop, outer_hop, out_far = gate(
        third_exp[0], small_query, inner_hop, outer_hop, out_far
    )
    inner, other = halves(hop_sum(inner, inner_hop), outer_flags[1])
    inner_hop = swap_batch(other, bits[1], "inner_z")
    outer, other = split_rows(hop_sum(outer, outer_hop), outer_flags[2])
    outer_hop = swap_batch(other, bits[2], "outer_w")
    out_sum = out_keep[0].astype(F32) + out_core[0].astype(F32) + out_far.astype(F32)
    out_sum = out_sum.astype(BF)
    out_hop = swap_batch(out_sum, bits[0], "out_y")

    dk_parts, dv_parts, lqg_parts = [], [], []
    for half in (0, 1):
        factor = jnp.exp(packs[half][:, HEAD_DIM : HEAD_DIM + 1] - lse_all[half])
        dk, dv, lqg = third_back_call(
            keys[half],
            values[half],
            (exp_in, third_exp[1])[half],
            factor,
            delta_all[half],
            carried_grad[half],
            land_q[half],
            backs[half],
        )
        dk_parts.append(dk)
        dv_parts.append(dv)
        lqg_parts.append(lqg)
    lqg_parts[0] = jnp.concatenate([lqg_parts[0][:own] + small_query, lqg_parts[0][own:]], axis=0)
    lkg_parts[0] = jnp.concatenate([lkg_parts[0][:own] + small_key, lkg_parts[0][own:]], axis=0)
    land_qg = [part.reshape(side_cols, SEGS).astype(BF) for part in lqg_parts]
    land_kg = [part.reshape(side_cols, SEGS).astype(BF) for part in lkg_parts]

    def weight_parts(lows, lands, factor):
        parts = []
        for half in (0, 1):
            part = tn(lows[half], tokens_in)
            if lands is not None:
                part = part + nn(lands[half], land_tokens)
            parts.append((part * factor).astype(BF))
        return slot_parts(parts)

    val_keep, val_send = weight_parts(dv_parts, None, 1.0)
    val_core = swap(val_send, 1, "val_core")
    dk_parts[1], inner_hop, outer_hop, out_hop = gate(dk_parts[1], inner_hop, outer_hop, out_hop)
    inner, other = halves(hop_sum(inner, inner_hop), outer_flags[2])
    inner_hop = swap_batch(other, bits[2], "inner_w")
    outer = hop_sum(outer, outer_hop)
    outer_hop = swap(outer[1], 2, "outer_x")
    out_sum = hop_sum(out_sum, out_hop)
    out_hop = swap_batch(out_sum, bits[1], "out_z")

    key_keep, key_send = weight_parts(dk_parts, land_kg, QK_SCALE)
    key_core = swap(key_send, 1, "key_core")
    val_far = swap(add_low(val_keep[1], val_core[1]), 2, "val_x")
    que_keep, que_send = weight_parts(dq_parts, land_qg, QK_SCALE)
    que_core = swap(que_send, 1, "que_core")
    key_far = swap(add_low(key_keep[1], key_core[1]), 2, "key_x")

    que_core, inner_hop, outer_hop, out_hop = gate(que_core, inner_hop, outer_hop, out_hop)
    que_far = swap(add_low(que_keep[1], que_core[1]), 2, "que_x")
    inner = hop_sum(inner, inner_hop)
    outer = hop_sum(outer[0], outer_hop)
    out_sum = hop_sum(out_sum, out_hop)
    inner_hop = swap_batch(inner, bits[2], "inner_w2")
    outer_hop = swap_batch(outer, bits[2], "outer_w2")
    out_hop = swap_batch(out_sum, bits[2], "out_w")
    land_back = sum(tn(land_qg[half], wq[half]) + tn(land_kg[half], wk[half]) for half in (0, 1))
    land_back = head_sum(QK_SCALE * land_back / counts[:, None]).astype(BF)
    scaled = sum(nn(dq_parts[half], wq[half]) + nn(dk_parts[half], wk[half]) for half in (0, 1))
    direct = sum(nn(dv_parts[half], wv[half]) for half in (0, 1))
    input_grad = (first_in_grad + QK_SCALE * scaled + direct + nn(member, land_back)).astype(BF)

    tails = []
    for keep, near, far, order, name in (
        (val_keep, val_core, val_far, (0, 1, 2), "val"),
        (key_keep, key_core, key_far, (1, 2, 0), "key"),
        (que_keep, que_core, que_far, (2, 0, 1), "que"),
    ):
        total = keep[0].astype(F32) + near[0].astype(F32) + far.astype(F32)
        tails.append((total.astype(BF), order, name))
    inner = ordered(outer_flags[2], inner, inner_hop)
    outer = ordered(outer_flags[2], outer, outer_hop)
    out_sum = hop_sum(out_sum, out_hop)
    for bit in bits[3:]:
        inner = hop_sum(inner, swap_batch(inner, bit, "inner_more"))
        outer = hop_sum(outer, swap_batch(outer, bit, "outer_more"))
        out_sum = hop_sum(out_sum, swap_batch(out_sum, bit, "out_more"))
    grad_output = out_sum.astype(F32)
    inner = ordered(outer_flags[1], inner, swap_batch(inner, bits[1], "inner_z2"))
    outer = ordered(outer_flags[1], outer, swap_batch(outer, bits[1], "outer_z2"))
    grad_inner = ordered(outer_flags[0], inner, swap_batch(inner, bits[0], "inner_y2")).astype(F32)
    grad_outer = ordered(outer_flags[0], outer, swap_batch(outer, bits[0], "outer_y2")).astype(F32)
    sums = []
    for total, order, name in tails:
        for index in order + tuple(range(3, len(bits))):
            total = hop_sum(total, swap_batch(total, bits[index], name))
        sums.append(total.astype(F32).T)
    grad_value, grad_key, grad_query = sums

    norms = jnp.stack([grad_first_gain, grad_first_bias, grad_second_gain, grad_second_bias])
    tap_lines_own = [jnp.pad(part, ((0, 0), (0, width - KW))) for part in tap_grads]
    keep = jnp.concatenate([norms] + [part[:own] for part in tap_lines_own], axis=0)
    send = jnp.concatenate([norms] + [part[own:] for part in tap_lines_own], axis=0)
    keep = keep + swap(send, 1)
    small = keep[: 4 + own] + swap(jnp.concatenate([keep[:4], keep[4 + own :]], axis=0), 2)
    for bit in bits:
        small = small + swap_batch(small, bit)
    return (
        layer_out,
        input_grad,
        grad_query,
        grad_key,
        grad_value,
        grad_output,
        small[4 : 4 + own, :KW],
        small[0],
        small[1],
        grad_inner,
        grad_outer,
        small[2],
        small[3],
    )


def solution(mesh):
    tokens = P(("batch", "head"), None)
    row = P("batch")
    cols = P(None, "head")
    lines = P("head", None)
    rep = P()
    return jax.shard_map(
        functools.partial(shards, mesh.shape["batch"]),
        mesh=mesh,
        in_specs=(
            tokens, row, row, row, cols, cols, cols, lines, lines,
            rep, rep, rep, rep, rep, rep, tokens,
        ),
        out_specs=(
            tokens, tokens, cols, cols, cols, lines, lines, rep, rep, cols, lines, rep, rep,
        ),
        check_vma=False,
    )
```

```python
import functools

import jax
import jax.numpy as jnp
from jax import lax
from jax.experimental import pallas as pl
from jax.experimental.pallas import tpu as pltpu
from jax.sharding import PartitionSpec as P

LAND = 64
KW = 33
HALF = KW // 2
HEAD_DIM = 64
NEWTON = 6
DOCS = 4
SEGS = DOCS * LAND
WIDE = 2 * SEGS
BLOCK = 128
CHUNK = 256
QK_SCALE = HEAD_DIM ** (-0.25)
FAR_TYPE = jnp.bfloat16

NEG_FILL = -1e30
NORM_EPS = 1e-05
BF = jnp.bfloat16
F32 = jnp.float32


def norm_forward(hidden, scale_vec, shift_vec):
    center = hidden - jnp.mean(hidden, axis=-1, keepdims=True)
    inv_spread = lax.rsqrt(jnp.mean(center * center, axis=-1, keepdims=True) + NORM_EPS)
    normed = center * inv_spread
    return (normed * scale_vec + shift_vec, normed, inv_spread)


def norm_backward(upstream, normed, inv_spread, scale_vec):
    scaled = upstream * scale_vec
    result_grad = inv_spread * (
        scaled
        - jnp.mean(scaled, axis=-1, keepdims=True)
        - normed * jnp.mean(scaled * normed, axis=-1, keepdims=True)
    )
    return (result_grad, jnp.sum(upstream * normed, axis=0), jnp.sum(upstream, axis=0))


def nn(a, b):
    return lax.dot_general(a, b, (((1,), (0,)), ((), ())), preferred_element_type=F32)


def nt(a, b):
    return lax.dot_general(a, b, (((1,), (1,)), ((), ())), preferred_element_type=F32)


def tn(a, b):
    return lax.dot_general(a, b, (((0,), (0,)), ((), ())), preferred_element_type=F32)


def pair_block(ref):
    zero = jnp.zeros((HEAD_DIM, SEGS), BF)
    top = jnp.concatenate([ref[0, :HEAD_DIM, :].astype(BF), zero], axis=1)
    low = jnp.concatenate([zero, ref[1, :HEAD_DIM, :].astype(BF)], axis=1)
    return jnp.concatenate([top, low], axis=0)


def put_pair(ref, value):
    ref[0] = value[:HEAD_DIM, :SEGS].astype(ref.dtype)
    ref[1] = value[HEAD_DIM:, SEGS:].astype(ref.dtype)


def doc_bias(code):
    lane_doc = lax.broadcasted_iota(jnp.int32, (code.shape[0], SEGS), 1) // LAND
    return jnp.where(code == lane_doc, 0.0, NEG_FILL)


def rows_of(i, size, base=0):
    return pl.ds(pl.multiple_of(base + i * size, 16), size)


def third_kernel(code_ref, k_ref, v_ref, lq_ref, c_ref, e_ref, s_scr, acc):
    steps = k_ref.shape[0] // CHUNK
    lq2 = pair_block(lq_ref)

    def scores(i, top):
        r = rows_of(i, CHUNK)
        bias = doc_bias(code_ref[r, :])
        s = nn(k_ref[r, :], lq2) + jnp.concatenate([bias, bias], axis=1)
        s_scr[r, :] = s
        return jnp.maximum(top, jnp.max(s, axis=0, keepdims=True))

    top = lax.fori_loop(0, steps, scores, jnp.full((1, WIDE), 3.0 * NEG_FILL, F32), unroll=True)
    acc[...] = jnp.zeros_like(acc)

    def weigh(i, total):
        r = rows_of(i, CHUNK)
        e = jnp.exp(s_scr[r, :] - top)
        low = e.astype(BF)
        e_ref[r, :] = low
        acc[...] += tn(v_ref[rows_of(i, CHUNK, HALF), :], low)
        return total + jnp.sum(e, axis=0, keepdims=True)

    total = lax.fori_loop(0, steps, weigh, jnp.zeros((1, WIDE), F32), unroll=True)
    mean = acc[...] / total
    for side in (0, 1):
        cols = slice(side * SEGS, (side + 1) * SEGS)
        c_ref[side, :HEAD_DIM, :] = mean[side * HEAD_DIM : (side + 1) * HEAD_DIM, cols]
        low = [top[:, cols], total[:, cols], jnp.zeros((6, SEGS), F32)]
        c_ref[side, HEAD_DIM:, :] = jnp.concatenate(low, axis=0)


def skew(x, left):
    row = lax.broadcasted_iota(jnp.int32, x.shape, 0)
    lanes = x.shape[1]
    for bit in range(x.shape[0].bit_length() - 1):
        step = 1 << bit
        moved = pltpu.roll(x, lanes - step if left else step, 1)
        x = jnp.where((row & step) != 0, moved, x)
    return x


def band(w_ref, index):
    return skew(jnp.broadcast_to(w_ref[index], (BLOCK, 2 * BLOCK)), False).astype(BF)


def band_mask(code_ref, line_ref, i):
    line = line_ref[:, pl.ds(pl.multiple_of(i * BLOCK, BLOCK), 2 * BLOCK)]
    return code_ref[rows_of(i, BLOCK), :] == line


def conv_kernel(code_ref, line_ref, v_ref, w_ref, conv_ref, t_scr):
    t_scr[0] = band(w_ref, 0)
    t_scr[1] = band(w_ref, 1)
    left_lane = lax.broadcasted_iota(jnp.int32, (BLOCK, BLOCK), 1) < HEAD_DIM

    def convolve(i, carry):
        mask = band_mask(code_ref, line_ref, i)
        window = v_ref[rows_of(i, BLOCK), :], v_ref[rows_of(i + 1, BLOCK), :]
        window = jnp.concatenate(window, axis=0)
        zero = jnp.zeros((BLOCK, 2 * BLOCK), BF)
        one = nn(jnp.where(mask, t_scr[0], zero), window)
        two = nn(jnp.where(mask, t_scr[1], zero), window)
        conv_ref[rows_of(i, BLOCK), :] = jnp.where(left_lane, one, two)
        return carry

    lax.fori_loop(0, conv_ref.shape[0] // BLOCK, convolve, 0, unroll=True)


def first_kernel(code_ref, q_ref, lk_ref, p_ref):
    lk2 = pair_block(lk_ref)

    def weigh(i, carry):
        r = rows_of(i, CHUNK)
        bias = doc_bias(code_ref[r, :])
        s = nn(q_ref[r, :], lk2)
        for side in (0, 1):
            cols = slice(side * SEGS, (side + 1) * SEGS)
            part = s[:, cols] + bias
            e = jnp.exp(part - jnp.max(part, axis=1, keepdims=True))
            p_ref[r, cols] = (e * (1.0 / jnp.sum(e, axis=1, keepdims=True))).astype(BF)
        return carry

    lax.fori_loop(0, q_ref.shape[0] // CHUNK, weigh, 0, unroll=True)


def heads_kernel(code_ref, p_ref, mix_ref, conv_ref, out_ref):
    mix2 = pair_block(mix_ref)

    def body(i, carry):
        r = rows_of(i, CHUNK)
        total = nt(p_ref[r, :], mix2) + conv_ref[r, :]
        out_ref[r, :] = jnp.where(code_ref[r, :] >= 0, total, 0.0).astype(BF)
        return carry

    lax.fori_loop(0, p_ref.shape[0] // CHUNK, body, 0, unroll=True)


def mixed_grad_kernel(hg_ref, p_ref, mg_ref):
    put_pair(mg_ref, tn(hg_ref[...], p_ref[...]))


def first_back_kernel(hg_ref, p_ref, q_ref, mix_ref, lk_ref, dq_ref, lkg_ref, acc):
    mix2 = pair_block(mix_ref)
    lk2 = pair_block(lk_ref)
    acc[...] = jnp.zeros_like(acc)

    def body(i, carry):
        r = rows_of(i, CHUNK)
        g = nn(hg_ref[r, :], mix2)
        parts = []
        for side in (0, 1):
            cols = slice(side * SEGS, (side + 1) * SEGS)
            p = p_ref[r, cols].astype(F32)
            gp = g[:, cols] * p
            parts.append((gp - p * jnp.sum(gp, axis=1, keepdims=True)).astype(BF))
        ds = jnp.concatenate(parts, axis=1)
        dq_ref[r, :] = nt(ds, lk2).astype(BF)
        acc[...] += tn(q_ref[r, :], ds)
        return carry

    lax.fori_loop(0, p_ref.shape[0] // CHUNK, body, 0, unroll=True)
    put_pair(lkg_ref, acc[...])


def conv_back_kernel(
    code_ref, line_ref, hg_ref, edge_ref, v_ref, w_ref, part_ref, dv_ref, tap_ref, t_scr, acc, hgx
):
    rows = hg_ref.shape[0]
    hgx[:HALF, :] = edge_ref[:HALF, :]
    hgx[HALF : HALF + rows, :] = hg_ref[...]
    hgx[HALF + rows : 2 * HALF + rows, :] = edge_ref[HALF:, :]
    hgx[2 * HALF + rows :, :] = jnp.zeros((BLOCK - 2 * HALF, BLOCK), BF)
    t_scr[0] = band(w_ref, 0)
    t_scr[1] = band(w_ref, 1)
    acc[...] = jnp.zeros_like(acc)
    left_lane = lax.broadcasted_iota(jnp.int32, (BLOCK, BLOCK), 1) < HEAD_DIM

    def body(i, carry):
        mask = band_mask(code_ref, line_ref, i)
        grads = hgx[rows_of(i, BLOCK), :], hgx[rows_of(i + 1, BLOCK), :]
        grads = jnp.concatenate(grads, axis=0)
        vals = v_ref[rows_of(i, BLOCK), :], v_ref[rows_of(i + 1, BLOCK), :]
        vals = jnp.concatenate(vals, axis=0)
        zero = jnp.zeros((BLOCK, 2 * BLOCK), BF)
        one = nn(jnp.where(mask, t_scr[0], zero), grads)
        two = nn(jnp.where(mask, t_scr[1], zero), grads)
        r = rows_of(i, BLOCK)
        dv_ref[r, :] = (part_ref[r, :] + jnp.where(left_lane, one, two)).astype(BF)
        here = hg_ref[r, :]
        none = jnp.zeros_like(here)
        acc[0] += jnp.where(mask, nt(jnp.where(left_lane, here, none), vals), 0.0)
        acc[1] += jnp.where(mask, nt(jnp.where(left_lane, none, here), vals), 0.0)
        return carry

    lax.fori_loop(0, rows // BLOCK, body, 0, unroll=True)
    for side in (0, 1):
        tap_ref[side, 0:1, :] = jnp.sum(skew(acc[side], True), axis=0, keepdims=True)


def third_back_kernel(
    k_ref, v_ref, e_ref, f_ref, d_ref, cg_ref, lq_ref, dk_ref, dv_ref, lqg_ref, acc
):
    cg2 = pair_block(cg_ref)
    lq2 = pair_block(lq_ref)
    factor = jnp.concatenate([f_ref[0], f_ref[1]], axis=1)
    delta = jnp.concatenate([d_ref[0], d_ref[1]], axis=1)
    acc[...] = jnp.zeros_like(acc)

    def body(i, carry):
        r = rows_of(i, CHUNK)
        h = nn(v_ref[rows_of(i, CHUNK, HALF), :], cg2)
        p = e_ref[r, :].astype(F32) * factor
        ds = (p * (h - delta)).astype(BF)
        dk_ref[r, :] = nt(ds, lq2).astype(BF)
        dv_ref[r, :] = nt(p.astype(BF), cg2)
        acc[...] += tn(k_ref[r, :], ds)
        return carry

    lax.fori_loop(0, e_ref.shape[0] // CHUNK, body, 0, unroll=True)
    put_pair(lqg_ref, acc[...])


def feed_kernel(x_ref, wi_ref, wo_ref, act_ref, slope_ref, out_ref):
    @pl.when(pl.program_id(0) == 0)
    def _():
        out_ref[...] = jnp.zeros_like(out_ref)

    def body(i, carry):
        r = rows_of(i, CHUNK)
        pre = nn(x_ref[r, :], wi_ref[...])
        cdf = 0.5 * (1.0 + lax.erf(pre * (0.5**0.5)))
        pdf = jnp.exp(-0.5 * pre * pre) * 0.3989422804014327
        act = (pre * cdf).astype(BF)
        act_ref[r, :] = act
        slope_ref[r, :] = (cdf + pre * pdf).astype(BF)
        out_ref[r, :] += nn(act, wo_ref[...])
        return carry

    lax.fori_loop(0, x_ref.shape[0] // CHUNK, body, 0, unroll=True)


def feed_back_kernel(
    table, og_ref, x_ref, wi_ref, wo_ref, act_ref, slope_ref, prev_ref, gi_ref, go_ref, fg_ref, pg
):
    @pl.when(pl.program_id(0) == 0)
    def _():
        fg_ref[...] = prev_ref[...]

    def body(i, carry):
        r = rows_of(i, CHUNK)
        grad = nt(og_ref[r, :], wo_ref[...])
        low = (slope_ref[r, :].astype(F32) * grad).astype(BF)
        pg[r, :] = low
        fg_ref[r, :] += nt(low, wi_ref[...])
        return carry

    lax.fori_loop(0, og_ref.shape[0] // CHUNK, body, 0, unroll=True)
    gi_ref[0] = tn(x_ref[...], pg[...]).astype(BF)
    go_ref[0] = tn(act_ref[...], og_ref[...]).astype(BF)


def split_low(a):
    high = a.astype(BF)
    return high, (a - high.astype(F32)).astype(BF)


def spread_docs(a):
    tall = jnp.concatenate([a] * DOCS, axis=0)
    row = lax.broadcasted_iota(jnp.int32, tall.shape, 0) // LAND
    lane = lax.broadcasted_iota(jnp.int32, tall.shape, 1) // LAND
    return jnp.where(row == lane, tall, jnp.zeros_like(tall))


def fold_docs(a):
    lane = lax.broadcasted_iota(jnp.int32, (LAND, SEGS), 1) // LAND
    out = a[:LAND]
    for doc in range(1, DOCS):
        out = jnp.where(lane == doc, a[doc * LAND : (doc + 1) * LAND], out)
    return out


def blocks_of(a):
    high, low = split_low(a)
    return spread_docs(high), spread_docs(low)


def times(a, blocks, form=nn):
    high, low = split_low(a)
    both = form(jnp.concatenate([high, low], axis=0), blocks[0])
    return both[:LAND] + (both[LAND:] + form(high, blocks[1]))


def cross(a, b):
    ah, al = split_low(a)
    bh, bl = split_low(b)
    return tn(ah, bh) + (tn(ah, bl) + tn(al, bh))


def doc_sum(a):
    line = jnp.sum(a, axis=0, keepdims=True)
    lane = lax.broadcasted_iota(jnp.int32, line.shape, 1) // LAND
    out = jnp.zeros_like(line)
    for doc in range(DOCS):
        part = jnp.sum(jnp.where(lane == doc, line, 0.0), axis=1, keepdims=True)
        out = jnp.where(lane == doc, part, out)
    return out


def eye_docs():
    row = lax.broadcasted_iota(jnp.int32, (LAND, SEGS), 0)
    lane = lax.broadcasted_iota(jnp.int32, (LAND, SEGS), 1) % LAND
    return jnp.where(row == lane, 1.0, 0.0)


def newton_kernel(lq_ref, lk_ref, inv_ref, at_ref, save_ref):
    heads = lq_ref.shape[0]
    eye = eye_docs()
    fixed, state = [], []
    for h in range(heads):
        scores = fold_docs(tn(lk_ref[h], lq_ref[h]))
        e = jnp.exp(scores - jnp.max(scores, axis=0, keepdims=True))
        at = e / jnp.sum(e, axis=0, keepdims=True)
        at_ref[h] = at
        blocks = blocks_of(at)
        fixed.append(blocks)
        state.append(times(eye, blocks, nt) / doc_sum(at * at))
    for step in range(NEWTON):
        x = [times(w, b) for w, b in zip(state, fixed)]
        t2 = [15.0 * eye - times(a, blocks_of(7.0 * eye - a)) for a in x]
        t3 = [13.0 * eye - times(a, blocks_of(b)) for a, b in zip(x, t2)]
        for h in range(heads):
            save_ref[step, h, 0] = state[h]
            save_ref[step, h, 1] = x[h]
            save_ref[step, h, 2] = t2[h]
            save_ref[step, h, 3] = t3[h]
        state = [0.25 * times(t, blocks_of(w)) for t, w in zip(t3, state)]
    for h in range(heads):
        inv_ref[h] = state[h]


def join_packs(a, b):
    top_a, top_b = a[HEAD_DIM : HEAD_DIM + 1], b[HEAD_DIM : HEAD_DIM + 1]
    top = jnp.maximum(top_a, top_b)
    share_a = a[HEAD_DIM + 1 : HEAD_DIM + 2] * jnp.exp(top_a - top)
    share_b = b[HEAD_DIM + 1 : HEAD_DIM + 2] * jnp.exp(top_b - top)
    total = share_a + share_b
    mean = (a[:HEAD_DIM] * share_a + b[:HEAD_DIM] * share_b) / total
    return mean, top, total


def join_kernel(a_ref, b_ref, o_ref):
    for h in range(a_ref.shape[0]):
        mean, top, total = join_packs(a_ref[h], b_ref[h])
        rest = jnp.zeros((6, SEGS), F32)
        o_ref[h] = jnp.concatenate([mean, top, total, rest], axis=0)


def three_parts(a):
    one = a.astype(BF)
    left = a - one.astype(F32)
    two = left.astype(BF)
    three = (left - two.astype(F32)).astype(BF)
    rows = [one.astype(F32), two.astype(F32), three.astype(F32), jnp.zeros((13, a.shape[1]), F32)]
    return jnp.concatenate(rows, axis=0).astype(BF)


def mix_kernel(a_ref, b_ref, inv_ref, mix_ref, carried_ref):
    for h in range(a_ref.shape[0]):
        mean, top, total = join_packs(a_ref[h], b_ref[h])
        carried_ref[h] = mean
        mix_ref[h, :HEAD_DIM, :] = times(mean, blocks_of(inv_ref[h])).astype(BF)
        mix_ref[h, HEAD_DIM:, :] = three_parts(top + jnp.log(total))


def carry_back_kernel(a_ref, b_ref, carried_ref, inv_ref, mg_ref, cg_ref):
    for h in range(a_ref.shape[0]):
        mg = a_ref[h] + b_ref[h]
        mg_ref[h] = mg
        cg = times(mg, blocks_of(inv_ref[h]), nt).astype(BF)
        cg_ref[h, :HEAD_DIM, :] = cg
        delta = jnp.sum(cg.astype(F32) * carried_ref[h], axis=0, keepdims=True)
        cg_ref[h, HEAD_DIM:, :] = three_parts(delta)


def newton_back_kernel(mg_ref, carried_ref, at_ref, save_ref, lq_ref, lk_ref, dq_ref, dk_ref, acc):
    heads = mg_ref.shape[0]
    eye = eye_docs()
    at = [at_ref[h] for h in range(heads)]
    fixed = [blocks_of(a) for a in at]
    grad = [fold_docs(cross(carried_ref[h], mg_ref[h])) for h in range(heads)]
    for step in reversed(range(NEWTON)):
        w, x, t2, t3 = ([save_ref[step, h, kind] for h in range(heads)] for kind in range(4))
        t3g = [0.25 * times(g, blocks_of(a), nt) for g, a in zip(grad, w)]
        wg = [0.25 * times(a, blocks_of(g)) for a, g in zip(t3, grad)]
        t2g = [-times(a, blocks_of(g)) for a, g in zip(x, t3g)]
        xg = [-times(g, blocks_of(a)) for g, a in zip(t3g, t2)]
        t1g = [-times(a, blocks_of(g)) for a, g in zip(x, t2g)]
        xg = [
            a - times(g, blocks_of(7.0 * eye - b)) - c
            for a, g, b, c in zip(xg, t2g, x, t1g)
        ]
        grad = [a + times(g, b, nt) for a, g, b in zip(wg, xg, fixed)]
        for h in range(heads):
            part = cross(w[h], xg[h])
            acc[h] = part if step == NEWTON - 1 else acc[h] + part
    for h in range(heads):
        square = doc_sum(at[h] * at[h])
        start = times(eye, fixed[h], nt)
        start_grad = grad[h] / square - start * (2.0 * doc_sum(grad[h] * start) / (square * square))
        atg = fold_docs(acc[h]) + times(eye, blocks_of(start_grad), nt)
        sg = at[h] * (atg - jnp.sum(atg * at[h], axis=0, keepdims=True))
        blocks = blocks_of(sg)
        dq_ref[h] = nn(lk_ref[h], blocks[0]) + nn(lk_ref[h], blocks[1])
        dk_ref[h] = nt(lq_ref[h], blocks[0]) + nt(lq_ref[h], blocks[1])


def project_kernel(x_ref, one_ref, two_ref, q_ref, k_ref, v_ref):
    local = one_ref.shape[0] // 3
    rows = q_ref.shape[0]
    weights = []
    for kind in range(3):
        cut = slice(kind * local, (kind + 1) * local)
        weights.append(jnp.concatenate([one_ref[cut, :], two_ref[cut, :]], axis=0))
    size = 2 * BLOCK
    for i in range(rows // size):
        x = x_ref[HALF + i * size : HALF + (i + 1) * size, :]
        r = slice(i * size, (i + 1) * size)
        q_ref[r, :] = (nt(x, weights[0]) * QK_SCALE).astype(BF)
        k_ref[r, :] = (nt(x, weights[1]) * QK_SCALE).astype(BF)
        v_ref[HALF + i * size : HALF + (i + 1) * size, :] = nt(x, weights[2]).astype(BF)
    ends = jnp.concatenate([x_ref[:HALF, :], x_ref[HALF + rows :, :]], axis=0)
    ends = nt(ends, weights[2]).astype(BF)
    v_ref[:HALF, :] = ends[:HALF]
    v_ref[HALF + rows :, :] = ends[HALF:]


def landmark_kernel(land_ref, one_ref, two_ref, lq_ref, lk_ref):
    local = one_ref.shape[0] // 3
    high, low = split_low(land_ref[...])
    for kind, out in ((0, lq_ref), (1, lk_ref)):
        for index, part in enumerate((one_ref, two_ref)):
            weight = part[kind * local : (kind + 1) * local, :]
            mapped = ((nt(weight, high) + nt(weight, low)) * QK_SCALE).astype(BF)
            for h in range(local // HEAD_DIM):
                head = index * (local // HEAD_DIM) + h
                out[head] = mapped[h * HEAD_DIM : (h + 1) * HEAD_DIM]


def weight_grad_kernel(count, with_land, x_ref, *refs):
    keep_ref, send_ref = refs[-2:]
    lows, rest = refs[: 2 * count], refs[2 * count : -2]
    x = x_ref[...]
    for index in range(count):
        for half in (0, 1):
            total = tn(lows[2 * index + half][...], x)
            if with_land:
                land = rest[1 + 2 * index + half]
                flat = [land[h].astype(BF) for h in range(land.shape[0])]
                total = total + nn(jnp.concatenate(flat, axis=0), rest[0][...])
                total = total * QK_SCALE
            local = total.shape[0] // 2
            cut = slice(index * local, (index + 1) * local)
            keep_ref[half, cut, :] = total[:local].astype(BF)
            send_ref[half, cut, :] = total[local:].astype(BF)


def input_grad_kernel(base_ref, *refs):
    out_ref = refs[-1]
    lows, pieces = refs[:6], refs[6:10]
    local = pieces[0].shape[0] // 3
    weights = []
    for kind in range(3):
        cut = slice(kind * local, (kind + 1) * local)
        for half in (0, 1):
            parts = [pieces[2 * half][cut, :], pieces[2 * half + 1][cut, :]]
            weights.append(jnp.concatenate(parts, axis=0))
    scaled = sum(nn(lows[j][...], weights[j]) for j in range(4))
    direct = nn(lows[4][...], weights[4]) + nn(lows[5][...], weights[5])
    out_ref[...] = base_ref[...] + QK_SCALE * scaled + direct


def call(body, grid, ins, outs, scratch=(), flops=0, moved=0, limit=20):
    return pl.pallas_call(
        body,
        grid=grid,
        in_specs=[spec for spec in ins],
        out_specs=[spec for spec, _ in outs],
        out_shape=[shape for _, shape in outs],
        scratch_shapes=list(scratch),
        compiler_params=pltpu.CompilerParams(vmem_limit_bytes=limit << 20),
        cost_estimate=pl.CostEstimate(flops=flops // 50, bytes_accessed=moved // 50, transcendentals=0),
    )


def plain(body, outs, scratch=(), flops=0, moved=0, limit=20):
    return pl.pallas_call(
        body,
        out_shape=list(outs),
        scratch_shapes=list(scratch),
        compiler_params=pltpu.CompilerParams(vmem_limit_bytes=limit << 20),
        cost_estimate=pl.CostEstimate(flops=flops // 50, bytes_accessed=moved // 50, transcendentals=0),
    )


def whole(shape):
    return pl.BlockSpec(shape, lambda p: (0,) * len(shape))


def column(rows, width):
    return pl.BlockSpec((rows, width), lambda p: (0, p))


def heads_spec(rows, cols):
    return pl.BlockSpec((2, rows, cols), lambda p: (p, 0, 0))


def shape_of(shape, dtype):
    return jax.ShapeDtypeStruct(shape, dtype)


def shards(
    batch_size,
    tokens_in,
    doc_ids,
    landmark_ids,
    pad_mask,
    w_query,
    w_key,
    w_value,
    w_output,
    conv_weight,
    first_gain,
    first_bias,
    w_inner,
    w_outer,
    second_gain,
    second_bias,
    out_grad,
):
    groups = 4
    rows, width = tokens_in.shape
    local = w_query.shape[1]
    own = local // HEAD_DIM
    side = 2 * own
    side_cols = 2 * local
    pairs = side // 2
    ext = rows + BLOCK
    ff = w_inner.shape[1]
    me = lax.axis_index("head")
    bat = lax.axis_index("batch")
    core = me & 1

    def swap(value, bit, name="swap"):
        with jax.named_scope(name):
            return lax.ppermute(value, "head", [(i, i ^ bit) for i in range(groups)])

    def swap_batch(value, bit, name="swap"):
        with jax.named_scope(name):
            return lax.ppermute(value, "batch", [(i, i ^ bit) for i in range(batch_size)])

    def spread(value, name):
        two = swap(value, 2, name)
        return value, swap(value, 1, name), two, swap(two, 1, name)

    def add_low(a, b):
        return (a.astype(F32) + b.astype(F32)).astype(BF)

    def gate(*values):
        return lax.optimization_barrier(values)

    def ordered(low_bit, mine, other):
        first = jnp.where(low_bit == 0, mine, other)
        second = jnp.where(low_bit == 0, other, mine)
        return jnp.concatenate([first, second], axis=0)

    def halves(value, flag):
        half = value.shape[0] // 2
        mine = lax.dynamic_slice_in_dim(value, flag * half, half, 0)
        return mine, lax.dynamic_slice_in_dim(value, (1 - flag) * half, half, 0)

    def head_sum(value, name, far=F32):
        mine, other = halves(value, core)
        mine = mine + swap(other, 1, name)
        mine = mine.astype(far)
        mine = mine.astype(F32) + swap(mine, 2, name).astype(F32)
        return ordered(core, mine, swap(mine, 1, name))

    bits = [1 << b for b in range(batch_size.bit_length() - 1)]

    def gather_heads(value, name):
        parts = value, swap(value, 1, name), swap(value, 2, name), swap(value, 3, name)
        return [jnp.concatenate(parts[2 * half : 2 * half + 2], axis=0) for half in (0, 1)]

    def hop_sum(value, got):
        return (value.astype(F32) + got.astype(F32)).astype(BF)

    code_row = jnp.where(pad_mask > 0, doc_ids, -1)
    outside = jnp.full((BLOCK - HALF,), -2, jnp.int32)
    code_pad = jnp.concatenate([outside[:HALF], code_row, outside])
    line = lax.dynamic_slice_in_dim(code_pad, me * rows, ext, 0)
    code = line[HALF : HALF + rows].reshape(rows, 1)
    line = line.reshape(1, ext)
    segment_row = jnp.where(pad_mask > 0, doc_ids * LAND + landmark_ids, -1)
    columns = jnp.arange(SEGS, dtype=jnp.int32)
    counts = jnp.sum((segment_row[:, None] == columns[None, :]).astype(F32), axis=0)
    segment = lax.dynamic_slice_in_dim(segment_row, me * rows, rows, 0)
    member = (segment[:, None] == columns[None, :]).astype(BF)

    packed = jnp.concatenate([w_query.T, w_key.T, w_value.T], axis=0)
    got = spread(packed, "weights")
    tap_pad = jnp.pad(conv_weight, ((0, 16 - own), (0, width - KW)))
    out_packed, far_weights = gate(
        jnp.concatenate([w_output, tap_pad], axis=0), got[2]
    )
    got = got[:2] + (far_weights,) + got[3:]
    out_far = swap(out_packed, 2, "w_output")
    out_parts = (
        out_packed, swap(out_packed, 1, "w_output"), out_far, swap(out_far, 1, "w_output")
    )

    wo = [
        jnp.concatenate([out_parts[2 * half + j][:local] for j in (0, 1)], axis=0)
        for half in (0, 1)
    ]
    tap_rows = [
        jnp.concatenate([out_parts[2 * half + j][local : local + own, :KW] for j in (0, 1)], axis=0)
        for half in (0, 1)
    ]

    def tap_lines(value):
        value = jnp.pad(value.astype(F32), ((0, 0), (0, 2 * BLOCK - KW)))
        return value.reshape(side, 1, 2 * BLOCK)

    def with_edges(value):
        before = lax.ppermute(value[-HALF:], "head", [(i, i + 1) for i in range(groups - 1)])
        after = lax.ppermute(value[:HALF], "head", [(i + 1, i) for i in range(groups - 1)])
        rest = jnp.zeros((BLOCK - 2 * HALF, value.shape[1]), value.dtype)
        return jnp.concatenate([before, value, after, rest], axis=0)

    tokens_ext = with_edges(tokens_in)

    land_part = tn(member, tokens_in) / counts[:, None]
    land_sum = head_sum(land_part, "land", FAR_TYPE)
    land_tokens = land_sum.astype(BF)

    queries, keys, values, land_q, land_k = [], [], [], [], []
    low_shape = shape_of((rows, side_cols), BF)
    land_shape = shape_of((side, HEAD_DIM, SEGS), BF)
    for half in (0, 1):
        one, two = got[2 * half : 2 * half + 2]
        projected = plain(
            project_kernel, [low_shape, low_shape, shape_of((ext, side_cols), BF)]
        )(tokens_ext, one, two)
        for target, value in zip((queries, keys, values), projected):
            target.append(value)
    for half in (0, 1):
        one, two = got[2 * half : 2 * half + 2]
        for target, value in zip(
            (land_q, land_k), plain(landmark_kernel, [land_shape, land_shape])(land_sum, one, two)
        ):
            target.append(value)

    third_call = call(
        third_kernel,
        (pairs,),
        [whole((rows, 1)), column(rows, BLOCK), column(ext, BLOCK), heads_spec(HEAD_DIM, SEGS)],
        [
            (heads_spec(HEAD_DIM + 8, SEGS), shape_of((side, HEAD_DIM + 8, SEGS), F32)),
            (column(rows, WIDE), shape_of((rows, side * SEGS), BF)),
        ],
        [pltpu.VMEM((rows, WIDE), F32), pltpu.VMEM((BLOCK, WIDE), F32)],
        flops=4 * rows * side_cols * SEGS,
        moved=2 * rows * (side_cols * 2 + side * SEGS),
    )
    packs, third_exp = [], []
    for half in (0, 1):
        pack, e_out = third_call(code, keys[half], values[half], land_q[half])
        packs.append(pack)
        third_exp.append(e_out)

    tall = HEAD_DIM + 8
    pack_keep = jnp.concatenate([part[:own] for part in packs], axis=0)
    pack_send = jnp.concatenate([part[own:] for part in packs], axis=0)
    docs_shape = shape_of((own, HEAD_DIM, SEGS), F32)
    own_q, own_k, pack_send = gate(land_q[0][:own], land_k[0][:own], pack_send)
    pack_core = swap(pack_send, 1, "pack")
    inverse, small_t, saved = plain(
        newton_kernel,
        [docs_shape, docs_shape, shape_of((NEWTON, own, 4, HEAD_DIM, SEGS), F32)],
        flops=own * NEWTON * 4 * 6 * LAND * SEGS * SEGS,
        moved=4 * own * NEWTON * 4 * HEAD_DIM * SEGS,
    )(own_q, own_k)
    pack_core, inverse = gate(pack_core, inverse)
    joined = plain(join_kernel, [shape_of((side, tall, SEGS), F32)], moved=12 * side * tall * SEGS)(
        pack_keep, pack_core
    )[0]

    first_call = call(
        first_kernel,
        (pairs,),
        [whole((rows, 1)), column(rows, BLOCK), heads_spec(HEAD_DIM, SEGS)],
        [(column(rows, WIDE), shape_of((rows, side * SEGS), BF))],
        flops=2 * rows * side_cols * SEGS,
        moved=2 * rows * (side_cols + side * SEGS),
    )
    conv_call = call(
        conv_kernel,
        (pairs,),
        [whole((rows, 1)), whole((1, ext)), column(ext, BLOCK), heads_spec(1, 2 * BLOCK)],
        [(column(rows, BLOCK), shape_of((rows, side_cols), F32))],
        [pltpu.VMEM((2, BLOCK, 2 * BLOCK), BF)],
        flops=2 * rows * side_cols * SEGS,
        moved=2 * rows * (side_cols * 3),
    )
    heads_call = call(
        heads_kernel,
        (pairs,),
        [
            whole((rows, 1)),
            column(rows, WIDE),
            heads_spec(HEAD_DIM + 16, SEGS),
            column(rows, BLOCK),
        ],
        [(column(rows, BLOCK), shape_of((rows, side_cols), BF))],
        flops=2 * rows * side_cols * SEGS,
        moved=2 * rows * (side_cols * 3 + side * SEGS),
    )
    wait_in, far_send = gate((queries, values), joined[own:])
    pack_far = swap(far_send, 2, "pack_x")
    queries, values = wait_in
    conv_outs = [
        conv_call(code, line, values[half], tap_lines(tap_rows[half]))[0] for half in (0, 1)
    ]
    first_low = [first_call(code, queries[half], land_k[half])[0] for half in (0, 1)]
    pack_far, first_low, conv_outs = gate(pack_far, first_low, conv_outs)
    mixed_own, carried = plain(
        mix_kernel,
        [shape_of((own, HEAD_DIM + 16, SEGS), BF), docs_shape],
        flops=6 * own * LAND * SEGS * SEGS,
        moved=16 * own * tall * SEGS,
    )(joined[:own], pack_far, inverse)
    mixed = gather_heads(mixed_own, "mixed")

    def row_of(parts):
        return [
            jnp.sum(part[:, HEAD_DIM : HEAD_DIM + 3].astype(F32), axis=1, keepdims=True)
            for part in parts
        ]

    heads_out = [
        heads_call(code, first_low[half], mixed[half], conv_outs[half])[0] for half in (0, 1)
    ]
    projected = nn(heads_out[0], wo[0]) + nn(heads_out[1], wo[1])
    first_out, first_normed, first_inv = norm_forward(
        tokens_in.astype(F32) + projected, first_gain, first_bias
    )
    norm_low = first_out.astype(BF)

    block = 512 if ff % 512 == 0 else ff
    act, slope, outer_out = call(
        feed_kernel,
        (ff // block,),
        [whole((rows, width)), column(width, block), pl.BlockSpec((block, width), lambda p: (p, 0))],
        [
            (column(rows, block), shape_of((rows, ff), BF)),
            (column(rows, block), shape_of((rows, ff), BF)),
            (whole((rows, width)), shape_of((rows, width), F32)),
        ],
        flops=4 * rows * width * ff,
        moved=2 * (2 * width * ff + 2 * rows * ff + 3 * rows * width),
        limit=30,
    )(norm_low, w_inner, w_outer)
    second_out, second_normed, second_inv = norm_forward(
        first_out + outer_out, second_gain, second_bias
    )
    layer_out = second_out.astype(BF)
    second_grad, grad_second_gain, grad_second_bias = norm_backward(
        out_grad.astype(F32), second_normed, second_inv, second_gain
    )
    outer_low = second_grad.astype(BF)

    share = ff // groups
    cut = share // 2

    def feed_back(slots, previous):
        table = jnp.stack([(me ^ slot) * 2 + part for slot in slots for part in (0, 1)])
        grid_spec = pltpu.PrefetchScalarGridSpec(
            num_scalar_prefetch=1,
            grid=(2 * len(slots),),
            in_specs=[
                pl.BlockSpec((rows, width), lambda p, t: (0, 0)),
                pl.BlockSpec((rows, width), lambda p, t: (0, 0)),
                pl.BlockSpec((width, cut), lambda p, t: (0, t[p])),
                pl.BlockSpec((cut, width), lambda p, t: (t[p], 0)),
                pl.BlockSpec((rows, cut), lambda p, t: (0, t[p])),
                pl.BlockSpec((rows, cut), lambda p, t: (0, t[p])),
                pl.BlockSpec((rows, width), lambda p, t: (0, 0)),
            ],
            out_specs=[
                pl.BlockSpec((1, width, cut), lambda p, t: (p // 2, 0, p % 2)),
                pl.BlockSpec((1, cut, width), lambda p, t: (p // 2, p % 2, 0)),
                pl.BlockSpec((rows, width), lambda p, t: (0, 0)),
            ],
            scratch_shapes=[pltpu.VMEM((rows, cut), BF)],
        )
        return pl.pallas_call(
            feed_back_kernel,
            grid_spec=grid_spec,
            out_shape=[
                shape_of((len(slots), width, share), BF),
                shape_of((len(slots), share, width), BF),
                shape_of((rows, width), F32),
            ],
            compiler_params=pltpu.CompilerParams(vmem_limit_bytes=36 << 20),
            cost_estimate=pl.CostEstimate(
                flops=8 * rows * width * share * len(slots),
                bytes_accessed=2 * len(slots) * share * (4 * width + 2 * rows) + 12 * rows * width,
                transcendentals=0,
            ),
        )(table, outer_low, norm_low, w_inner, w_outer, act, slope, previous)

    gi_send, go_send, first_grad = feed_back((1, 3), second_grad)
    gi_core, go_core = swap(gi_send, 1, "inner_core"), swap(go_send, 1, "outer_core")
    gi_keep, go_keep, first_grad = feed_back((0, 2), first_grad)
    first_grad, gi_core, go_core = gate(first_grad, gi_core, go_core)
    outer_flags = [jnp.where((bat & bit) != 0, 1, 0) for bit in bits]

    def split_rows(value, flag):
        half = value.shape[1] // 2
        mine = lax.dynamic_slice_in_dim(value, flag * half, half, 1)
        return mine, lax.dynamic_slice_in_dim(value, (1 - flag) * half, half, 1)

    own_keep, other_keep = split_rows(go_keep, outer_flags[0])
    own_core, other_core = split_rows(go_core, outer_flags[0])
    first_grad, near_send, far_send = gate(
        first_grad, add_low(other_keep, other_core), add_low(gi_keep[1], gi_core[1])
    )
    outer_near = swap_batch(near_send, bits[0], "outer_y")
    inner_far = swap(far_send, 2, "inner_x")
    first_in_grad, grad_first_gain, grad_first_bias = norm_backward(
        first_grad, first_normed, first_inv, first_gain
    )
    proj_low = first_in_grad.astype(BF)

    def edge_rows(value, name):
        with jax.named_scope(name):
            down = [(i, i + 1) for i in range(groups - 1)]
            up = [(i + 1, i) for i in range(groups - 1)]
            before = lax.ppermute(value[-HALF:], "head", down)
            after = lax.ppermute(value[:HALF], "head", up)
        return jnp.concatenate([before, after], axis=0)

    heads_grad = [
        jnp.where(code >= 0, nt(proj_low, wo[half]), 0.0).astype(BF) for half in (0, 1)
    ]

    mixed_grad_call = call(
        mixed_grad_kernel,
        (pairs,),
        [column(rows, BLOCK), column(rows, WIDE)],
        [(heads_spec(HEAD_DIM, SEGS), shape_of((side, HEAD_DIM, SEGS), F32))],
        flops=2 * rows * side_cols * SEGS,
        moved=2 * rows * (side_cols + side * SEGS),
    )
    mixed_part = [mixed_grad_call(heads_grad[half], first_low[half])[0] for half in (0, 1)]

    mg_keep = jnp.concatenate([part[:own] for part in mixed_part], axis=0)
    mg_send = jnp.concatenate([part[own:] for part in mixed_part], axis=0)
    heads_grad, mg_keep, mg_send = gate(heads_grad, mg_keep, mg_send)
    mg_core = swap(mg_send, 1, "mixed_grad")

    first_back_call = call(
        first_back_kernel,
        (pairs,),
        [
            column(rows, BLOCK),
            column(rows, WIDE),
            column(rows, BLOCK),
            heads_spec(HEAD_DIM + 16, SEGS),
            heads_spec(HEAD_DIM, SEGS),
        ],
        [
            (column(rows, BLOCK), shape_of((rows, side_cols), BF)),
            (heads_spec(HEAD_DIM, SEGS), shape_of((side, HEAD_DIM, SEGS), F32)),
        ],
        [pltpu.VMEM((BLOCK, WIDE), F32)],
        flops=6 * rows * side_cols * SEGS,
        moved=2 * rows * (side_cols * 3 + side * SEGS),
    )
    conv_back_call = call(
        conv_back_kernel,
        (pairs,),
        [
            whole((rows, 1)),
            whole((1, ext)),
            column(rows, BLOCK),
            column(2 * HALF, BLOCK),
            column(ext, BLOCK),
            heads_spec(1, 2 * BLOCK),
            column(rows, BLOCK),
        ],
        [
            (column(rows, BLOCK), shape_of((rows, side_cols), BF)),
            (heads_spec(8, 2 * BLOCK), shape_of((side, 8, 2 * BLOCK), F32)),
        ],
        [
            pltpu.VMEM((2, BLOCK, 2 * BLOCK), BF),
            pltpu.VMEM((2, BLOCK, 2 * BLOCK), F32),
            pltpu.VMEM((ext, BLOCK), BF),
        ],
        flops=4 * rows * side_cols * SEGS,
        moved=2 * rows * side_cols * 5,
    )
    third_back_call = call(
        third_back_kernel,
        (pairs,),
        [
            column(rows, BLOCK),
            column(ext, BLOCK),
            column(rows, WIDE),
            heads_spec(1, SEGS),
            heads_spec(1, SEGS),
            heads_spec(HEAD_DIM + 16, SEGS),
            heads_spec(HEAD_DIM, SEGS),
        ],
        [
            (column(rows, BLOCK), shape_of((rows, side_cols), BF)),
            (column(rows, BLOCK), shape_of((rows, side_cols), F32)),
            (heads_spec(HEAD_DIM, SEGS), shape_of((side, HEAD_DIM, SEGS), F32)),
        ],
        [pltpu.VMEM((BLOCK, WIDE), F32)],
        flops=8 * rows * side_cols * SEGS,
        moved=2 * rows * (side_cols * 6 + side * SEGS),
    )
    def slot_parts(parts):
        cut_rows = parts[0].shape[0] // 2
        keep = [part[:cut_rows] for part in parts]
        send = jnp.stack([part[cut_rows:] for part in parts])
        return keep, send

    def grads_call(count, with_land, *args):
        shape = shape_of((2, count * local, width), BF)
        return plain(
            functools.partial(weight_grad_kernel, count, with_land), [shape, shape], limit=28
        )(*args)

    def spread_sum(keep, near, far):
        return (keep[0].astype(F32) + near[0].astype(F32) + far.astype(F32)).astype(BF)

    dq_parts, lkg_parts = [], []
    for half in (0, 1):
        dq, lkg = first_back_call(
            heads_grad[half], first_low[half], queries[half], mixed[half], land_k[half]
        )
        dq_parts.append(dq)
        lkg_parts.append(lkg)
        if half == 0:
            mg_core, lkg_parts, dq_parts = gate(mg_core, lkg_parts, dq_parts)
            mg_sum = mg_keep + mg_core
            heads_grad, mg_sum = gate(heads_grad, mg_sum)
            mg_far = swap(mg_sum[own:], 2, "mixed_grad_x")
            edges = edge_rows(proj_low, "grad_edges")
    heads_out, dq_parts, lkg_parts, edges = gate(heads_out, dq_parts, lkg_parts, edges)
    out_keep, out_send = grads_call(1, False, proj_low, *heads_out)
    out_core = swap(out_send, 1, "out_core")

    mg_sum, mg_far, out_core = gate(mg_sum, mg_far, out_core)
    mixed_grad, carried_low = plain(
        carry_back_kernel, [docs_shape, shape_of((own, HEAD_DIM + 16, SEGS), BF)]
    )(mg_sum[:own], mg_far, carried, inverse)
    carried_low, mixed_grad, outer_near, inner_far = gate(
        carried_low, mixed_grad, outer_near, inner_far
    )
    carried_grad = gather_heads(carried_low, "carried_grad")
    inner = (gi_keep[0].astype(F32) + gi_core[0].astype(F32) + inner_far.astype(F32)).astype(BF)
    inner, inner_send = halves(inner, outer_flags[0])
    outer = (own_keep.astype(F32) + own_core.astype(F32) + outer_near.astype(F32)).astype(BF)
    outer, outer_send = split_rows(outer, outer_flags[1])
    mixed_grad, inner_send, outer_send = gate(mixed_grad, inner_send, outer_send)
    inner_hop = swap_batch(inner_send, bits[0], "inner_y")
    outer_hop = swap_batch(outer_send, bits[1], "outer_z")
    small_query, small_key = plain(
        newton_back_kernel, [docs_shape, docs_shape], [pltpu.VMEM((own, SEGS, SEGS), F32)]
    )(mixed_grad, carried, small_t, saved, own_q, own_k)

    small_query, small_key, carried_grad = gate(small_query, small_key, carried_grad)
    delta_all, lse_all = row_of(carried_grad), row_of(mixed)
    dk_parts, dv_parts, lqg_parts = [], [], []
    for half in (0, 1):
        factor = jnp.exp(packs[half][:, HEAD_DIM : HEAD_DIM + 1] - lse_all[half])
        third_in = third_exp[half]
        if half == 1:
            third_in, lqg_parts, inner_hop, outer_hop = gate(
                third_in, lqg_parts, inner_hop, outer_hop
            )
            inner = hop_sum(inner, inner_hop)
            outer = hop_sum(outer, outer_hop)
            third_in, inner, outer, out_send = gate(
                third_in, inner, outer, add_low(out_keep[1], out_core[1])
            )
            outer_hop = swap_batch(outer, bits[2], "outer_w")
            inner_hop = swap_batch(inner, bits[1], "inner_z")
            out_far = swap(out_send, 2, "out_x")
        dk, dv, lqg = third_back_call(
            keys[half], values[half], third_in, factor, delta_all[half], carried_grad[half],
            land_q[half],
        )
        dk_parts.append(dk)
        dv_parts.append(dv)
        lqg_parts.append(lqg)
    lqg_parts[0] = jnp.concatenate([lqg_parts[0][:own] + small_query, lqg_parts[0][own:]], axis=0)
    lkg_parts[0] = jnp.concatenate([lkg_parts[0][:own] + small_key, lkg_parts[0][own:]], axis=0)

    dk_parts, lqg_parts, lkg_parts = gate(dk_parts, lqg_parts, lkg_parts)
    pair_keep, pair_send = grads_call(
        2, True, tokens_in, *dk_parts, *dq_parts, land_tokens, *lkg_parts, *lqg_parts
    )
    def flat(parts):
        return [part.reshape(side_cols, SEGS).astype(BF) for part in parts]

    def weight_rows(half, kind):
        cut = slice(kind * local, (kind + 1) * local)
        return jnp.concatenate([got[2 * half][cut], got[2 * half + 1][cut]], axis=0)

    land_back = sum(
        tn(land, weight_rows(half, kind))
        for kind, lands in ((0, flat(lqg_parts)), (1, flat(lkg_parts)))
        for half, land in enumerate(lands)
    )
    land_mine, land_send = halves(QK_SCALE * land_back / counts[:, None], core)
    dv_parts, pair_send, land_send = gate(dv_parts, pair_send, land_send)
    pair_core = swap(pair_send, 1, "pair_core")
    land_hop = swap(land_send, 1, "land_core")
    edge_code = jnp.concatenate([line[0, :HALF], line[0, HALF + rows : 2 * HALF + rows]])
    edge_real = edge_code.reshape(2 * HALF, 1) >= 0
    edge_parts = [
        jnp.where(edge_real, nt(edges, wo[half]), 0.0).astype(BF) for half in (0, 1)
    ]
    tap_grads = []
    for half in (0, 1):
        if half == 1:
            pair_core, land_hop, tap_grads, dv_parts = gate(
                pair_core, land_hop, tap_grads, dv_parts
            )
            land_mine = (land_mine + land_hop).astype(BF)
            dv_parts, pair_far_send, land_mine = gate(
                dv_parts, add_low(pair_keep[1], pair_core[1]), land_mine
            )
            pair_far = swap(pair_far_send, 2, "pair_x")
            land_hop = swap(land_mine, 2, "land_x")
        dv_parts[half], tap_out = conv_back_call(
            code, line, heads_grad[half], edge_parts[half], values[half],
            tap_lines(tap_rows[half][:, ::-1]), dv_parts[half],
        )
        tap_grads.append(tap_out[:, 0, :KW])
    dv_parts, tap_grads, inner_hop, outer_hop, out_far, land_hop = gate(
        dv_parts, tap_grads, inner_hop, outer_hop, out_far, land_hop
    )
    inner = hop_sum(inner, inner_hop)
    outer = hop_sum(outer, outer_hop)
    out_sum = spread_sum(out_keep, out_core, out_far)
    land_mine = land_mine.astype(F32) + land_hop.astype(F32)
    dv_parts, inner, outer, out_sum, land_mine = gate(dv_parts, inner, outer, out_sum, land_mine)
    outer_hop = swap(outer[1], 2, "outer_x")
    inner_hop = swap_batch(inner, bits[2], "inner_w")
    out_hop = swap_batch(out_sum, bits[0], "out_y")
    land_hop = swap(land_mine, 1, "land_core")
    val_keep, val_send = grads_call(1, False, tokens_in, *dv_parts)
    norms = jnp.stack([grad_first_gain, grad_first_bias, grad_second_gain, grad_second_bias])

    def small_rows(first):
        lines = [
            jnp.concatenate([norms, jnp.pad(part[first : first + own], ((0, 0), (0, width - KW)))])
            for part in tap_grads
        ]
        return jnp.pad(jnp.stack(lines), ((0, 0), (0, 16 - 4 - own), (0, 0))).astype(BF)

    val_keep = jnp.concatenate([val_keep, small_rows(0)], axis=1)
    val_send = jnp.concatenate([val_send, small_rows(own)], axis=1)
    val_send, pair_far, land_hop = gate(val_send, pair_far, land_hop)
    land_back = ordered(core, land_mine, land_hop).astype(BF)
    pair_sum = spread_sum(pair_keep, pair_core, pair_far)
    pair_sum, pair_other = halves(pair_sum, outer_flags[0])
    val_send, pair_other = gate(val_send, pair_other)
    pair_hop = swap_batch(pair_other, bits[0], "pair_y")
    val_core = swap(val_send, 1, "val_core")
    val_core, dv_parts = gate(val_core, dv_parts)
    dv_parts, val_far_send = gate(dv_parts, add_low(val_keep[1], val_core[1]))
    val_far = swap(val_far_send, 2, "val_x")
    row_block = 2 * BLOCK
    rows_spec = pl.BlockSpec((row_block, side_cols), lambda p: (p, 0))
    full_spec = pl.BlockSpec((row_block, width), lambda p: (p, 0))
    input_part = call(
        input_grad_kernel,
        (rows // row_block,),
        [full_spec] + [rows_spec] * 6 + [whole((3 * local, width))] * 4,
        [(full_spec, shape_of((rows, width), F32))],
    )(first_in_grad, *dq_parts, *dk_parts, *dv_parts, *got)[0]

    input_part, outer_hop, pair_hop, val_far, out_hop = gate(
        input_part, outer_hop, pair_hop, val_far, out_hop
    )
    val_sum = spread_sum(val_keep, val_core, val_far)
    pair_sum = hop_sum(pair_sum, pair_hop)
    outer = hop_sum(outer[0], outer_hop)
    out_sum = hop_sum(out_sum, out_hop)
    val_hop = swap_batch(val_sum, bits[0], "val_y")
    pair_hop = swap_batch(pair_sum, bits[2], "pair_w")
    outer_hop = swap_batch(outer, bits[1], "outer_z2")
    out_hop = swap_batch(out_sum, bits[1], "out_z")
    input_grad = (input_part + nn(member, land_back)).astype(BF)

    input_grad, pair_hop, val_hop, outer_hop = gate(input_grad, pair_hop, val_hop, outer_hop)
    pair_sum = hop_sum(pair_sum, pair_hop)
    val_sum = hop_sum(val_sum, val_hop)
    outer = ordered(outer_flags[1], outer, outer_hop)
    for bit in bits[3:]:
        outer = hop_sum(outer, swap_batch(outer, bit, "outer_more"))
    pair_hop = swap_batch(pair_sum, bits[1], "pair_z")
    val_hop = swap_batch(val_sum, bits[2], "val_w")
    outer_hop = swap_batch(outer, bits[0], "outer_y2")
    inner_hop, out_hop, pair_sum = gate(inner_hop, out_hop, pair_sum)
    inner = hop_sum(inner, inner_hop)
    out_sum = hop_sum(out_sum, out_hop)
    for bit in bits[3:]:
        inner = hop_sum(inner, swap_batch(inner, bit, "inner_more"))
        out_sum = hop_sum(out_sum, swap_batch(out_sum, bit, "out_more"))
    inner_hop = swap_batch(inner, bits[0], "inner_y2")
    out_hop = swap_batch(out_sum, bits[2], "out_w")

    pair_hop, val_hop, inner = gate(pair_hop, val_hop, inner)
    pair_sum = hop_sum(pair_sum, pair_hop)
    val_sum = hop_sum(val_sum, val_hop)
    for bit in bits[3:]:
        pair_sum = hop_sum(pair_sum, swap_batch(pair_sum, bit, "pair_more"))
        val_sum = hop_sum(val_sum, swap_batch(val_sum, bit, "val_more"))
    pair_hop = swap_batch(pair_sum, bits[0], "pair_y2")
    val_hop = swap_batch(val_sum, bits[1], "val_z")
    outer_hop, out_hop, pair_sum = gate(outer_hop, out_hop, pair_sum)
    grad_outer = ordered(outer_flags[0], outer, outer_hop).astype(F32)
    grad_output = hop_sum(out_sum, out_hop).astype(F32)
    inner_hop, grad_outer = gate(inner_hop, grad_outer)
    grad_inner = ordered(outer_flags[0], inner, inner_hop).astype(F32)
    pair_sum = ordered(outer_flags[0], pair_sum, pair_hop)
    val_sum = hop_sum(val_sum, val_hop)
    grad_key, grad_query, grad_value = (
        part.astype(F32).T for part in (pair_sum[:local], pair_sum[local:], val_sum[:local])
    )
    small = val_sum[local:].astype(F32)
    return (
        layer_out,
        input_grad,
        grad_query,
        grad_key,
        grad_value,
        grad_output,
        small[4 : 4 + own, :KW],
        small[0],
        small[1],
        grad_inner,
        grad_outer,
        small[2],
        small[3],
    )


def solution(mesh):
    tokens = P(("batch", "head"), None)
    row = P("batch")
    cols = P(None, "head")
    lines = P("head", None)
    rep = P()
    return jax.shard_map(
        functools.partial(shards, mesh.shape["batch"]),
        mesh=mesh,
        in_specs=(
            tokens, row, row, row, cols, cols, cols, lines, lines,
            rep, rep, rep, rep, rep, rep, tokens,
        ),
        out_specs=(
            tokens, tokens, cols, cols, cols, lines, lines, rep, rep, cols, lines, rep, rep,
        ),
        check_vma=False,
    )
```

```python
import functools

import jax
import jax.numpy as jnp
from jax import lax
from jax.experimental import pallas as pl
from jax.experimental.pallas import tpu as pltpu
from jax.sharding import PartitionSpec as P

LAND = 64
KW = 33
HALF = KW // 2
HEAD_DIM = 64
NEWTON = 6
DOCS = 4
SEGS = DOCS * LAND
WIDE = 2 * SEGS
BLOCK = 128
CHUNK = 256
QK_SCALE = HEAD_DIM ** (-0.25)
FAR_TYPE = jnp.bfloat16
TAP_ROWS = 16

NEG_FILL = -1e30
NORM_EPS = 1e-05
BF = jnp.bfloat16
F32 = jnp.float32


def norm_forward(hidden, scale_vec, shift_vec):
    center = hidden - jnp.mean(hidden, axis=-1, keepdims=True)
    inv_spread = lax.rsqrt(jnp.mean(center * center, axis=-1, keepdims=True) + NORM_EPS)
    normed = center * inv_spread
    return (normed * scale_vec + shift_vec, normed, inv_spread)


def norm_backward(upstream, normed, inv_spread, scale_vec):
    scaled = upstream * scale_vec
    result_grad = inv_spread * (
        scaled
        - jnp.mean(scaled, axis=-1, keepdims=True)
        - normed * jnp.mean(scaled * normed, axis=-1, keepdims=True)
    )
    return (result_grad, jnp.sum(upstream * normed, axis=0), jnp.sum(upstream, axis=0))


def nn(a, b):
    return lax.dot_general(a, b, (((1,), (0,)), ((), ())), preferred_element_type=F32)


def nt(a, b):
    return lax.dot_general(a, b, (((1,), (1,)), ((), ())), preferred_element_type=F32)


def tn(a, b):
    return lax.dot_general(a, b, (((0,), (0,)), ((), ())), preferred_element_type=F32)


def pair_block(ref):
    zero = jnp.zeros((HEAD_DIM, SEGS), BF)
    top = jnp.concatenate([ref[0, :HEAD_DIM, :].astype(BF), zero], axis=1)
    low = jnp.concatenate([zero, ref[1, :HEAD_DIM, :].astype(BF)], axis=1)
    return jnp.concatenate([top, low], axis=0)


def put_pair(ref, value):
    ref[0] = value[:HEAD_DIM, :SEGS].astype(ref.dtype)
    ref[1] = value[HEAD_DIM:, SEGS:].astype(ref.dtype)


def doc_bias(code):
    lane_doc = lax.broadcasted_iota(jnp.int32, (code.shape[0], SEGS), 1) // LAND
    return jnp.where(code == lane_doc, 0.0, NEG_FILL)


def rows_of(i, size, base=0):
    return pl.ds(pl.multiple_of(base + i * size, 16), size)


def third_kernel(code_ref, k_ref, v_ref, lq_ref, c_ref, e_ref, s_scr, acc):
    steps = k_ref.shape[0] // CHUNK
    lq2 = pair_block(lq_ref)

    def scores(i, top):
        r = rows_of(i, CHUNK)
        bias = doc_bias(code_ref[r, :])
        s = nn(k_ref[r, :], lq2) + jnp.concatenate([bias, bias], axis=1)
        s_scr[r, :] = s
        return jnp.maximum(top, jnp.max(s, axis=0, keepdims=True))

    top = lax.fori_loop(0, steps, scores, jnp.full((1, WIDE), 3.0 * NEG_FILL, F32), unroll=True)
    acc[...] = jnp.zeros_like(acc)

    def weigh(i, total):
        r = rows_of(i, CHUNK)
        e = jnp.exp(s_scr[r, :] - top)
        low = e.astype(BF)
        e_ref[r, :] = low
        acc[...] += tn(v_ref[rows_of(i, CHUNK, HALF), :], low)
        return total + jnp.sum(e, axis=0, keepdims=True)

    total = lax.fori_loop(0, steps, weigh, jnp.zeros((1, WIDE), F32), unroll=True)
    mean = acc[...] / total
    for side in (0, 1):
        cols = slice(side * SEGS, (side + 1) * SEGS)
        c_ref[side, :HEAD_DIM, :] = mean[side * HEAD_DIM : (side + 1) * HEAD_DIM, cols]
        low = [top[:, cols], total[:, cols], jnp.zeros((6, SEGS), F32)]
        c_ref[side, HEAD_DIM:, :] = jnp.concatenate(low, axis=0)


def skew(x, left):
    row = lax.broadcasted_iota(jnp.int32, x.shape, 0)
    lanes = x.shape[1]
    for bit in range(x.shape[0].bit_length() - 1):
        step = 1 << bit
        moved = pltpu.roll(x, lanes - step if left else step, 1)
        x = jnp.where((row & step) != 0, moved, x)
    return x


def band(w_ref, index):
    return skew(jnp.broadcast_to(w_ref[index], (BLOCK, 2 * BLOCK)), False).astype(BF)


def band_mask(code_ref, line_ref, i):
    line = line_ref[:, pl.ds(pl.multiple_of(i * BLOCK, BLOCK), 2 * BLOCK)]
    return code_ref[rows_of(i, BLOCK), :] == line


def conv_kernel(code_ref, line_ref, v_ref, w_ref, conv_ref, t_scr):
    t_scr[0] = band(w_ref, 0)
    t_scr[1] = band(w_ref, 1)
    left_lane = lax.broadcasted_iota(jnp.int32, (BLOCK, BLOCK), 1) < HEAD_DIM

    def convolve(i, carry):
        mask = band_mask(code_ref, line_ref, i)
        window = v_ref[rows_of(i, BLOCK), :], v_ref[rows_of(i + 1, BLOCK), :]
        window = jnp.concatenate(window, axis=0)
        zero = jnp.zeros((BLOCK, 2 * BLOCK), BF)
        one = nn(jnp.where(mask, t_scr[0], zero), window)
        two = nn(jnp.where(mask, t_scr[1], zero), window)
        conv_ref[rows_of(i, BLOCK), :] = jnp.where(left_lane, one, two)
        return carry

    lax.fori_loop(0, conv_ref.shape[0] // BLOCK, convolve, 0, unroll=True)


def first_kernel(code_ref, q_ref, lk_ref, p_ref):
    lk2 = pair_block(lk_ref)

    def weigh(i, carry):
        r = rows_of(i, CHUNK)
        bias = doc_bias(code_ref[r, :])
        s = nn(q_ref[r, :], lk2)
        for side in (0, 1):
            cols = slice(side * SEGS, (side + 1) * SEGS)
            part = s[:, cols] + bias
            e = jnp.exp(part - jnp.max(part, axis=1, keepdims=True))
            p_ref[r, cols] = (e * (1.0 / jnp.sum(e, axis=1, keepdims=True))).astype(BF)
        return carry

    lax.fori_loop(0, q_ref.shape[0] // CHUNK, weigh, 0, unroll=True)


def heads_kernel(code_ref, p_ref, mix_ref, conv_ref, out_ref):
    mix2 = pair_block(mix_ref)

    def body(i, carry):
        r = rows_of(i, CHUNK)
        total = nt(p_ref[r, :], mix2) + conv_ref[r, :]
        out_ref[r, :] = jnp.where(code_ref[r, :] >= 0, total, 0.0).astype(BF)
        return carry

    lax.fori_loop(0, p_ref.shape[0] // CHUNK, body, 0, unroll=True)


def mixed_grad_kernel(hg_ref, p_ref, mg_ref):
    put_pair(mg_ref, tn(hg_ref[...], p_ref[...]))


def first_back_kernel(hg_ref, p_ref, q_ref, mix_ref, lk_ref, dq_ref, lkg_ref, acc):
    mix2 = pair_block(mix_ref)
    lk2 = pair_block(lk_ref)
    acc[...] = jnp.zeros_like(acc)

    def body(i, carry):
        r = rows_of(i, CHUNK)
        g = nn(hg_ref[r, :], mix2)
        parts = []
        for side in (0, 1):
            cols = slice(side * SEGS, (side + 1) * SEGS)
            p = p_ref[r, cols].astype(F32)
            gp = g[:, cols] * p
            parts.append((gp - p * jnp.sum(gp, axis=1, keepdims=True)).astype(BF))
        ds = jnp.concatenate(parts, axis=1)
        dq_ref[r, :] = nt(ds, lk2).astype(BF)
        acc[...] += tn(q_ref[r, :], ds)
        return carry

    lax.fori_loop(0, p_ref.shape[0] // CHUNK, body, 0, unroll=True)
    put_pair(lkg_ref, acc[...])


def conv_back_kernel(
    code_ref, line_ref, hg_ref, edge_ref, v_ref, w_ref, part_ref, dv_ref, tap_ref, t_scr, acc, hgx
):
    rows = hg_ref.shape[0]
    hgx[:HALF, :] = edge_ref[:HALF, :]
    hgx[HALF : HALF + rows, :] = hg_ref[...]
    hgx[HALF + rows : 2 * HALF + rows, :] = edge_ref[HALF:, :]
    hgx[2 * HALF + rows :, :] = jnp.zeros((BLOCK - 2 * HALF, BLOCK), BF)
    t_scr[0] = band(w_ref, 0)
    t_scr[1] = band(w_ref, 1)
    acc[...] = jnp.zeros_like(acc)
    left_lane = lax.broadcasted_iota(jnp.int32, (BLOCK, BLOCK), 1) < HEAD_DIM

    def body(i, carry):
        mask = band_mask(code_ref, line_ref, i)
        grads = hgx[rows_of(i, BLOCK), :], hgx[rows_of(i + 1, BLOCK), :]
        grads = jnp.concatenate(grads, axis=0)
        vals = v_ref[rows_of(i, BLOCK), :], v_ref[rows_of(i + 1, BLOCK), :]
        vals = jnp.concatenate(vals, axis=0)
        zero = jnp.zeros((BLOCK, 2 * BLOCK), BF)
        one = nn(jnp.where(mask, t_scr[0], zero), grads)
        two = nn(jnp.where(mask, t_scr[1], zero), grads)
        r = rows_of(i, BLOCK)
        dv_ref[r, :] = (part_ref[r, :] + jnp.where(left_lane, one, two)).astype(BF)
        here = hg_ref[r, :]
        none = jnp.zeros_like(here)
        acc[0] += jnp.where(mask, nt(jnp.where(left_lane, here, none), vals), 0.0)
        acc[1] += jnp.where(mask, nt(jnp.where(left_lane, none, here), vals), 0.0)
        return carry

    lax.fori_loop(0, rows // BLOCK, body, 0, unroll=True)
    for side in (0, 1):
        tap_ref[side, 0:1, :] = jnp.sum(skew(acc[side], True), axis=0, keepdims=True)


def third_back_kernel(
    k_ref, v_ref, e_ref, f_ref, d_ref, cg_ref, lq_ref, dk_ref, dv_ref, lqg_ref, acc
):
    cg2 = pair_block(cg_ref)
    lq2 = pair_block(lq_ref)
    factor = jnp.concatenate([f_ref[0], f_ref[1]], axis=1)
    delta = jnp.concatenate([d_ref[0], d_ref[1]], axis=1)
    acc[...] = jnp.zeros_like(acc)

    def body(i, carry):
        r = rows_of(i, CHUNK)
        h = nn(v_ref[rows_of(i, CHUNK, HALF), :], cg2)
        p = e_ref[r, :].astype(F32) * factor
        ds = (p * (h - delta)).astype(BF)
        dk_ref[r, :] = nt(ds, lq2).astype(BF)
        dv_ref[r, :] = nt(p.astype(BF), cg2)
        acc[...] += tn(k_ref[r, :], ds)
        return carry

    lax.fori_loop(0, e_ref.shape[0] // CHUNK, body, 0, unroll=True)
    put_pair(lqg_ref, acc[...])


def feed_kernel(x_ref, wi_ref, wo_ref, act_ref, slope_ref, out_ref):
    @pl.when(pl.program_id(0) == 0)
    def _():
        out_ref[...] = jnp.zeros_like(out_ref)

    def body(i, carry):
        r = rows_of(i, CHUNK)
        pre = nn(x_ref[r, :], wi_ref[...])
        cdf = 0.5 * (1.0 + lax.erf(pre * (0.5**0.5)))
        pdf = jnp.exp(-0.5 * pre * pre) * 0.3989422804014327
        act = (pre * cdf).astype(BF)
        act_ref[r, :] = act
        slope_ref[r, :] = (cdf + pre * pdf).astype(BF)
        out_ref[r, :] += nn(act, wo_ref[...])
        return carry

    lax.fori_loop(0, x_ref.shape[0] // CHUNK, body, 0, unroll=True)


def feed_back_kernel(
    table, og_ref, x_ref, wi_ref, wo_ref, act_ref, slope_ref, prev_ref, gi_ref, go_ref, fg_ref, pg
):
    @pl.when(pl.program_id(0) == 0)
    def _():
        fg_ref[...] = prev_ref[...]

    def body(i, carry):
        r = rows_of(i, CHUNK)
        grad = nt(og_ref[r, :], wo_ref[...])
        low = (slope_ref[r, :].astype(F32) * grad).astype(BF)
        pg[r, :] = low
        fg_ref[r, :] += nt(low, wi_ref[...])
        return carry

    lax.fori_loop(0, og_ref.shape[0] // CHUNK, body, 0, unroll=True)
    gi_ref[0] = tn(x_ref[...], pg[...]).astype(BF)
    go_ref[0] = tn(act_ref[...], og_ref[...]).astype(BF)


def split_low(a):
    high = a.astype(BF)
    return high, (a - high.astype(F32)).astype(BF)


def spread_docs(a):
    tall = jnp.concatenate([a] * DOCS, axis=0)
    row = lax.broadcasted_iota(jnp.int32, tall.shape, 0) // LAND
    lane = lax.broadcasted_iota(jnp.int32, tall.shape, 1) // LAND
    return jnp.where(row == lane, tall, jnp.zeros_like(tall))


def fold_docs(a):
    lane = lax.broadcasted_iota(jnp.int32, (LAND, SEGS), 1) // LAND
    out = a[:LAND]
    for doc in range(1, DOCS):
        out = jnp.where(lane == doc, a[doc * LAND : (doc + 1) * LAND], out)
    return out


def blocks_of(a):
    high, low = split_low(a)
    return spread_docs(high), spread_docs(low)


def times(a, blocks, form=nn):
    high, low = split_low(a)
    both = form(jnp.concatenate([high, low], axis=0), blocks[0])
    return both[:LAND] + (both[LAND:] + form(high, blocks[1]))


def cross(a, b):
    ah, al = split_low(a)
    bh, bl = split_low(b)
    return tn(ah, bh) + (tn(ah, bl) + tn(al, bh))


def doc_sum(a):
    line = jnp.sum(a, axis=0, keepdims=True)
    lane = lax.broadcasted_iota(jnp.int32, line.shape, 1) // LAND
    out = jnp.zeros_like(line)
    for doc in range(DOCS):
        part = jnp.sum(jnp.where(lane == doc, line, 0.0), axis=1, keepdims=True)
        out = jnp.where(lane == doc, part, out)
    return out


def eye_docs():
    row = lax.broadcasted_iota(jnp.int32, (LAND, SEGS), 0)
    lane = lax.broadcasted_iota(jnp.int32, (LAND, SEGS), 1) % LAND
    return jnp.where(row == lane, 1.0, 0.0)


def newton_kernel(lq_ref, lk_ref, inv_ref, at_ref, save_ref):
    heads = lq_ref.shape[0]
    eye = eye_docs()
    fixed, state = [], []
    for h in range(heads):
        scores = fold_docs(tn(lk_ref[h], lq_ref[h]))
        e = jnp.exp(scores - jnp.max(scores, axis=0, keepdims=True))
        at = e / jnp.sum(e, axis=0, keepdims=True)
        at_ref[h] = at
        blocks = blocks_of(at)
        fixed.append(blocks)
        state.append(times(eye, blocks, nt) / doc_sum(at * at))
    for step in range(NEWTON):
        x = [times(w, b) for w, b in zip(state, fixed)]
        t2 = [15.0 * eye - times(a, blocks_of(7.0 * eye - a)) for a in x]
        t3 = [13.0 * eye - times(a, blocks_of(b)) for a, b in zip(x, t2)]
        for h in range(heads):
            save_ref[step, h, 0] = state[h]
            save_ref[step, h, 1] = x[h]
            save_ref[step, h, 2] = t2[h]
            save_ref[step, h, 3] = t3[h]
        state = [0.25 * times(t, blocks_of(w)) for t, w in zip(t3, state)]
    for h in range(heads):
        inv_ref[h] = state[h]


def join_packs(a, b):
    top_a, top_b = a[HEAD_DIM : HEAD_DIM + 1], b[HEAD_DIM : HEAD_DIM + 1]
    top = jnp.maximum(top_a, top_b)
    share_a = a[HEAD_DIM + 1 : HEAD_DIM + 2] * jnp.exp(top_a - top)
    share_b = b[HEAD_DIM + 1 : HEAD_DIM + 2] * jnp.exp(top_b - top)
    total = share_a + share_b
    mean = (a[:HEAD_DIM] * share_a + b[:HEAD_DIM] * share_b) / total
    return mean, top, total


def join_kernel(a_ref, b_ref, o_ref):
    for h in range(a_ref.shape[0]):
        mean, top, total = join_packs(a_ref[h], b_ref[h])
        rest = jnp.zeros((6, SEGS), F32)
        o_ref[h] = jnp.concatenate([mean, top, total, rest], axis=0)


def three_parts(a):
    one = a.astype(BF)
    left = a - one.astype(F32)
    two = left.astype(BF)
    three = (left - two.astype(F32)).astype(BF)
    rows = [one.astype(F32), two.astype(F32), three.astype(F32), jnp.zeros((13, a.shape[1]), F32)]
    return jnp.concatenate(rows, axis=0).astype(BF)


def mix_kernel(a_ref, b_ref, inv_ref, mix_ref, carried_ref):
    for h in range(a_ref.shape[0]):
        mean, top, total = join_packs(a_ref[h], b_ref[h])
        carried_ref[h] = mean
        mix_ref[h, :HEAD_DIM, :] = times(mean, blocks_of(inv_ref[h])).astype(BF)
        mix_ref[h, HEAD_DIM:, :] = three_parts(top + jnp.log(total))


def carry_back_kernel(a_ref, b_ref, carried_ref, inv_ref, mg_ref, cg_ref):
    for h in range(a_ref.shape[0]):
        mg = a_ref[h] + b_ref[h]
        mg_ref[h] = mg
        cg = times(mg, blocks_of(inv_ref[h]), nt).astype(BF)
        cg_ref[h, :HEAD_DIM, :] = cg
        delta = jnp.sum(cg.astype(F32) * carried_ref[h], axis=0, keepdims=True)
        cg_ref[h, HEAD_DIM:, :] = three_parts(delta)


def newton_back_kernel(mg_ref, carried_ref, at_ref, save_ref, lq_ref, lk_ref, dq_ref, dk_ref, acc):
    heads = mg_ref.shape[0]
    eye = eye_docs()
    at = [at_ref[h] for h in range(heads)]
    fixed = [blocks_of(a) for a in at]
    grad = [fold_docs(cross(carried_ref[h], mg_ref[h])) for h in range(heads)]
    for step in reversed(range(NEWTON)):
        w, x, t2, t3 = ([save_ref[step, h, kind] for h in range(heads)] for kind in range(4))
        t3g = [0.25 * times(g, blocks_of(a), nt) for g, a in zip(grad, w)]
        wg = [0.25 * times(a, blocks_of(g)) for a, g in zip(t3, grad)]
        t2g = [-times(a, blocks_of(g)) for a, g in zip(x, t3g)]
        xg = [-times(g, blocks_of(a)) for g, a in zip(t3g, t2)]
        t1g = [-times(a, blocks_of(g)) for a, g in zip(x, t2g)]
        xg = [
            a - times(g, blocks_of(7.0 * eye - b)) - c
            for a, g, b, c in zip(xg, t2g, x, t1g)
        ]
        grad = [a + times(g, b, nt) for a, g, b in zip(wg, xg, fixed)]
        for h in range(heads):
            part = cross(w[h], xg[h])
            acc[h] = part if step == NEWTON - 1 else acc[h] + part
    for h in range(heads):
        square = doc_sum(at[h] * at[h])
        start = times(eye, fixed[h], nt)
        start_grad = grad[h] / square - start * (2.0 * doc_sum(grad[h] * start) / (square * square))
        atg = fold_docs(acc[h]) + times(eye, blocks_of(start_grad), nt)
        sg = at[h] * (atg - jnp.sum(atg * at[h], axis=0, keepdims=True))
        blocks = blocks_of(sg)
        dq_ref[h] = nn(lk_ref[h], blocks[0]) + nn(lk_ref[h], blocks[1])
        dk_ref[h] = nt(lq_ref[h], blocks[0]) + nt(lq_ref[h], blocks[1])


def project_kernel(x_ref, one_ref, two_ref, q_ref, k_ref, v_ref):
    local = (one_ref.shape[0] - TAP_ROWS) // 3
    rows = q_ref.shape[0]
    weights = []
    for kind in range(3):
        cut = slice(kind * local, (kind + 1) * local)
        weights.append(jnp.concatenate([one_ref[cut, :], two_ref[cut, :]], axis=0))
    size = 2 * BLOCK
    for i in range(rows // size):
        x = x_ref[HALF + i * size : HALF + (i + 1) * size, :]
        r = slice(i * size, (i + 1) * size)
        q_ref[r, :] = (nt(x, weights[0]) * QK_SCALE).astype(BF)
        k_ref[r, :] = (nt(x, weights[1]) * QK_SCALE).astype(BF)
        v_ref[HALF + i * size : HALF + (i + 1) * size, :] = nt(x, weights[2]).astype(BF)
    ends = jnp.concatenate([x_ref[:HALF, :], x_ref[HALF + rows :, :]], axis=0)
    ends = nt(ends, weights[2]).astype(BF)
    v_ref[:HALF, :] = ends[:HALF]
    v_ref[HALF + rows :, :] = ends[HALF:]


def landmark_kernel(land_ref, one_ref, two_ref, lq_ref, lk_ref):
    local = (one_ref.shape[0] - TAP_ROWS) // 3
    high, low = split_low(land_ref[...])
    for kind, out in ((0, lq_ref), (1, lk_ref)):
        for index, part in enumerate((one_ref, two_ref)):
            weight = part[kind * local : (kind + 1) * local, :]
            mapped = ((nt(weight, high) + nt(weight, low)) * QK_SCALE).astype(BF)
            for h in range(local // HEAD_DIM):
                head = index * (local // HEAD_DIM) + h
                out[head] = mapped[h * HEAD_DIM : (h + 1) * HEAD_DIM]


def weight_grad_kernel(count, with_land, x_ref, *refs):
    keep_ref, send_ref = refs[-2:]
    lows, rest = refs[: 2 * count], refs[2 * count : -2]
    x = x_ref[...]
    for index in range(count):
        for half in (0, 1):
            total = tn(lows[2 * index + half][...], x)
            if with_land:
                land = rest[1 + 2 * index + half]
                flat = [land[h].astype(BF) for h in range(land.shape[0])]
                total = total + nn(jnp.concatenate(flat, axis=0), rest[0][...])
                total = total * QK_SCALE
            local = total.shape[0] // 2
            cut = slice(index * local, (index + 1) * local)
            keep_ref[half, cut, :] = total[:local].astype(BF)
            send_ref[half, cut, :] = total[local:].astype(BF)


def input_grad_kernel(base_ref, *refs):
    out_ref = refs[-1]
    lows, pieces = refs[:6], refs[6:10]
    local = (pieces[0].shape[0] - TAP_ROWS) // 3
    weights = []
    for kind in range(3):
        cut = slice(kind * local, (kind + 1) * local)
        for half in (0, 1):
            parts = [pieces[2 * half][cut, :], pieces[2 * half + 1][cut, :]]
            weights.append(jnp.concatenate(parts, axis=0))
    scaled = sum(nn(lows[j][...], weights[j]) for j in range(4))
    direct = nn(lows[4][...], weights[4]) + nn(lows[5][...], weights[5])
    out_ref[...] = base_ref[...] + QK_SCALE * scaled + direct


def call(body, grid, ins, outs, scratch=(), flops=0, moved=0, limit=20):
    return pl.pallas_call(
        body,
        grid=grid,
        in_specs=[spec for spec in ins],
        out_specs=[spec for spec, _ in outs],
        out_shape=[shape for _, shape in outs],
        scratch_shapes=list(scratch),
        compiler_params=pltpu.CompilerParams(vmem_limit_bytes=limit << 20),
        cost_estimate=pl.CostEstimate(flops=flops // 50, bytes_accessed=moved // 50, transcendentals=0),
    )


def plain(body, outs, scratch=(), flops=0, moved=0, limit=20):
    return pl.pallas_call(
        body,
        out_shape=list(outs),
        scratch_shapes=list(scratch),
        compiler_params=pltpu.CompilerParams(vmem_limit_bytes=limit << 20),
        cost_estimate=pl.CostEstimate(flops=flops // 50, bytes_accessed=moved // 50, transcendentals=0),
    )


def whole(shape):
    return pl.BlockSpec(shape, lambda p: (0,) * len(shape))


def column(rows, width):
    return pl.BlockSpec((rows, width), lambda p: (0, p))


def heads_spec(rows, cols):
    return pl.BlockSpec((2, rows, cols), lambda p: (p, 0, 0))


def shape_of(shape, dtype):
    return jax.ShapeDtypeStruct(shape, dtype)


def shards(
    batch_size,
    tokens_in,
    doc_ids,
    landmark_ids,
    pad_mask,
    w_query,
    w_key,
    w_value,
    w_output,
    conv_weight,
    first_gain,
    first_bias,
    w_inner,
    w_outer,
    second_gain,
    second_bias,
    out_grad,
):
    groups = 4
    rows, width = tokens_in.shape
    local = w_query.shape[1]
    own = local // HEAD_DIM
    side = 2 * own
    side_cols = 2 * local
    pairs = side // 2
    ext = rows + BLOCK
    ff = w_inner.shape[1]
    me = lax.axis_index("head")
    bat = lax.axis_index("batch")
    core = me & 1

    def swap(value, bit, name="swap"):
        with jax.named_scope(name):
            return lax.ppermute(value, "head", [(i, i ^ bit) for i in range(groups)])

    def swap_batch(value, bit, name="swap"):
        with jax.named_scope(name):
            return lax.ppermute(value, "batch", [(i, i ^ bit) for i in range(batch_size)])

    def spread(value, name):
        two = swap(value, 2, name)
        return value, swap(value, 1, name), two, swap(two, 1, name)

    def add_low(a, b):
        return (a.astype(F32) + b.astype(F32)).astype(BF)

    def gate(*values):
        return lax.optimization_barrier(values)

    def ordered(low_bit, mine, other):
        first = jnp.where(low_bit == 0, mine, other)
        second = jnp.where(low_bit == 0, other, mine)
        return jnp.concatenate([first, second], axis=0)

    def halves(value, flag):
        half = value.shape[0] // 2
        mine = lax.dynamic_slice_in_dim(value, flag * half, half, 0)
        return mine, lax.dynamic_slice_in_dim(value, (1 - flag) * half, half, 0)

    def head_sum(value, name, far=F32):
        mine, other = halves(value, core)
        mine = mine + swap(other, 1, name)
        mine = mine.astype(far)
        mine = mine.astype(F32) + swap(mine, 2, name).astype(F32)
        return ordered(core, mine, swap(mine, 1, name))

    bits = [1 << b for b in range(batch_size.bit_length() - 1)]

    def gather_heads(value, name):
        parts = value, swap(value, 1, name), swap(value, 2, name), swap(value, 3, name)
        return [jnp.concatenate(parts[2 * half : 2 * half + 2], axis=0) for half in (0, 1)]

    def hop_sum(value, got):
        return (value.astype(F32) + got.astype(F32)).astype(BF)

    code_row = jnp.where(pad_mask > 0, doc_ids, -1)
    outside = jnp.full((BLOCK - HALF,), -2, jnp.int32)
    code_pad = jnp.concatenate([outside[:HALF], code_row, outside])
    line = lax.dynamic_slice_in_dim(code_pad, me * rows, ext, 0)
    code = line[HALF : HALF + rows].reshape(rows, 1)
    line = line.reshape(1, ext)
    segment_row = jnp.where(pad_mask > 0, doc_ids * LAND + landmark_ids, -1)
    columns = jnp.arange(SEGS, dtype=jnp.int32)
    counts = jnp.sum((segment_row[:, None] == columns[None, :]).astype(F32), axis=0)
    segment = lax.dynamic_slice_in_dim(segment_row, me * rows, rows, 0)
    member = (segment[:, None] == columns[None, :]).astype(BF)

    tap_pad = jnp.pad(conv_weight, ((0, TAP_ROWS - own), (0, width - KW)))
    packed = jnp.concatenate([w_query.T, w_key.T, w_value.T, tap_pad], axis=0)
    packed, member_in = gate(packed, member)
    got = spread(packed, "weights")
    out_packed, far_weights = gate(w_output, got[2])
    got = got[:2] + (far_weights,) + got[3:]
    out_far = swap(out_packed, 2, "w_output")
    out_parts = (
        out_packed, swap(out_packed, 1, "w_output"), out_far, swap(out_far, 1, "w_output")
    )

    wo = [
        jnp.concatenate([out_parts[2 * half + j] for j in (0, 1)], axis=0)
        for half in (0, 1)
    ]
    tap_rows = [
        jnp.concatenate(
            [got[2 * half + j][3 * local : 3 * local + own, :KW] for j in (0, 1)], axis=0
        )
        for half in (0, 1)
    ]

    def tap_lines(value):
        value = jnp.pad(value.astype(F32), ((0, 0), (0, 2 * BLOCK - KW)))
        return value.reshape(side, 1, 2 * BLOCK)

    def with_edges(value):
        before = lax.ppermute(value[-HALF:], "head", [(i, i + 1) for i in range(groups - 1)])
        after = lax.ppermute(value[:HALF], "head", [(i + 1, i) for i in range(groups - 1)])
        rest = jnp.zeros((BLOCK - 2 * HALF, value.shape[1]), value.dtype)
        return jnp.concatenate([before, value, after, rest], axis=0)

    tokens_ext = with_edges(tokens_in)

    land_part = tn(member_in, tokens_in) / counts[:, None]
    land_sum = head_sum(land_part, "land", FAR_TYPE)
    land_tokens = land_sum.astype(BF)

    queries, keys, values, land_q, land_k = [], [], [], [], []
    low_shape = shape_of((rows, side_cols), BF)
    land_shape = shape_of((side, HEAD_DIM, SEGS), BF)
    for half in (0, 1):
        one, two = got[2 * half : 2 * half + 2]
        projected = plain(
            project_kernel, [low_shape, low_shape, shape_of((ext, side_cols), BF)]
        )(tokens_ext, one, two)
        for target, value in zip((queries, keys, values), projected):
            target.append(value)
    for half in (0, 1):
        one, two = got[2 * half : 2 * half + 2]
        for target, value in zip(
            (land_q, land_k), plain(landmark_kernel, [land_shape, land_shape])(land_sum, one, two)
        ):
            target.append(value)

    third_call = call(
        third_kernel,
        (pairs,),
        [whole((rows, 1)), column(rows, BLOCK), column(ext, BLOCK), heads_spec(HEAD_DIM, SEGS)],
        [
            (heads_spec(HEAD_DIM + 8, SEGS), shape_of((side, HEAD_DIM + 8, SEGS), F32)),
            (column(rows, WIDE), shape_of((rows, side * SEGS), BF)),
        ],
        [pltpu.VMEM((rows, WIDE), F32), pltpu.VMEM((BLOCK, WIDE), F32)],
        flops=4 * rows * side_cols * SEGS,
        moved=2 * rows * (side_cols * 2 + side * SEGS),
    )
    packs, third_exp = [], []
    for half in (0, 1):
        third_land = land_q[half]
        if half == 1:
            third_land, wo, tap_rows = gate(third_land, wo, tap_rows)
        pack, e_out = third_call(code, keys[half], values[half], third_land)
        packs.append(pack)
        third_exp.append(e_out)

    tall = HEAD_DIM + 8
    pack_keep = jnp.concatenate([part[:own] for part in packs], axis=0)
    pack_send = jnp.concatenate([part[own:] for part in packs], axis=0)
    docs_shape = shape_of((own, HEAD_DIM, SEGS), F32)
    own_q, own_k, pack_send = gate(land_q[0][:own], land_k[0][:own], pack_send)
    pack_core = swap(pack_send, 1, "pack")
    inverse, small_t, saved = plain(
        newton_kernel,
        [docs_shape, docs_shape, shape_of((NEWTON, own, 4, HEAD_DIM, SEGS), F32)],
        flops=own * NEWTON * 4 * 6 * LAND * SEGS * SEGS,
        moved=4 * own * NEWTON * 4 * HEAD_DIM * SEGS,
    )(own_q, own_k)
    pack_core, inverse = gate(pack_core, inverse)
    joined = plain(join_kernel, [shape_of((side, tall, SEGS), F32)], moved=12 * side * tall * SEGS)(
        pack_keep, pack_core
    )[0]

    first_call = call(
        first_kernel,
        (pairs,),
        [whole((rows, 1)), column(rows, BLOCK), heads_spec(HEAD_DIM, SEGS)],
        [(column(rows, WIDE), shape_of((rows, side * SEGS), BF))],
        flops=2 * rows * side_cols * SEGS,
        moved=2 * rows * (side_cols + side * SEGS),
    )
    conv_call = call(
        conv_kernel,
        (pairs,),
        [whole((rows, 1)), whole((1, ext)), column(ext, BLOCK), heads_spec(1, 2 * BLOCK)],
        [(column(rows, BLOCK), shape_of((rows, side_cols), F32))],
        [pltpu.VMEM((2, BLOCK, 2 * BLOCK), BF)],
        flops=2 * rows * side_cols * SEGS,
        moved=2 * rows * (side_cols * 3),
    )
    heads_call = call(
        heads_kernel,
        (pairs,),
        [
            whole((rows, 1)),
            column(rows, WIDE),
            heads_spec(HEAD_DIM + 16, SEGS),
            column(rows, BLOCK),
        ],
        [(column(rows, BLOCK), shape_of((rows, side_cols), BF))],
        flops=2 * rows * side_cols * SEGS,
        moved=2 * rows * (side_cols * 3 + side * SEGS),
    )
    wait_in, far_send = gate((queries, values), joined[own:])
    pack_far = swap(far_send, 2, "pack_x")
    queries, values = wait_in
    first_low = [first_call(code, queries[half], land_k[half])[0] for half in (0, 1)]
    pack_far, first_low = gate(pack_far, first_low)
    mixed_own, carried = plain(
        mix_kernel,
        [shape_of((own, HEAD_DIM + 16, SEGS), BF), docs_shape],
        flops=6 * own * LAND * SEGS * SEGS,
        moved=16 * own * tall * SEGS,
    )(joined[:own], pack_far, inverse)
    values_in, mixed_own = gate(values, mixed_own)
    mixed = gather_heads(mixed_own, "mixed")
    conv_outs = [
        conv_call(code, line, values_in[half], tap_lines(tap_rows[half]))[0] for half in (0, 1)
    ]
    mixed, conv_outs = gate(mixed, conv_outs)

    def row_of(parts):
        return [
            jnp.sum(part[:, HEAD_DIM : HEAD_DIM + 3].astype(F32), axis=1, keepdims=True)
            for part in parts
        ]

    heads_out = [
        heads_call(code, first_low[half], mixed[half], conv_outs[half])[0] for half in (0, 1)
    ]
    projected = nn(heads_out[0], wo[0]) + nn(heads_out[1], wo[1])
    first_out, first_normed, first_inv = norm_forward(
        tokens_in.astype(F32) + projected, first_gain, first_bias
    )
    norm_low = first_out.astype(BF)

    block = 512 if ff % 512 == 0 else ff
    act, slope, outer_out = call(
        feed_kernel,
        (ff // block,),
        [whole((rows, width)), column(width, block), pl.BlockSpec((block, width), lambda p: (p, 0))],
        [
            (column(rows, block), shape_of((rows, ff), BF)),
            (column(rows, block), shape_of((rows, ff), BF)),
            (whole((rows, width)), shape_of((rows, width), F32)),
        ],
        flops=4 * rows * width * ff,
        moved=2 * (2 * width * ff + 2 * rows * ff + 3 * rows * width),
        limit=30,
    )(norm_low, w_inner, w_outer)
    second_out, second_normed, second_inv = norm_forward(
        first_out + outer_out, second_gain, second_bias
    )
    layer_out = second_out.astype(BF)
    second_grad, grad_second_gain, grad_second_bias = norm_backward(
        out_grad.astype(F32), second_normed, second_inv, second_gain
    )
    outer_low = second_grad.astype(BF)

    share = ff // groups
    cut = share // 2

    def feed_back(slots, previous):
        table = jnp.stack([(me ^ slot) * 2 + part for slot in slots for part in (0, 1)])
        grid_spec = pltpu.PrefetchScalarGridSpec(
            num_scalar_prefetch=1,
            grid=(2 * len(slots),),
            in_specs=[
                pl.BlockSpec((rows, width), lambda p, t: (0, 0)),
                pl.BlockSpec((rows, width), lambda p, t: (0, 0)),
                pl.BlockSpec((width, cut), lambda p, t: (0, t[p])),
                pl.BlockSpec((cut, width), lambda p, t: (t[p], 0)),
                pl.BlockSpec((rows, cut), lambda p, t: (0, t[p])),
                pl.BlockSpec((rows, cut), lambda p, t: (0, t[p])),
                pl.BlockSpec((rows, width), lambda p, t: (0, 0)),
            ],
            out_specs=[
                pl.BlockSpec((1, width, cut), lambda p, t: (p // 2, 0, p % 2)),
                pl.BlockSpec((1, cut, width), lambda p, t: (p // 2, p % 2, 0)),
                pl.BlockSpec((rows, width), lambda p, t: (0, 0)),
            ],
            scratch_shapes=[pltpu.VMEM((rows, cut), BF)],
        )
        return pl.pallas_call(
            feed_back_kernel,
            grid_spec=grid_spec,
            out_shape=[
                shape_of((len(slots), width, share), BF),
                shape_of((len(slots), share, width), BF),
                shape_of((rows, width), F32),
            ],
            compiler_params=pltpu.CompilerParams(vmem_limit_bytes=36 << 20),
            cost_estimate=pl.CostEstimate(
                flops=8 * rows * width * share * len(slots),
                bytes_accessed=2 * len(slots) * share * (4 * width + 2 * rows) + 12 * rows * width,
                transcendentals=0,
            ),
        )(table, outer_low, norm_low, w_inner, w_outer, act, slope, previous)

    gi_send, go_send, first_grad = feed_back((1, 3), second_grad)
    gi_core, go_core = swap(gi_send, 1, "inner_core"), swap(go_send, 1, "outer_core")
    gi_keep, go_keep, first_grad = feed_back((0, 2), first_grad)
    first_grad, gi_core, go_core = gate(first_grad, gi_core, go_core)
    outer_flags = [jnp.where((bat & bit) != 0, 1, 0) for bit in bits]

    def split_rows(value, flag):
        half = value.shape[1] // 2
        mine = lax.dynamic_slice_in_dim(value, flag * half, half, 1)
        return mine, lax.dynamic_slice_in_dim(value, (1 - flag) * half, half, 1)

    own_keep, other_keep = split_rows(go_keep, outer_flags[0])
    own_core, other_core = split_rows(go_core, outer_flags[0])
    first_grad, near_send, far_send = gate(
        first_grad, add_low(other_keep, other_core), add_low(gi_keep[1], gi_core[1])
    )
    outer_near = swap_batch(near_send, bits[0], "outer_y")
    inner_far = swap(far_send, 2, "inner_x")
    first_in_grad, grad_first_gain, grad_first_bias = norm_backward(
        first_grad, first_normed, first_inv, first_gain
    )
    proj_low = first_in_grad.astype(BF)

    def edge_rows(value, name):
        with jax.named_scope(name):
            down = [(i, i + 1) for i in range(groups - 1)]
            up = [(i + 1, i) for i in range(groups - 1)]
            before = lax.ppermute(value[-HALF:], "head", down)
            after = lax.ppermute(value[:HALF], "head", up)
        return jnp.concatenate([before, after], axis=0)

    heads_grad = [
        jnp.where(code >= 0, nt(proj_low, wo[half]), 0.0).astype(BF) for half in (0, 1)
    ]

    mixed_grad_call = call(
        mixed_grad_kernel,
        (pairs,),
        [column(rows, BLOCK), column(rows, WIDE)],
        [(heads_spec(HEAD_DIM, SEGS), shape_of((side, HEAD_DIM, SEGS), F32))],
        flops=2 * rows * side_cols * SEGS,
        moved=2 * rows * (side_cols + side * SEGS),
    )
    mixed_part = [mixed_grad_call(heads_grad[half], first_low[half])[0] for half in (0, 1)]

    mg_keep = jnp.concatenate([part[:own] for part in mixed_part], axis=0)
    mg_send = jnp.concatenate([part[own:] for part in mixed_part], axis=0)
    heads_grad, mg_keep, mg_send = gate(heads_grad, mg_keep, mg_send)
    mg_core = swap(mg_send, 1, "mixed_grad")

    first_back_call = call(
        first_back_kernel,
        (pairs,),
        [
            column(rows, BLOCK),
            column(rows, WIDE),
            column(rows, BLOCK),
            heads_spec(HEAD_DIM + 16, SEGS),
            heads_spec(HEAD_DIM, SEGS),
        ],
        [
            (column(rows, BLOCK), shape_of((rows, side_cols), BF)),
            (heads_spec(HEAD_DIM, SEGS), shape_of((side, HEAD_DIM, SEGS), F32)),
        ],
        [pltpu.VMEM((BLOCK, WIDE), F32)],
        flops=6 * rows * side_cols * SEGS,
        moved=2 * rows * (side_cols * 3 + side * SEGS),
    )
    conv_back_call = call(
        conv_back_kernel,
        (pairs,),
        [
            whole((rows, 1)),
            whole((1, ext)),
            column(rows, BLOCK),
            column(2 * HALF, BLOCK),
            column(ext, BLOCK),
            heads_spec(1, 2 * BLOCK),
            column(rows, BLOCK),
        ],
        [
            (column(rows, BLOCK), shape_of((rows, side_cols), BF)),
            (heads_spec(8, 2 * BLOCK), shape_of((side, 8, 2 * BLOCK), F32)),
        ],
        [
            pltpu.VMEM((2, BLOCK, 2 * BLOCK), BF),
            pltpu.VMEM((2, BLOCK, 2 * BLOCK), F32),
            pltpu.VMEM((ext, BLOCK), BF),
        ],
        flops=4 * rows * side_cols * SEGS,
        moved=2 * rows * side_cols * 5,
    )
    third_back_call = call(
        third_back_kernel,
        (pairs,),
        [
            column(rows, BLOCK),
            column(ext, BLOCK),
            column(rows, WIDE),
            heads_spec(1, SEGS),
            heads_spec(1, SEGS),
            heads_spec(HEAD_DIM + 16, SEGS),
            heads_spec(HEAD_DIM, SEGS),
        ],
        [
            (column(rows, BLOCK), shape_of((rows, side_cols), BF)),
            (column(rows, BLOCK), shape_of((rows, side_cols), F32)),
            (heads_spec(HEAD_DIM, SEGS), shape_of((side, HEAD_DIM, SEGS), F32)),
        ],
        [pltpu.VMEM((BLOCK, WIDE), F32)],
        flops=8 * rows * side_cols * SEGS,
        moved=2 * rows * (side_cols * 6 + side * SEGS),
    )
    def slot_parts(parts):
        cut_rows = parts[0].shape[0] // 2
        keep = [part[:cut_rows] for part in parts]
        send = jnp.stack([part[cut_rows:] for part in parts])
        return keep, send

    def grads_call(count, with_land, *args):
        shape = shape_of((2, count * local, width), BF)
        return plain(
            functools.partial(weight_grad_kernel, count, with_land), [shape, shape], limit=28
        )(*args)

    def spread_sum(keep, near, far):
        return (keep[0].astype(F32) + near[0].astype(F32) + far.astype(F32)).astype(BF)

    dq_parts, lkg_parts = [], []
    for half in (0, 1):
        dq, lkg = first_back_call(
            heads_grad[half], first_low[half], queries[half], mixed[half], land_k[half]
        )
        dq_parts.append(dq)
        lkg_parts.append(lkg)
        if half == 0:
            mg_core, lkg_parts, dq_parts = gate(mg_core, lkg_parts, dq_parts)
            mg_sum = mg_keep + mg_core
            heads_grad, mg_sum = gate(heads_grad, mg_sum)
            mg_far = swap(mg_sum[own:], 2, "mixed_grad_x")
            edges = edge_rows(proj_low, "grad_edges")
    heads_out, dq_parts, lkg_parts, edges = gate(heads_out, dq_parts, lkg_parts, edges)
    out_keep, out_send = grads_call(1, False, proj_low, *heads_out)
    out_core = swap(out_send, 1, "out_core")

    mg_sum, mg_far, out_core = gate(mg_sum, mg_far, out_core)
    mixed_grad, carried_low = plain(
        carry_back_kernel, [docs_shape, shape_of((own, HEAD_DIM + 16, SEGS), BF)]
    )(mg_sum[:own], mg_far, carried, inverse)
    carried_low, mixed_grad, outer_near, inner_far = gate(
        carried_low, mixed_grad, outer_near, inner_far
    )
    carried_grad = gather_heads(carried_low, "carried_grad")
    inner = (gi_keep[0].astype(F32) + gi_core[0].astype(F32) + inner_far.astype(F32)).astype(BF)
    inner, inner_send = halves(inner, outer_flags[0])
    outer = (own_keep.astype(F32) + own_core.astype(F32) + outer_near.astype(F32)).astype(BF)
    outer, outer_send = split_rows(outer, outer_flags[1])
    mixed_grad, inner_send, outer_send = gate(mixed_grad, inner_send, outer_send)
    inner_hop = swap_batch(inner_send, bits[0], "inner_y")
    outer_hop = swap_batch(outer_send, bits[1], "outer_z")
    small_query, small_key = plain(
        newton_back_kernel, [docs_shape, docs_shape], [pltpu.VMEM((own, SEGS, SEGS), F32)]
    )(mixed_grad, carried, small_t, saved, own_q, own_k)

    small_query, small_key, carried_grad = gate(small_query, small_key, carried_grad)
    delta_all, lse_all = row_of(carried_grad), row_of(mixed)
    dk_parts, dv_parts, lqg_parts = [], [], []
    for half in (0, 1):
        factor = jnp.exp(packs[half][:, HEAD_DIM : HEAD_DIM + 1] - lse_all[half])
        third_in = third_exp[half]
        if half == 1:
            third_in, lqg_parts, inner_hop, outer_hop = gate(
                third_in, lqg_parts, inner_hop, outer_hop
            )
            inner = hop_sum(inner, inner_hop)
            outer = hop_sum(outer, outer_hop)
            third_in, inner, outer, out_send = gate(
                third_in, inner, outer, add_low(out_keep[1], out_core[1])
            )
            outer_hop = swap_batch(outer, bits[2], "outer_w")
            inner_hop = swap_batch(inner, bits[1], "inner_z")
            out_far = swap(out_send, 2, "out_x")
        dk, dv, lqg = third_back_call(
            keys[half], values[half], third_in, factor, delta_all[half], carried_grad[half],
            land_q[half],
        )
        dk_parts.append(dk)
        dv_parts.append(dv)
        lqg_parts.append(lqg)
    lqg_parts[0] = jnp.concatenate([lqg_parts[0][:own] + small_query, lqg_parts[0][own:]], axis=0)
    lkg_parts[0] = jnp.concatenate([lkg_parts[0][:own] + small_key, lkg_parts[0][own:]], axis=0)

    dk_parts, lqg_parts, lkg_parts = gate(dk_parts, lqg_parts, lkg_parts)
    pair_keep, pair_send = grads_call(
        2, True, tokens_in, *dk_parts, *dq_parts, land_tokens, *lkg_parts, *lqg_parts
    )
    def flat(parts):
        return [part.reshape(side_cols, SEGS).astype(BF) for part in parts]

    def weight_rows(half, kind):
        cut = slice(kind * local, (kind + 1) * local)
        return jnp.concatenate([got[2 * half][cut], got[2 * half + 1][cut]], axis=0)

    land_back = sum(
        tn(land, weight_rows(half, kind))
        for kind, lands in ((0, flat(lqg_parts)), (1, flat(lkg_parts)))
        for half, land in enumerate(lands)
    )
    land_mine, land_send = halves(QK_SCALE * land_back / counts[:, None], core)
    dv_parts, pair_send, land_send = gate(dv_parts, pair_send, land_send)
    pair_core = swap(pair_send, 1, "pair_core")
    land_hop = swap(land_send, 1, "land_core")
    edge_code = jnp.concatenate([line[0, :HALF], line[0, HALF + rows : 2 * HALF + rows]])
    edge_real = edge_code.reshape(2 * HALF, 1) >= 0
    edge_parts = [
        jnp.where(edge_real, nt(edges, wo[half]), 0.0).astype(BF) for half in (0, 1)
    ]
    tap_grads = []
    for half in (0, 1):
        if half == 1:
            pair_core, land_hop, tap_grads, dv_parts = gate(
                pair_core, land_hop, tap_grads, dv_parts
            )
            land_mine = (land_mine + land_hop).astype(BF)
            dv_parts, pair_far_send, land_mine = gate(
                dv_parts, add_low(pair_keep[1], pair_core[1]), land_mine
            )
            pair_far = swap(pair_far_send, 2, "pair_x")
            land_hop = swap(land_mine, 2, "land_x")
        dv_parts[half], tap_out = conv_back_call(
            code, line, heads_grad[half], edge_parts[half], values[half],
            tap_lines(tap_rows[half][:, ::-1]), dv_parts[half],
        )
        tap_grads.append(tap_out[:, 0, :KW])
    dv_parts, tap_grads, inner_hop, outer_hop, out_far, land_hop = gate(
        dv_parts, tap_grads, inner_hop, outer_hop, out_far, land_hop
    )
    inner = hop_sum(inner, inner_hop)
    outer = hop_sum(outer, outer_hop)
    out_sum = spread_sum(out_keep, out_core, out_far)
    land_mine = land_mine.astype(F32) + land_hop.astype(F32)
    dv_parts, inner, outer, out_sum, land_mine = gate(dv_parts, inner, outer, out_sum, land_mine)
    outer_hop = swap(outer[1], 2, "outer_x")
    inner_hop = swap_batch(inner, bits[2], "inner_w")
    out_hop = swap_batch(out_sum, bits[0], "out_y")
    land_hop = swap(land_mine, 1, "land_core")
    val_keep, val_send = grads_call(1, False, tokens_in, *dv_parts)
    norms = jnp.stack([grad_first_gain, grad_first_bias, grad_second_gain, grad_second_bias])

    def small_rows(first):
        lines = [
            jnp.concatenate([norms, jnp.pad(part[first : first + own], ((0, 0), (0, width - KW)))])
            for part in tap_grads
        ]
        return jnp.pad(jnp.stack(lines), ((0, 0), (0, 16 - 4 - own), (0, 0))).astype(BF)

    val_keep = jnp.concatenate([val_keep, small_rows(0)], axis=1)
    val_send = jnp.concatenate([val_send, small_rows(own)], axis=1)
    val_send, pair_far, land_hop = gate(val_send, pair_far, land_hop)
    land_back = ordered(core, land_mine, land_hop).astype(BF)
    pair_sum = spread_sum(pair_keep, pair_core, pair_far)
    pair_sum, pair_other = halves(pair_sum, outer_flags[0])
    val_send, pair_other = gate(val_send, pair_other)
    pair_hop = swap_batch(pair_other, bits[0], "pair_y")
    val_core = swap(val_send, 1, "val_core")
    val_core, dv_parts = gate(val_core, dv_parts)
    dv_parts, val_far_send = gate(dv_parts, add_low(val_keep[1], val_core[1]))
    val_far = swap(val_far_send, 2, "val_x")
    row_block = 2 * BLOCK
    rows_spec = pl.BlockSpec((row_block, side_cols), lambda p: (p, 0))
    full_spec = pl.BlockSpec((row_block, width), lambda p: (p, 0))
    input_part = call(
        input_grad_kernel,
        (rows // row_block,),
        [full_spec] + [rows_spec] * 6 + [whole((3 * local + TAP_ROWS, width))] * 4,
        [(full_spec, shape_of((rows, width), F32))],
    )(first_in_grad, *dq_parts, *dk_parts, *dv_parts, *got)[0]

    input_part, outer_hop, pair_hop, val_far, out_hop = gate(
        input_part, outer_hop, pair_hop, val_far, out_hop
    )
    val_sum = spread_sum(val_keep, val_core, val_far)
    pair_sum = hop_sum(pair_sum, pair_hop)
    outer = hop_sum(outer[0], outer_hop)
    out_sum = hop_sum(out_sum, out_hop)
    val_hop = swap_batch(val_sum, bits[0], "val_y")
    pair_hop = swap_batch(pair_sum, bits[2], "pair_w")
    outer_hop = swap_batch(outer, bits[1], "outer_z2")
    out_hop = swap_batch(out_sum, bits[1], "out_z")
    input_grad = (input_part + nn(member, land_back)).astype(BF)

    input_grad, pair_hop, val_hop, outer_hop = gate(input_grad, pair_hop, val_hop, outer_hop)
    pair_sum = hop_sum(pair_sum, pair_hop)
    val_sum = hop_sum(val_sum, val_hop)
    outer = ordered(outer_flags[1], outer, outer_hop)
    for bit in bits[3:]:
        outer = hop_sum(outer, swap_batch(outer, bit, "outer_more"))
    pair_hop = swap_batch(pair_sum, bits[1], "pair_z")
    val_hop = swap_batch(val_sum, bits[2], "val_w")
    outer_hop = swap_batch(outer, bits[0], "outer_y2")
    inner_hop, out_hop, pair_sum = gate(inner_hop, out_hop, pair_sum)
    inner = hop_sum(inner, inner_hop)
    out_sum = hop_sum(out_sum, out_hop)
    for bit in bits[3:]:
        inner = hop_sum(inner, swap_batch(inner, bit, "inner_more"))
        out_sum = hop_sum(out_sum, swap_batch(out_sum, bit, "out_more"))
    inner_hop = swap_batch(inner, bits[0], "inner_y2")
    out_hop = swap_batch(out_sum, bits[2], "out_w")

    pair_hop, val_hop, inner = gate(pair_hop, val_hop, inner)
    pair_sum = hop_sum(pair_sum, pair_hop)
    val_sum = hop_sum(val_sum, val_hop)
    for bit in bits[3:]:
        pair_sum = hop_sum(pair_sum, swap_batch(pair_sum, bit, "pair_more"))
        val_sum = hop_sum(val_sum, swap_batch(val_sum, bit, "val_more"))
    pair_hop = swap_batch(pair_sum, bits[0], "pair_y2")
    val_hop = swap_batch(val_sum, bits[1], "val_z")
    outer_hop, out_hop, pair_sum = gate(outer_hop, out_hop, pair_sum)
    grad_outer = ordered(outer_flags[0], outer, outer_hop).astype(F32)
    grad_output = hop_sum(out_sum, out_hop).astype(F32)
    inner_hop, grad_outer = gate(inner_hop, grad_outer)
    grad_inner = ordered(outer_flags[0], inner, inner_hop).astype(F32)
    pair_sum = ordered(outer_flags[0], pair_sum, pair_hop)
    val_sum = hop_sum(val_sum, val_hop)
    grad_key, grad_query, grad_value = (
        part.astype(F32).T for part in (pair_sum[:local], pair_sum[local:], val_sum[:local])
    )
    small = val_sum[local:].astype(F32)
    return (
        layer_out,
        input_grad,
        grad_query,
        grad_key,
        grad_value,
        grad_output,
        small[4 : 4 + own, :KW],
        small[0],
        small[1],
        grad_inner,
        grad_outer,
        small[2],
        small[3],
    )


def solution(mesh):
    tokens = P(("batch", "head"), None)
    row = P("batch")
    cols = P(None, "head")
    lines = P("head", None)
    rep = P()
    return jax.shard_map(
        functools.partial(shards, mesh.shape["batch"]),
        mesh=mesh,
        in_specs=(
            tokens, row, row, row, cols, cols, cols, lines, lines,
            rep, rep, rep, rep, rep, rep, tokens,
        ),
        out_specs=(
            tokens, tokens, cols, cols, cols, lines, lines, rep, rep, cols, lines, rep, rep,
        ),
        check_vma=False,
    )
```

```python
import functools

import jax
import jax.numpy as jnp
from jax import lax
from jax.experimental import pallas as pl
from jax.experimental.pallas import tpu as pltpu
from jax.sharding import PartitionSpec as P

LAND = 64
KW = 33
HALF = KW // 2
HEAD_DIM = 64
NEWTON = 6
DOCS = 4
SEGS = DOCS * LAND
WIDE = 2 * SEGS
BLOCK = 128
CHUNK = 256
QK_SCALE = HEAD_DIM ** (-0.25)
FAR_TYPE = jnp.bfloat16
TAP_ROWS = 16

NEG_FILL = -1e30
NORM_EPS = 1e-05
BF = jnp.bfloat16
F32 = jnp.float32


def norm_forward(hidden, scale_vec, shift_vec):
    center = hidden - jnp.mean(hidden, axis=-1, keepdims=True)
    inv_spread = lax.rsqrt(jnp.mean(center * center, axis=-1, keepdims=True) + NORM_EPS)
    normed = center * inv_spread
    return (normed * scale_vec + shift_vec, normed, inv_spread)


def norm_backward(upstream, normed, inv_spread, scale_vec):
    scaled = upstream * scale_vec
    result_grad = inv_spread * (
        scaled
        - jnp.mean(scaled, axis=-1, keepdims=True)
        - normed * jnp.mean(scaled * normed, axis=-1, keepdims=True)
    )
    return (result_grad, jnp.sum(upstream * normed, axis=0), jnp.sum(upstream, axis=0))


def nn(a, b):
    return lax.dot_general(a, b, (((1,), (0,)), ((), ())), preferred_element_type=F32)


def nt(a, b):
    return lax.dot_general(a, b, (((1,), (1,)), ((), ())), preferred_element_type=F32)


def tn(a, b):
    return lax.dot_general(a, b, (((0,), (0,)), ((), ())), preferred_element_type=F32)


def pair_block(ref):
    zero = jnp.zeros((HEAD_DIM, SEGS), BF)
    top = jnp.concatenate([ref[0, :HEAD_DIM, :].astype(BF), zero], axis=1)
    low = jnp.concatenate([zero, ref[1, :HEAD_DIM, :].astype(BF)], axis=1)
    return jnp.concatenate([top, low], axis=0)


def put_pair(ref, value):
    ref[0] = value[:HEAD_DIM, :SEGS].astype(ref.dtype)
    ref[1] = value[HEAD_DIM:, SEGS:].astype(ref.dtype)


def doc_bias(code):
    lane_doc = lax.broadcasted_iota(jnp.int32, (code.shape[0], SEGS), 1) // LAND
    return jnp.where(code == lane_doc, 0.0, NEG_FILL)


def rows_of(i, size, base=0):
    return pl.ds(pl.multiple_of(base + i * size, 16), size)


def third_kernel(code_ref, k_ref, v_ref, lq_ref, c_ref, e_ref, s_scr, acc):
    steps = k_ref.shape[0] // CHUNK
    lq2 = pair_block(lq_ref)

    def scores(i, top):
        r = rows_of(i, CHUNK)
        bias = doc_bias(code_ref[r, :])
        s = nn(k_ref[r, :], lq2) + jnp.concatenate([bias, bias], axis=1)
        s_scr[r, :] = s
        return jnp.maximum(top, jnp.max(s, axis=0, keepdims=True))

    top = lax.fori_loop(0, steps, scores, jnp.full((1, WIDE), 3.0 * NEG_FILL, F32), unroll=True)
    acc[...] = jnp.zeros_like(acc)

    def weigh(i, total):
        r = rows_of(i, CHUNK)
        e = jnp.exp(s_scr[r, :] - top)
        low = e.astype(BF)
        e_ref[r, :] = low
        acc[...] += tn(v_ref[rows_of(i, CHUNK, HALF), :], low)
        return total + jnp.sum(e, axis=0, keepdims=True)

    total = lax.fori_loop(0, steps, weigh, jnp.zeros((1, WIDE), F32), unroll=True)
    mean = acc[...] / total
    for side in (0, 1):
        cols = slice(side * SEGS, (side + 1) * SEGS)
        c_ref[side, :HEAD_DIM, :] = mean[side * HEAD_DIM : (side + 1) * HEAD_DIM, cols]
        low = [top[:, cols], total[:, cols], jnp.zeros((6, SEGS), F32)]
        c_ref[side, HEAD_DIM:, :] = jnp.concatenate(low, axis=0)


def skew(x, left):
    row = lax.broadcasted_iota(jnp.int32, x.shape, 0)
    lanes = x.shape[1]
    for bit in range(x.shape[0].bit_length() - 1):
        step = 1 << bit
        moved = pltpu.roll(x, lanes - step if left else step, 1)
        x = jnp.where((row & step) != 0, moved, x)
    return x


def band(w_ref, index):
    return skew(jnp.broadcast_to(w_ref[index], (BLOCK, 2 * BLOCK)), False).astype(BF)


def band_mask(code_ref, line_ref, i):
    line = line_ref[:, pl.ds(pl.multiple_of(i * BLOCK, BLOCK), 2 * BLOCK)]
    return code_ref[rows_of(i, BLOCK), :] == line


def conv_kernel(code_ref, line_ref, v_ref, w_ref, conv_ref, t_scr):
    t_scr[0] = band(w_ref, 0)
    t_scr[1] = band(w_ref, 1)
    left_lane = lax.broadcasted_iota(jnp.int32, (BLOCK, BLOCK), 1) < HEAD_DIM

    def convolve(i, carry):
        mask = band_mask(code_ref, line_ref, i)
        window = v_ref[rows_of(i, BLOCK), :], v_ref[rows_of(i + 1, BLOCK), :]
        window = jnp.concatenate(window, axis=0)
        zero = jnp.zeros((BLOCK, 2 * BLOCK), BF)
        one = nn(jnp.where(mask, t_scr[0], zero), window)
        two = nn(jnp.where(mask, t_scr[1], zero), window)
        conv_ref[rows_of(i, BLOCK), :] = jnp.where(left_lane, one, two)
        return carry

    lax.fori_loop(0, conv_ref.shape[0] // BLOCK, convolve, 0, unroll=True)


def first_kernel(code_ref, q_ref, lk_ref, p_ref):
    lk2 = pair_block(lk_ref)

    def weigh(i, carry):
        r = rows_of(i, CHUNK)
        bias = doc_bias(code_ref[r, :])
        s = nn(q_ref[r, :], lk2)
        for side in (0, 1):
            cols = slice(side * SEGS, (side + 1) * SEGS)
            part = s[:, cols] + bias
            e = jnp.exp(part - jnp.max(part, axis=1, keepdims=True))
            p_ref[r, cols] = (e * (1.0 / jnp.sum(e, axis=1, keepdims=True))).astype(BF)
        return carry

    lax.fori_loop(0, q_ref.shape[0] // CHUNK, weigh, 0, unroll=True)


def heads_kernel(code_ref, p_ref, mix_ref, conv_ref, out_ref):
    mix2 = pair_block(mix_ref)

    def body(i, carry):
        r = rows_of(i, CHUNK)
        total = nt(p_ref[r, :], mix2) + conv_ref[r, :]
        out_ref[r, :] = jnp.where(code_ref[r, :] >= 0, total, 0.0).astype(BF)
        return carry

    lax.fori_loop(0, p_ref.shape[0] // CHUNK, body, 0, unroll=True)


def mixed_grad_kernel(hg_ref, p_ref, mg_ref):
    put_pair(mg_ref, tn(hg_ref[...], p_ref[...]))


def first_back_kernel(hg_ref, p_ref, q_ref, mix_ref, lk_ref, dq_ref, lkg_ref, acc):
    mix2 = pair_block(mix_ref)
    lk2 = pair_block(lk_ref)
    acc[...] = jnp.zeros_like(acc)

    def body(i, carry):
        r = rows_of(i, CHUNK)
        g = nn(hg_ref[r, :], mix2)
        parts = []
        for side in (0, 1):
            cols = slice(side * SEGS, (side + 1) * SEGS)
            p = p_ref[r, cols].astype(F32)
            gp = g[:, cols] * p
            parts.append((gp - p * jnp.sum(gp, axis=1, keepdims=True)).astype(BF))
        ds = jnp.concatenate(parts, axis=1)
        dq_ref[r, :] = nt(ds, lk2).astype(BF)
        acc[...] += tn(q_ref[r, :], ds)
        return carry

    lax.fori_loop(0, p_ref.shape[0] // CHUNK, body, 0, unroll=True)
    put_pair(lkg_ref, acc[...])


def conv_back_kernel(
    code_ref, line_ref, hg_ref, edge_ref, v_ref, w_ref, part_ref, dv_ref, tap_ref, t_scr, acc, hgx
):
    rows = hg_ref.shape[0]
    hgx[:HALF, :] = edge_ref[:HALF, :]
    hgx[HALF : HALF + rows, :] = hg_ref[...]
    hgx[HALF + rows : 2 * HALF + rows, :] = edge_ref[HALF:, :]
    hgx[2 * HALF + rows :, :] = jnp.zeros((BLOCK - 2 * HALF, BLOCK), BF)
    t_scr[0] = band(w_ref, 0)
    t_scr[1] = band(w_ref, 1)
    acc[...] = jnp.zeros_like(acc)
    left_lane = lax.broadcasted_iota(jnp.int32, (BLOCK, BLOCK), 1) < HEAD_DIM

    def body(i, carry):
        mask = band_mask(code_ref, line_ref, i)
        grads = hgx[rows_of(i, BLOCK), :], hgx[rows_of(i + 1, BLOCK), :]
        grads = jnp.concatenate(grads, axis=0)
        vals = v_ref[rows_of(i, BLOCK), :], v_ref[rows_of(i + 1, BLOCK), :]
        vals = jnp.concatenate(vals, axis=0)
        zero = jnp.zeros((BLOCK, 2 * BLOCK), BF)
        one = nn(jnp.where(mask, t_scr[0], zero), grads)
        two = nn(jnp.where(mask, t_scr[1], zero), grads)
        r = rows_of(i, BLOCK)
        dv_ref[r, :] = (part_ref[r, :] + jnp.where(left_lane, one, two)).astype(BF)
        here = hg_ref[r, :]
        none = jnp.zeros_like(here)
        acc[0] += jnp.where(mask, nt(jnp.where(left_lane, here, none), vals), 0.0)
        acc[1] += jnp.where(mask, nt(jnp.where(left_lane, none, here), vals), 0.0)
        return carry

    lax.fori_loop(0, rows // BLOCK, body, 0, unroll=True)
    for side in (0, 1):
        tap_ref[side, 0:1, :] = jnp.sum(skew(acc[side], True), axis=0, keepdims=True)


def third_back_kernel(
    k_ref, v_ref, e_ref, f_ref, d_ref, cg_ref, lq_ref, dk_ref, dv_ref, lqg_ref, acc
):
    cg2 = pair_block(cg_ref)
    lq2 = pair_block(lq_ref)
    factor = jnp.concatenate([f_ref[0], f_ref[1]], axis=1)
    delta = jnp.concatenate([d_ref[0], d_ref[1]], axis=1)
    acc[...] = jnp.zeros_like(acc)

    def body(i, carry):
        r = rows_of(i, CHUNK)
        h = nn(v_ref[rows_of(i, CHUNK, HALF), :], cg2)
        p = e_ref[r, :].astype(F32) * factor
        ds = (p * (h - delta)).astype(BF)
        dk_ref[r, :] = nt(ds, lq2).astype(BF)
        dv_ref[r, :] = nt(p.astype(BF), cg2)
        acc[...] += tn(k_ref[r, :], ds)
        return carry

    lax.fori_loop(0, e_ref.shape[0] // CHUNK, body, 0, unroll=True)
    put_pair(lqg_ref, acc[...])


def feed_kernel(x_ref, wi_ref, wo_ref, act_ref, slope_ref, out_ref):
    @pl.when(pl.program_id(0) == 0)
    def _():
        out_ref[...] = jnp.zeros_like(out_ref)

    def body(i, carry):
        r = rows_of(i, CHUNK)
        pre = nn(x_ref[r, :], wi_ref[...])
        cdf = 0.5 * (1.0 + lax.erf(pre * (0.5**0.5)))
        pdf = jnp.exp(-0.5 * pre * pre) * 0.3989422804014327
        act = (pre * cdf).astype(BF)
        act_ref[r, :] = act
        slope_ref[r, :] = (cdf + pre * pdf).astype(BF)
        out_ref[r, :] += nn(act, wo_ref[...])
        return carry

    lax.fori_loop(0, x_ref.shape[0] // CHUNK, body, 0, unroll=True)


def feed_back_kernel(
    table, og_ref, x_ref, wi_ref, wo_ref, act_ref, slope_ref, prev_ref, gi_ref, go_ref, fg_ref, pg
):
    @pl.when(pl.program_id(0) == 0)
    def _():
        fg_ref[...] = prev_ref[...]

    def body(i, carry):
        r = rows_of(i, CHUNK)
        grad = nt(og_ref[r, :], wo_ref[...])
        low = (slope_ref[r, :].astype(F32) * grad).astype(BF)
        pg[r, :] = low
        fg_ref[r, :] += nt(low, wi_ref[...])
        return carry

    lax.fori_loop(0, og_ref.shape[0] // CHUNK, body, 0, unroll=True)
    gi_ref[0] = tn(x_ref[...], pg[...]).astype(BF)
    go_ref[0] = tn(act_ref[...], og_ref[...]).astype(BF)


def split_low(a):
    high = a.astype(BF)
    return high, (a - high.astype(F32)).astype(BF)


def spread_docs(a):
    tall = jnp.concatenate([a] * DOCS, axis=0)
    row = lax.broadcasted_iota(jnp.int32, tall.shape, 0) // LAND
    lane = lax.broadcasted_iota(jnp.int32, tall.shape, 1) // LAND
    return jnp.where(row == lane, tall, jnp.zeros_like(tall))


def fold_docs(a):
    lane = lax.broadcasted_iota(jnp.int32, (LAND, SEGS), 1) // LAND
    out = a[:LAND]
    for doc in range(1, DOCS):
        out = jnp.where(lane == doc, a[doc * LAND : (doc + 1) * LAND], out)
    return out


def blocks_of(a):
    high, low = split_low(a)
    return spread_docs(high), spread_docs(low)


def times(a, blocks, form=nn):
    high, low = split_low(a)
    both = form(jnp.concatenate([high, low], axis=0), blocks[0])
    return both[:LAND] + (both[LAND:] + form(high, blocks[1]))


def cross(a, b):
    ah, al = split_low(a)
    bh, bl = split_low(b)
    return tn(ah, bh) + (tn(ah, bl) + tn(al, bh))


def doc_sum(a):
    line = jnp.sum(a, axis=0, keepdims=True)
    lane = lax.broadcasted_iota(jnp.int32, line.shape, 1) // LAND
    out = jnp.zeros_like(line)
    for doc in range(DOCS):
        part = jnp.sum(jnp.where(lane == doc, line, 0.0), axis=1, keepdims=True)
        out = jnp.where(lane == doc, part, out)
    return out


def eye_docs():
    row = lax.broadcasted_iota(jnp.int32, (LAND, SEGS), 0)
    lane = lax.broadcasted_iota(jnp.int32, (LAND, SEGS), 1) % LAND
    return jnp.where(row == lane, 1.0, 0.0)


def newton_kernel(lq_ref, lk_ref, inv_ref, at_ref, save_ref):
    heads = lq_ref.shape[0]
    eye = eye_docs()
    fixed, state = [], []
    for h in range(heads):
        scores = fold_docs(tn(lk_ref[h], lq_ref[h]))
        e = jnp.exp(scores - jnp.max(scores, axis=0, keepdims=True))
        at = e / jnp.sum(e, axis=0, keepdims=True)
        at_ref[h] = at
        blocks = blocks_of(at)
        fixed.append(blocks)
        state.append(times(eye, blocks, nt) / doc_sum(at * at))
    for step in range(NEWTON):
        x = [times(w, b) for w, b in zip(state, fixed)]
        t2 = [15.0 * eye - times(a, blocks_of(7.0 * eye - a)) for a in x]
        t3 = [13.0 * eye - times(a, blocks_of(b)) for a, b in zip(x, t2)]
        for h in range(heads):
            save_ref[step, h, 0] = state[h]
            save_ref[step, h, 1] = x[h]
            save_ref[step, h, 2] = t2[h]
            save_ref[step, h, 3] = t3[h]
        state = [0.25 * times(t, blocks_of(w)) for t, w in zip(t3, state)]
    for h in range(heads):
        inv_ref[h] = state[h]


def join_packs(a, b):
    top_a, top_b = a[HEAD_DIM : HEAD_DIM + 1], b[HEAD_DIM : HEAD_DIM + 1]
    top = jnp.maximum(top_a, top_b)
    share_a = a[HEAD_DIM + 1 : HEAD_DIM + 2] * jnp.exp(top_a - top)
    share_b = b[HEAD_DIM + 1 : HEAD_DIM + 2] * jnp.exp(top_b - top)
    total = share_a + share_b
    mean = (a[:HEAD_DIM] * share_a + b[:HEAD_DIM] * share_b) / total
    return mean, top, total


def join_kernel(a_ref, b_ref, o_ref):
    for h in range(a_ref.shape[0]):
        mean, top, total = join_packs(a_ref[h], b_ref[h])
        rest = jnp.zeros((6, SEGS), F32)
        o_ref[h] = jnp.concatenate([mean, top, total, rest], axis=0)


def three_parts(a):
    one = a.astype(BF)
    left = a - one.astype(F32)
    two = left.astype(BF)
    three = (left - two.astype(F32)).astype(BF)
    rows = [one.astype(F32), two.astype(F32), three.astype(F32), jnp.zeros((13, a.shape[1]), F32)]
    return jnp.concatenate(rows, axis=0).astype(BF)


def mix_kernel(a_ref, b_ref, inv_ref, mix_ref, carried_ref):
    for h in range(a_ref.shape[0]):
        mean, top, total = join_packs(a_ref[h], b_ref[h])
        carried_ref[h] = mean
        mix_ref[h, :HEAD_DIM, :] = times(mean, blocks_of(inv_ref[h])).astype(BF)
        mix_ref[h, HEAD_DIM:, :] = three_parts(top + jnp.log(total))


def carry_back_kernel(a_ref, b_ref, carried_ref, inv_ref, mg_ref, cg_ref):
    for h in range(a_ref.shape[0]):
        mg = a_ref[h] + b_ref[h]
        mg_ref[h] = mg
        cg = times(mg, blocks_of(inv_ref[h]), nt).astype(BF)
        cg_ref[h, :HEAD_DIM, :] = cg
        delta = jnp.sum(cg.astype(F32) * carried_ref[h], axis=0, keepdims=True)
        cg_ref[h, HEAD_DIM:, :] = three_parts(delta)


def newton_back_kernel(mg_ref, carried_ref, at_ref, save_ref, lq_ref, lk_ref, dq_ref, dk_ref, acc):
    heads = mg_ref.shape[0]
    eye = eye_docs()
    at = [at_ref[h] for h in range(heads)]
    fixed = [blocks_of(a) for a in at]
    grad = [fold_docs(cross(carried_ref[h], mg_ref[h])) for h in range(heads)]
    for step in reversed(range(NEWTON)):
        w, x, t2, t3 = ([save_ref[step, h, kind] for h in range(heads)] for kind in range(4))
        t3g = [0.25 * times(g, blocks_of(a), nt) for g, a in zip(grad, w)]
        wg = [0.25 * times(a, blocks_of(g)) for a, g in zip(t3, grad)]
        t2g = [-times(a, blocks_of(g)) for a, g in zip(x, t3g)]
        xg = [-times(g, blocks_of(a)) for g, a in zip(t3g, t2)]
        t1g = [-times(a, blocks_of(g)) for a, g in zip(x, t2g)]
        xg = [
            a - times(g, blocks_of(7.0 * eye - b)) - c
            for a, g, b, c in zip(xg, t2g, x, t1g)
        ]
        grad = [a + times(g, b, nt) for a, g, b in zip(wg, xg, fixed)]
        for h in range(heads):
            part = cross(w[h], xg[h])
            acc[h] = part if step == NEWTON - 1 else acc[h] + part
    for h in range(heads):
        square = doc_sum(at[h] * at[h])
        start = times(eye, fixed[h], nt)
        start_grad = grad[h] / square - start * (2.0 * doc_sum(grad[h] * start) / (square * square))
        atg = fold_docs(acc[h]) + times(eye, blocks_of(start_grad), nt)
        sg = at[h] * (atg - jnp.sum(atg * at[h], axis=0, keepdims=True))
        blocks = blocks_of(sg)
        dq_ref[h] = nn(lk_ref[h], blocks[0]) + nn(lk_ref[h], blocks[1])
        dk_ref[h] = nt(lq_ref[h], blocks[0]) + nt(lq_ref[h], blocks[1])


def project_kernel(x_ref, one_ref, two_ref, q_ref, k_ref, v_ref):
    local = (one_ref.shape[0] - TAP_ROWS) // 3
    rows = q_ref.shape[0]
    weights = []
    for kind in range(3):
        cut = slice(kind * local, (kind + 1) * local)
        weights.append(jnp.concatenate([one_ref[cut, :], two_ref[cut, :]], axis=0))
    size = 2 * BLOCK
    for i in range(rows // size):
        x = x_ref[HALF + i * size : HALF + (i + 1) * size, :]
        r = slice(i * size, (i + 1) * size)
        q_ref[r, :] = (nt(x, weights[0]) * QK_SCALE).astype(BF)
        k_ref[r, :] = (nt(x, weights[1]) * QK_SCALE).astype(BF)
        v_ref[HALF + i * size : HALF + (i + 1) * size, :] = nt(x, weights[2]).astype(BF)
    ends = jnp.concatenate([x_ref[:HALF, :], x_ref[HALF + rows :, :]], axis=0)
    ends = nt(ends, weights[2]).astype(BF)
    v_ref[:HALF, :] = ends[:HALF]
    v_ref[HALF + rows :, :] = ends[HALF:]


def landmark_kernel(land_ref, one_ref, two_ref, lq_ref, lk_ref):
    local = (one_ref.shape[0] - TAP_ROWS) // 3
    high, low = split_low(land_ref[...])
    for kind, out in ((0, lq_ref), (1, lk_ref)):
        for index, part in enumerate((one_ref, two_ref)):
            weight = part[kind * local : (kind + 1) * local, :]
            mapped = ((nt(weight, high) + nt(weight, low)) * QK_SCALE).astype(BF)
            for h in range(local // HEAD_DIM):
                head = index * (local // HEAD_DIM) + h
                out[head] = mapped[h * HEAD_DIM : (h + 1) * HEAD_DIM]


def weight_grad_kernel(count, with_land, x_ref, *refs):
    keep_ref, send_ref = refs[-2:]
    lows, rest = refs[: 2 * count], refs[2 * count : -2]
    x = x_ref[...]
    for index in range(count):
        for half in (0, 1):
            total = tn(lows[2 * index + half][...], x)
            if with_land:
                land = rest[1 + 2 * index + half]
                flat = [land[h].astype(BF) for h in range(land.shape[0])]
                total = total + nn(jnp.concatenate(flat, axis=0), rest[0][...])
                total = total * QK_SCALE
            local = total.shape[0] // 2
            cut = slice(index * local, (index + 1) * local)
            keep_ref[half, cut, :] = total[:local].astype(BF)
            send_ref[half, cut, :] = total[local:].astype(BF)


def input_grad_kernel(base_ref, *refs):
    out_ref = refs[-1]
    lows, pieces = refs[:6], refs[6:10]
    local = (pieces[0].shape[0] - TAP_ROWS) // 3
    weights = []
    for kind in range(3):
        cut = slice(kind * local, (kind + 1) * local)
        for half in (0, 1):
            parts = [pieces[2 * half][cut, :], pieces[2 * half + 1][cut, :]]
            weights.append(jnp.concatenate(parts, axis=0))
    scaled = sum(nn(lows[j][...], weights[j]) for j in range(4))
    direct = nn(lows[4][...], weights[4]) + nn(lows[5][...], weights[5])
    out_ref[...] = base_ref[...] + QK_SCALE * scaled + direct


def call(body, grid, ins, outs, scratch=(), flops=0, moved=0, limit=20):
    return pl.pallas_call(
        body,
        grid=grid,
        in_specs=[spec for spec in ins],
        out_specs=[spec for spec, _ in outs],
        out_shape=[shape for _, shape in outs],
        scratch_shapes=list(scratch),
        compiler_params=pltpu.CompilerParams(vmem_limit_bytes=limit << 20),
        cost_estimate=pl.CostEstimate(flops=flops // 50, bytes_accessed=moved // 50, transcendentals=0),
    )


def plain(body, outs, scratch=(), flops=0, moved=0, limit=20):
    return pl.pallas_call(
        body,
        out_shape=list(outs),
        scratch_shapes=list(scratch),
        compiler_params=pltpu.CompilerParams(vmem_limit_bytes=limit << 20),
        cost_estimate=pl.CostEstimate(flops=flops // 50, bytes_accessed=moved // 50, transcendentals=0),
    )


def whole(shape):
    return pl.BlockSpec(shape, lambda p: (0,) * len(shape))


def column(rows, width):
    return pl.BlockSpec((rows, width), lambda p: (0, p))


def heads_spec(rows, cols):
    return pl.BlockSpec((2, rows, cols), lambda p: (p, 0, 0))


def shape_of(shape, dtype):
    return jax.ShapeDtypeStruct(shape, dtype)


def shards(
    batch_size,
    tokens_in,
    doc_ids,
    landmark_ids,
    pad_mask,
    w_query,
    w_key,
    w_value,
    w_output,
    conv_weight,
    first_gain,
    first_bias,
    w_inner,
    w_outer,
    second_gain,
    second_bias,
    out_grad,
):
    groups = 4
    rows, width = tokens_in.shape
    local = w_query.shape[1]
    own = local // HEAD_DIM
    side = 2 * own
    side_cols = 2 * local
    pairs = side // 2
    ext = rows + BLOCK
    ff = w_inner.shape[1]
    me = lax.axis_index("head")
    bat = lax.axis_index("batch")
    core = me & 1

    def swap(value, bit, name="swap"):
        with jax.named_scope(name):
            return lax.ppermute(value, "head", [(i, i ^ bit) for i in range(groups)])

    def swap_batch(value, bit, name="swap"):
        with jax.named_scope(name):
            return lax.ppermute(value, "batch", [(i, i ^ bit) for i in range(batch_size)])

    def spread(value, name):
        two = swap(value, 2, name)
        return value, swap(value, 1, name), two, swap(two, 1, name)

    def add_low(a, b):
        return (a.astype(F32) + b.astype(F32)).astype(BF)

    def gate(*values):
        return lax.optimization_barrier(values)

    def ordered(low_bit, mine, other):
        first = jnp.where(low_bit == 0, mine, other)
        second = jnp.where(low_bit == 0, other, mine)
        return jnp.concatenate([first, second], axis=0)

    def halves(value, flag):
        half = value.shape[0] // 2
        mine = lax.dynamic_slice_in_dim(value, flag * half, half, 0)
        return mine, lax.dynamic_slice_in_dim(value, (1 - flag) * half, half, 0)

    def head_sum(value, name, far=F32):
        mine, other = halves(value, core)
        mine = mine + swap(other, 1, name)
        mine = mine.astype(far)
        mine = mine.astype(F32) + swap(mine, 2, name).astype(F32)
        return ordered(core, mine, swap(mine, 1, name))

    bits = [1 << b for b in range(batch_size.bit_length() - 1)]

    def gather_heads(value, name):
        parts = value, swap(value, 1, name), swap(value, 2, name), swap(value, 3, name)
        return [jnp.concatenate(parts[2 * half : 2 * half + 2], axis=0) for half in (0, 1)]

    def hop_sum(value, got):
        return (value.astype(F32) + got.astype(F32)).astype(BF)

    code_row = jnp.where(pad_mask > 0, doc_ids, -1)
    outside = jnp.full((BLOCK - HALF,), -2, jnp.int32)
    code_pad = jnp.concatenate([outside[:HALF], code_row, outside])
    line = lax.dynamic_slice_in_dim(code_pad, me * rows, ext, 0)
    code = line[HALF : HALF + rows].reshape(rows, 1)
    line = line.reshape(1, ext)
    segment_row = jnp.where(pad_mask > 0, doc_ids * LAND + landmark_ids, -1)
    tap_pad = jnp.pad(conv_weight, ((0, TAP_ROWS - own), (0, width - KW)))
    packed = jnp.concatenate([w_query.T, w_key.T, w_value.T, tap_pad], axis=0)
    packed, segment_row = gate(packed, segment_row)
    columns = jnp.arange(SEGS, dtype=jnp.int32)
    counts = jnp.sum((segment_row[:, None] == columns[None, :]).astype(F32), axis=0)
    segment = lax.dynamic_slice_in_dim(segment_row, me * rows, rows, 0)
    member = (segment[:, None] == columns[None, :]).astype(BF)

    packed, member_in = gate(packed, member)
    got = spread(packed, "weights")
    out_packed, far_weights = gate(w_output, got[2])
    got = got[:2] + (far_weights,) + got[3:]
    out_far = swap(out_packed, 2, "w_output")
    out_parts = (
        out_packed, swap(out_packed, 1, "w_output"), out_far, swap(out_far, 1, "w_output")
    )

    wo = [
        jnp.concatenate([out_parts[2 * half + j] for j in (0, 1)], axis=0)
        for half in (0, 1)
    ]
    tap_rows = [
        jnp.concatenate(
            [got[2 * half + j][3 * local : 3 * local + own, :KW] for j in (0, 1)], axis=0
        )
        for half in (0, 1)
    ]

    def tap_lines(value):
        value = jnp.pad(value.astype(F32), ((0, 0), (0, 2 * BLOCK - KW)))
        return value.reshape(side, 1, 2 * BLOCK)

    def with_edges(value):
        before = lax.ppermute(value[-HALF:], "head", [(i, i + 1) for i in range(groups - 1)])
        after = lax.ppermute(value[:HALF], "head", [(i + 1, i) for i in range(groups - 1)])
        rest = jnp.zeros((BLOCK - 2 * HALF, value.shape[1]), value.dtype)
        return jnp.concatenate([before, value, after, rest], axis=0)

    tokens_ext = with_edges(tokens_in)

    land_part = tn(member_in, tokens_in) / counts[:, None]
    land_sum = head_sum(land_part, "land", FAR_TYPE)
    land_tokens = land_sum.astype(BF)

    queries, keys, values, land_q, land_k = [], [], [], [], []
    low_shape = shape_of((rows, side_cols), BF)
    land_shape = shape_of((side, HEAD_DIM, SEGS), BF)
    for half in (0, 1):
        one, two = got[2 * half : 2 * half + 2]
        projected = plain(
            project_kernel, [low_shape, low_shape, shape_of((ext, side_cols), BF)]
        )(tokens_ext, one, two)
        for target, value in zip((queries, keys, values), projected):
            target.append(value)
    for half in (0, 1):
        one, two = got[2 * half : 2 * half + 2]
        for target, value in zip(
            (land_q, land_k), plain(landmark_kernel, [land_shape, land_shape])(land_sum, one, two)
        ):
            target.append(value)

    third_call = call(
        third_kernel,
        (pairs,),
        [whole((rows, 1)), column(rows, BLOCK), column(ext, BLOCK), heads_spec(HEAD_DIM, SEGS)],
        [
            (heads_spec(HEAD_DIM + 8, SEGS), shape_of((side, HEAD_DIM + 8, SEGS), F32)),
            (column(rows, WIDE), shape_of((rows, side * SEGS), BF)),
        ],
        [pltpu.VMEM((rows, WIDE), F32), pltpu.VMEM((BLOCK, WIDE), F32)],
        flops=4 * rows * side_cols * SEGS,
        moved=2 * rows * (side_cols * 2 + side * SEGS),
    )
    packs, third_exp = [], []
    for half in (0, 1):
        third_land = land_q[half]
        if half == 1:
            third_land, wo, tap_rows = gate(third_land, wo, tap_rows)
        pack, e_out = third_call(code, keys[half], values[half], third_land)
        packs.append(pack)
        third_exp.append(e_out)

    tall = HEAD_DIM + 8
    pack_keep = jnp.concatenate([part[:own] for part in packs], axis=0)
    pack_send = jnp.concatenate([part[own:] for part in packs], axis=0)
    docs_shape = shape_of((own, HEAD_DIM, SEGS), F32)
    own_q, own_k, pack_send = gate(land_q[0][:own], land_k[0][:own], pack_send)
    pack_core = swap(pack_send, 1, "pack")
    inverse, small_t, saved = plain(
        newton_kernel,
        [docs_shape, docs_shape, shape_of((NEWTON, own, 4, HEAD_DIM, SEGS), F32)],
        flops=own * NEWTON * 4 * 6 * LAND * SEGS * SEGS,
        moved=4 * own * NEWTON * 4 * HEAD_DIM * SEGS,
    )(own_q, own_k)
    pack_core, inverse = gate(pack_core, inverse)
    joined = plain(join_kernel, [shape_of((side, tall, SEGS), F32)], moved=12 * side * tall * SEGS)(
        pack_keep, pack_core
    )[0]

    first_call = call(
        first_kernel,
        (pairs,),
        [whole((rows, 1)), column(rows, BLOCK), heads_spec(HEAD_DIM, SEGS)],
        [(column(rows, WIDE), shape_of((rows, side * SEGS), BF))],
        flops=2 * rows * side_cols * SEGS,
        moved=2 * rows * (side_cols + side * SEGS),
    )
    conv_call = call(
        conv_kernel,
        (pairs,),
        [whole((rows, 1)), whole((1, ext)), column(ext, BLOCK), heads_spec(1, 2 * BLOCK)],
        [(column(rows, BLOCK), shape_of((rows, side_cols), F32))],
        [pltpu.VMEM((2, BLOCK, 2 * BLOCK), BF)],
        flops=2 * rows * side_cols * SEGS,
        moved=2 * rows * (side_cols * 3),
    )
    heads_call = call(
        heads_kernel,
        (pairs,),
        [
            whole((rows, 1)),
            column(rows, WIDE),
            heads_spec(HEAD_DIM + 16, SEGS),
            column(rows, BLOCK),
        ],
        [(column(rows, BLOCK), shape_of((rows, side_cols), BF))],
        flops=2 * rows * side_cols * SEGS,
        moved=2 * rows * (side_cols * 3 + side * SEGS),
    )
    wait_in, far_send = gate((queries, values), joined[own:])
    pack_far = swap(far_send, 2, "pack_x")
    queries, values = wait_in
    first_low = [first_call(code, queries[half], land_k[half])[0] for half in (0, 1)]
    pack_far, first_low = gate(pack_far, first_low)
    mixed_own, carried = plain(
        mix_kernel,
        [shape_of((own, HEAD_DIM + 16, SEGS), BF), docs_shape],
        flops=6 * own * LAND * SEGS * SEGS,
        moved=16 * own * tall * SEGS,
    )(joined[:own], pack_far, inverse)
    values_in, mixed_own = gate(values, mixed_own)
    mixed = gather_heads(mixed_own, "mixed")
    conv_outs = [
        conv_call(code, line, values_in[half], tap_lines(tap_rows[half]))[0] for half in (0, 1)
    ]
    mixed, conv_outs = gate(mixed, conv_outs)

    def row_of(parts):
        return [
            jnp.sum(part[:, HEAD_DIM : HEAD_DIM + 3].astype(F32), axis=1, keepdims=True)
            for part in parts
        ]

    heads_out = [
        heads_call(code, first_low[half], mixed[half], conv_outs[half])[0] for half in (0, 1)
    ]
    projected = nn(heads_out[0], wo[0]) + nn(heads_out[1], wo[1])
    first_out, first_normed, first_inv = norm_forward(
        tokens_in.astype(F32) + projected, first_gain, first_bias
    )
    norm_low = first_out.astype(BF)

    block = 512 if ff % 512 == 0 else ff
    act, slope, outer_out = call(
        feed_kernel,
        (ff // block,),
        [whole((rows, width)), column(width, block), pl.BlockSpec((block, width), lambda p: (p, 0))],
        [
            (column(rows, block), shape_of((rows, ff), BF)),
            (column(rows, block), shape_of((rows, ff), BF)),
            (whole((rows, width)), shape_of((rows, width), F32)),
        ],
        flops=4 * rows * width * ff,
        moved=2 * (2 * width * ff + 2 * rows * ff + 3 * rows * width),
        limit=30,
    )(norm_low, w_inner, w_outer)
    second_out, second_normed, second_inv = norm_forward(
        first_out + outer_out, second_gain, second_bias
    )
    layer_out = second_out.astype(BF)
    second_grad, grad_second_gain, grad_second_bias = norm_backward(
        out_grad.astype(F32), second_normed, second_inv, second_gain
    )
    outer_low = second_grad.astype(BF)

    share = ff // groups
    cut = share // 2

    def feed_back(slots, previous):
        table = jnp.stack([(me ^ slot) * 2 + part for slot in slots for part in (0, 1)])
        grid_spec = pltpu.PrefetchScalarGridSpec(
            num_scalar_prefetch=1,
            grid=(2 * len(slots),),
            in_specs=[
                pl.BlockSpec((rows, width), lambda p, t: (0, 0)),
                pl.BlockSpec((rows, width), lambda p, t: (0, 0)),
                pl.BlockSpec((width, cut), lambda p, t: (0, t[p])),
                pl.BlockSpec((cut, width), lambda p, t: (t[p], 0)),
                pl.BlockSpec((rows, cut), lambda p, t: (0, t[p])),
                pl.BlockSpec((rows, cut), lambda p, t: (0, t[p])),
                pl.BlockSpec((rows, width), lambda p, t: (0, 0)),
            ],
            out_specs=[
                pl.BlockSpec((1, width, cut), lambda p, t: (p // 2, 0, p % 2)),
                pl.BlockSpec((1, cut, width), lambda p, t: (p // 2, p % 2, 0)),
                pl.BlockSpec((rows, width), lambda p, t: (0, 0)),
            ],
            scratch_shapes=[pltpu.VMEM((rows, cut), BF)],
        )
        return pl.pallas_call(
            feed_back_kernel,
            grid_spec=grid_spec,
            out_shape=[
                shape_of((len(slots), width, share), BF),
                shape_of((len(slots), share, width), BF),
                shape_of((rows, width), F32),
            ],
            compiler_params=pltpu.CompilerParams(vmem_limit_bytes=36 << 20),
            cost_estimate=pl.CostEstimate(
                flops=8 * rows * width * share * len(slots),
                bytes_accessed=2 * len(slots) * share * (4 * width + 2 * rows) + 12 * rows * width,
                transcendentals=0,
            ),
        )(table, outer_low, norm_low, w_inner, w_outer, act, slope, previous)

    gi_send, go_send, first_grad = feed_back((1, 3), second_grad)
    gi_core, go_core = swap(gi_send, 1, "inner_core"), swap(go_send, 1, "outer_core")
    gi_keep, go_keep, first_grad = feed_back((0, 2), first_grad)
    first_grad, gi_core, go_core = gate(first_grad, gi_core, go_core)
    outer_flags = [jnp.where((bat & bit) != 0, 1, 0) for bit in bits]

    def split_rows(value, flag):
        half = value.shape[1] // 2
        mine = lax.dynamic_slice_in_dim(value, flag * half, half, 1)
        return mine, lax.dynamic_slice_in_dim(value, (1 - flag) * half, half, 1)

    own_keep, other_keep = split_rows(go_keep, outer_flags[0])
    own_core, other_core = split_rows(go_core, outer_flags[0])
    first_grad, near_send, far_send = gate(
        first_grad, add_low(other_keep, other_core), add_low(gi_keep[1], gi_core[1])
    )
    outer_near = swap_batch(near_send, bits[0], "outer_y")
    inner_far = swap(far_send, 2, "inner_x")
    first_in_grad, grad_first_gain, grad_first_bias = norm_backward(
        first_grad, first_normed, first_inv, first_gain
    )
    proj_low = first_in_grad.astype(BF)

    def edge_rows(value, name):
        with jax.named_scope(name):
            down = [(i, i + 1) for i in range(groups - 1)]
            up = [(i + 1, i) for i in range(groups - 1)]
            before = lax.ppermute(value[-HALF:], "head", down)
            after = lax.ppermute(value[:HALF], "head", up)
        return jnp.concatenate([before, after], axis=0)

    heads_grad = [
        jnp.where(code >= 0, nt(proj_low, wo[half]), 0.0).astype(BF) for half in (0, 1)
    ]

    mixed_grad_call = call(
        mixed_grad_kernel,
        (pairs,),
        [column(rows, BLOCK), column(rows, WIDE)],
        [(heads_spec(HEAD_DIM, SEGS), shape_of((side, HEAD_DIM, SEGS), F32))],
        flops=2 * rows * side_cols * SEGS,
        moved=2 * rows * (side_cols + side * SEGS),
    )
    mixed_part = [mixed_grad_call(heads_grad[half], first_low[half])[0] for half in (0, 1)]

    mg_keep = jnp.concatenate([part[:own] for part in mixed_part], axis=0)
    mg_send = jnp.concatenate([part[own:] for part in mixed_part], axis=0)
    heads_grad, mg_keep, mg_send = gate(heads_grad, mg_keep, mg_send)
    mg_core = swap(mg_send, 1, "mixed_grad")

    first_back_call = call(
        first_back_kernel,
        (pairs,),
        [
            column(rows, BLOCK),
            column(rows, WIDE),
            column(rows, BLOCK),
            heads_spec(HEAD_DIM + 16, SEGS),
            heads_spec(HEAD_DIM, SEGS),
        ],
        [
            (column(rows, BLOCK), shape_of((rows, side_cols), BF)),
            (heads_spec(HEAD_DIM, SEGS), shape_of((side, HEAD_DIM, SEGS), F32)),
        ],
        [pltpu.VMEM((BLOCK, WIDE), F32)],
        flops=6 * rows * side_cols * SEGS,
        moved=2 * rows * (side_cols * 3 + side * SEGS),
    )
    conv_back_call = call(
        conv_back_kernel,
        (pairs,),
        [
            whole((rows, 1)),
            whole((1, ext)),
            column(rows, BLOCK),
            column(2 * HALF, BLOCK),
            column(ext, BLOCK),
            heads_spec(1, 2 * BLOCK),
            column(rows, BLOCK),
        ],
        [
            (column(rows, BLOCK), shape_of((rows, side_cols), BF)),
            (heads_spec(8, 2 * BLOCK), shape_of((side, 8, 2 * BLOCK), F32)),
        ],
        [
            pltpu.VMEM((2, BLOCK, 2 * BLOCK), BF),
            pltpu.VMEM((2, BLOCK, 2 * BLOCK), F32),
            pltpu.VMEM((ext, BLOCK), BF),
        ],
        flops=4 * rows * side_cols * SEGS,
        moved=2 * rows * side_cols * 5,
    )
    third_back_call = call(
        third_back_kernel,
        (pairs,),
        [
            column(rows, BLOCK),
            column(ext, BLOCK),
            column(rows, WIDE),
            heads_spec(1, SEGS),
            heads_spec(1, SEGS),
            heads_spec(HEAD_DIM + 16, SEGS),
            heads_spec(HEAD_DIM, SEGS),
        ],
        [
            (column(rows, BLOCK), shape_of((rows, side_cols), BF)),
            (column(rows, BLOCK), shape_of((rows, side_cols), F32)),
            (heads_spec(HEAD_DIM, SEGS), shape_of((side, HEAD_DIM, SEGS), F32)),
        ],
        [pltpu.VMEM((BLOCK, WIDE), F32)],
        flops=8 * rows * side_cols * SEGS,
        moved=2 * rows * (side_cols * 6 + side * SEGS),
    )
    def slot_parts(parts):
        cut_rows = parts[0].shape[0] // 2
        keep = [part[:cut_rows] for part in parts]
        send = jnp.stack([part[cut_rows:] for part in parts])
        return keep, send

    def grads_call(count, with_land, *args):
        shape = shape_of((2, count * local, width), BF)
        return plain(
            functools.partial(weight_grad_kernel, count, with_land), [shape, shape], limit=28
        )(*args)

    def spread_sum(keep, near, far):
        return (keep[0].astype(F32) + near[0].astype(F32) + far.astype(F32)).astype(BF)

    dq_parts, lkg_parts = [], []
    for half in (0, 1):
        dq, lkg = first_back_call(
            heads_grad[half], first_low[half], queries[half], mixed[half], land_k[half]
        )
        dq_parts.append(dq)
        lkg_parts.append(lkg)
        if half == 0:
            mg_core, lkg_parts, dq_parts = gate(mg_core, lkg_parts, dq_parts)
            mg_sum = mg_keep + mg_core
            heads_grad, mg_sum = gate(heads_grad, mg_sum)
            mg_far = swap(mg_sum[own:], 2, "mixed_grad_x")
            edges = edge_rows(proj_low, "grad_edges")
    heads_out, dq_parts, lkg_parts, edges = gate(heads_out, dq_parts, lkg_parts, edges)
    out_keep, out_send = grads_call(1, False, proj_low, *heads_out)
    out_core = swap(out_send, 1, "out_core")

    mg_sum, mg_far, out_core = gate(mg_sum, mg_far, out_core)
    mixed_grad, carried_low = plain(
        carry_back_kernel, [docs_shape, shape_of((own, HEAD_DIM + 16, SEGS), BF)]
    )(mg_sum[:own], mg_far, carried, inverse)
    carried_low, mixed_grad, outer_near, inner_far = gate(
        carried_low, mixed_grad, outer_near, inner_far
    )
    carried_grad = gather_heads(carried_low, "carried_grad")
    inner = (gi_keep[0].astype(F32) + gi_core[0].astype(F32) + inner_far.astype(F32)).astype(BF)
    inner, inner_send = halves(inner, outer_flags[0])
    outer = (own_keep.astype(F32) + own_core.astype(F32) + outer_near.astype(F32)).astype(BF)
    outer, outer_send = split_rows(outer, outer_flags[1])
    mixed_grad, inner_send, outer_send = gate(mixed_grad, inner_send, outer_send)
    inner_hop = swap_batch(inner_send, bits[0], "inner_y")
    outer_hop = swap_batch(outer_send, bits[1], "outer_z")
    small_query, small_key = plain(
        newton_back_kernel, [docs_shape, docs_shape], [pltpu.VMEM((own, SEGS, SEGS), F32)]
    )(mixed_grad, carried, small_t, saved, own_q, own_k)

    small_query, small_key, carried_grad = gate(small_query, small_key, carried_grad)
    delta_all, lse_all = row_of(carried_grad), row_of(mixed)
    dk_parts, dv_parts, lqg_parts = [], [], []
    for half in (0, 1):
        factor = jnp.exp(packs[half][:, HEAD_DIM : HEAD_DIM + 1] - lse_all[half])
        third_in = third_exp[half]
        if half == 1:
            third_in, lqg_parts, inner_hop, outer_hop = gate(
                third_in, lqg_parts, inner_hop, outer_hop
            )
            inner = hop_sum(inner, inner_hop)
            outer = hop_sum(outer, outer_hop)
            third_in, inner, outer, out_send = gate(
                third_in, inner, outer, add_low(out_keep[1], out_core[1])
            )
            outer_hop = swap_batch(outer, bits[2], "outer_w")
            inner_hop = swap_batch(inner, bits[1], "inner_z")
            out_far = swap(out_send, 2, "out_x")
        dk, dv, lqg = third_back_call(
            keys[half], values[half], third_in, factor, delta_all[half], carried_grad[half],
            land_q[half],
        )
        dk_parts.append(dk)
        dv_parts.append(dv)
        lqg_parts.append(lqg)
    lqg_parts[0] = jnp.concatenate([lqg_parts[0][:own] + small_query, lqg_parts[0][own:]], axis=0)
    lkg_parts[0] = jnp.concatenate([lkg_parts[0][:own] + small_key, lkg_parts[0][own:]], axis=0)

    dk_parts, lqg_parts, lkg_parts = gate(dk_parts, lqg_parts, lkg_parts)
    pair_keep, pair_send = grads_call(
        2, True, tokens_in, *dk_parts, *dq_parts, land_tokens, *lkg_parts, *lqg_parts
    )
    def flat(parts):
        return [part.reshape(side_cols, SEGS).astype(BF) for part in parts]

    def weight_rows(half, kind):
        cut = slice(kind * local, (kind + 1) * local)
        return jnp.concatenate([got[2 * half][cut], got[2 * half + 1][cut]], axis=0)

    land_back = sum(
        tn(land, weight_rows(half, kind))
        for kind, lands in ((0, flat(lqg_parts)), (1, flat(lkg_parts)))
        for half, land in enumerate(lands)
    )
    land_mine, land_send = halves(QK_SCALE * land_back / counts[:, None], core)
    dv_parts, pair_send, land_send = gate(dv_parts, pair_send, land_send)
    pair_core = swap(pair_send, 1, "pair_core")
    land_hop = swap(land_send, 1, "land_core")
    edge_code = jnp.concatenate([line[0, :HALF], line[0, HALF + rows : 2 * HALF + rows]])
    edge_real = edge_code.reshape(2 * HALF, 1) >= 0
    edge_parts = [
        jnp.where(edge_real, nt(edges, wo[half]), 0.0).astype(BF) for half in (0, 1)
    ]
    tap_grads = []
    for half in (0, 1):
        if half == 1:
            pair_core, land_hop, tap_grads, dv_parts = gate(
                pair_core, land_hop, tap_grads, dv_parts
            )
            land_mine = (land_mine + land_hop).astype(BF)
            dv_parts, pair_far_send, land_mine = gate(
                dv_parts, add_low(pair_keep[1], pair_core[1]), land_mine
            )
            pair_far = swap(pair_far_send, 2, "pair_x")
            land_hop = swap(land_mine, 2, "land_x")
        dv_parts[half], tap_out = conv_back_call(
            code, line, heads_grad[half], edge_parts[half], values[half],
            tap_lines(tap_rows[half][:, ::-1]), dv_parts[half],
        )
        tap_grads.append(tap_out[:, 0, :KW])
    dv_parts, tap_grads, inner_hop, outer_hop, out_far, land_hop = gate(
        dv_parts, tap_grads, inner_hop, outer_hop, out_far, land_hop
    )
    inner = hop_sum(inner, inner_hop)
    outer = hop_sum(outer, outer_hop)
    out_sum = spread_sum(out_keep, out_core, out_far)
    land_mine = land_mine.astype(F32) + land_hop.astype(F32)
    dv_parts, inner, outer, out_sum, land_mine = gate(dv_parts, inner, outer, out_sum, land_mine)
    outer_hop = swap(outer[1], 2, "outer_x")
    inner_hop = swap_batch(inner, bits[2], "inner_w")
    out_hop = swap_batch(out_sum, bits[0], "out_y")
    land_hop = swap(land_mine, 1, "land_core")
    val_keep, val_send = grads_call(1, False, tokens_in, *dv_parts)
    norms = jnp.stack([grad_first_gain, grad_first_bias, grad_second_gain, grad_second_bias])

    def small_rows(first):
        lines = [
            jnp.concatenate([norms, jnp.pad(part[first : first + own], ((0, 0), (0, width - KW)))])
            for part in tap_grads
        ]
        return jnp.pad(jnp.stack(lines), ((0, 0), (0, 16 - 4 - own), (0, 0))).astype(BF)

    val_keep = jnp.concatenate([val_keep, small_rows(0)], axis=1)
    val_send = jnp.concatenate([val_send, small_rows(own)], axis=1)
    val_send, pair_far, land_hop = gate(val_send, pair_far, land_hop)
    land_back = ordered(core, land_mine, land_hop).astype(BF)
    pair_sum = spread_sum(pair_keep, pair_core, pair_far)
    pair_sum, pair_other = halves(pair_sum, outer_flags[0])
    val_send, pair_other = gate(val_send, pair_other)
    pair_hop = swap_batch(pair_other, bits[0], "pair_y")
    val_core = swap(val_send, 1, "val_core")
    val_core, dv_parts = gate(val_core, dv_parts)
    dv_parts, val_far_send = gate(dv_parts, add_low(val_keep[1], val_core[1]))
    val_far = swap(val_far_send, 2, "val_x")
    row_block = 2 * BLOCK
    rows_spec = pl.BlockSpec((row_block, side_cols), lambda p: (p, 0))
    full_spec = pl.BlockSpec((row_block, width), lambda p: (p, 0))
    input_part = call(
        input_grad_kernel,
        (rows // row_block,),
        [full_spec] + [rows_spec] * 6 + [whole((3 * local + TAP_ROWS, width))] * 4,
        [(full_spec, shape_of((rows, width), F32))],
    )(first_in_grad, *dq_parts, *dk_parts, *dv_parts, *got)[0]

    input_part, outer_hop, pair_hop, val_far, out_hop = gate(
        input_part, outer_hop, pair_hop, val_far, out_hop
    )
    val_sum = spread_sum(val_keep, val_core, val_far)
    pair_sum = hop_sum(pair_sum, pair_hop)
    outer = hop_sum(outer[0], outer_hop)
    out_sum = hop_sum(out_sum, out_hop)
    val_hop = swap_batch(val_sum, bits[0], "val_y")
    pair_hop = swap_batch(pair_sum, bits[2], "pair_w")
    outer_hop = swap_batch(outer, bits[1], "outer_z2")
    out_hop = swap_batch(out_sum, bits[1], "out_z")
    input_grad = (input_part + nn(member, land_back)).astype(BF)

    input_grad, pair_hop, val_hop, outer_hop = gate(input_grad, pair_hop, val_hop, outer_hop)
    pair_sum = hop_sum(pair_sum, pair_hop)
    val_sum = hop_sum(val_sum, val_hop)
    outer = ordered(outer_flags[1], outer, outer_hop)
    for bit in bits[3:]:
        outer = hop_sum(outer, swap_batch(outer, bit, "outer_more"))
    pair_hop = swap_batch(pair_sum, bits[1], "pair_z")
    val_hop = swap_batch(val_sum, bits[2], "val_w")
    outer_hop = swap_batch(outer, bits[0], "outer_y2")
    inner_hop, out_hop, pair_sum = gate(inner_hop, out_hop, pair_sum)
    inner = hop_sum(inner, inner_hop)
    out_sum = hop_sum(out_sum, out_hop)
    for bit in bits[3:]:
        inner = hop_sum(inner, swap_batch(inner, bit, "inner_more"))
        out_sum = hop_sum(out_sum, swap_batch(out_sum, bit, "out_more"))
    inner_hop = swap_batch(inner, bits[0], "inner_y2")
    out_hop = swap_batch(out_sum, bits[2], "out_w")

    pair_hop, val_hop, inner = gate(pair_hop, val_hop, inner)
    pair_sum = hop_sum(pair_sum, pair_hop)
    val_sum = hop_sum(val_sum, val_hop)
    for bit in bits[3:]:
        pair_sum = hop_sum(pair_sum, swap_batch(pair_sum, bit, "pair_more"))
        val_sum = hop_sum(val_sum, swap_batch(val_sum, bit, "val_more"))
    pair_hop = swap_batch(pair_sum, bits[0], "pair_y2")
    val_hop = swap_batch(val_sum, bits[1], "val_z")
    outer_hop, out_hop, pair_sum = gate(outer_hop, out_hop, pair_sum)
    grad_outer = ordered(outer_flags[0], outer, outer_hop).astype(F32)
    grad_output = hop_sum(out_sum, out_hop).astype(F32)
    inner_hop, grad_outer = gate(inner_hop, grad_outer)
    grad_inner = ordered(outer_flags[0], inner, inner_hop).astype(F32)
    pair_sum = ordered(outer_flags[0], pair_sum, pair_hop)
    val_sum = hop_sum(val_sum, val_hop)
    grad_key, grad_query, grad_value = (
        part.astype(F32).T for part in (pair_sum[:local], pair_sum[local:], val_sum[:local])
    )
    small = val_sum[local:].astype(F32)
    return (
        layer_out,
        input_grad,
        grad_query,
        grad_key,
        grad_value,
        grad_output,
        small[4 : 4 + own, :KW],
        small[0],
        small[1],
        grad_inner,
        grad_outer,
        small[2],
        small[3],
    )


def solution(mesh):
    tokens = P(("batch", "head"), None)
    row = P("batch")
    cols = P(None, "head")
    lines = P("head", None)
    rep = P()
    return jax.shard_map(
        functools.partial(shards, mesh.shape["batch"]),
        mesh=mesh,
        in_specs=(
            tokens, row, row, row, cols, cols, cols, lines, lines,
            rep, rep, rep, rep, rep, rep, tokens,
        ),
        out_specs=(
            tokens, tokens, cols, cols, cols, lines, lines, rep, rep, cols, lines, rep, rep,
        ),
        check_vma=False,
    )
```
